128 devices in a mesh: gx: 8 (over y, core), gy: 16 (over x, z).
Axes of the slice: x: 4, y: 4, z: 4, core: 2. Of those that a mesh axis runs over, the one named last changes fastest.
Arguments:
- payload: bfloat16 [16384, 4, 35, 128], P(('gx', 'gy')), may hold values from -6 to 6
- opacity: bfloat16 [16384, 4, 128], P(('gx', 'gy')), may hold values from 0.049804688 to 0.34960938
- depth_order: int32 [1024, 16], P(('gx', 'gy')), may hold values from 0 to 127, as said below
- footprints: int32 [128, 128], replicated, may hold values from 0 to 1023, as said below
- panel_map: int32 [16], replicated, may hold values from 0 to 15, each once
- conv1_weight: bfloat16 [9, 32, 36], replicated, may hold values from -0.3125 to 0.3125
- conv1_bias: float32 [32], replicated, may hold values from -3 to 3
- conv2_weight: bfloat16 [9, 32, 32], replicated, may hold values from -0.375 to 0.375
- conv2_bias: float32 [32], replicated, may hold values from -3 to 3
Outputs:
- display: bfloat16 [8, 16, 1, 32, 4096], P('gx', 'gy')
The draws below stay inside these ranges and needn't reach their ends.
Inputs may be any that keep to these rules, and one draw needn't show every extreme that they name: Each tile lists 16 different bricks; brick b lists tile t in footprints exactly when b appears in row t of depth_order, each tile at most once, 128 tiles a brick. The tiles of the brick of device (x, y) are the 4 consecutive screen tile rows 4x + s .. 4x + s + 3 (modulo 32), for some s from 1 to 3, each with all 32 tile columns; so they belong to devices of gx index x or x + 1 modulo 8, every brick has tiles on both, and every device along gy gets exactly 8 of them. `footprints`: tile numbers as described for depth_order.
All inputs are finite; a program needn't handle non-finite values.
Results may differ from the reference program's by a relative error of at most 0.0052.
Values may be sent and summed in bfloat16 or wider, within the bound.
A program may use at most 64 MiB of HBM per device.

```python
import jax
import jax.numpy as jnp

FEAT = 32
TILE_W = 128
TILE_H = 4
TYD = 4
TXD = 2
TILES_DEV = 8
DEPTH = 16
BRICKS = 128
TILES = 1024
FRAGS = 128
CH = 35
STRIP = 1
SCREEN_H = 128
SCREEN_W = 4096
N_GX = 8
N_GY = 16


def tile_layout(key):
    tile_rows = N_GX * TYD
    tile_cols = N_GY * TXD
    column_range = jnp.arange(N_GY, dtype=jnp.int32)
    scores = jax.random.randint(jax.random.fold_in(key, 11), (N_GX, N_GY), 0, 1 << 20) * N_GY + column_range[None, :]
    slab_of = jnp.argsort(jnp.argsort(scores, axis=1), axis=1).astype(jnp.int32)
    holder = jnp.argsort(slab_of, axis=1).astype(jnp.int32)
    shifts = jax.random.randint(jax.random.fold_in(key, 12), (DEPTH,), 1, TYD).astype(jnp.int32)
    tile_range = jnp.arange(TILES, dtype=jnp.int32)
    owner = tile_range // TILES_DEV
    local = tile_range % TILES_DEV
    tile_row = owner // N_GY * TYD + local // TXD
    depth_range = jnp.arange(DEPTH, dtype=jnp.int32)
    cell = (tile_row[:, None] - shifts[None, :]) % tile_rows // TYD
    ordered = cell * N_GY + holder[cell, depth_range[None, :]]
    brick_range = jnp.arange(BRICKS, dtype=jnp.int32)
    brick_row = brick_range // N_GY
    brick_col = brick_range % N_GY
    offset = shifts[slab_of[brick_row, brick_col]]
    frag_range = jnp.arange(FRAGS, dtype=jnp.int32)
    band_step = frag_range // tile_cols
    column = frag_range % tile_cols
    row = (brick_row[:, None] * TYD + offset[:, None] + band_step[None, :]) % tile_rows
    listed = (row // TYD * N_GY + column[None, :] // TXD) * TILES_DEV + row % TYD * TXD + column[None, :] % TXD
    order_scores = jax.random.randint(jax.random.fold_in(key, 13), (BRICKS, FRAGS), 0, 1 << 20) * FRAGS
    order_scores = order_scores + frag_range[None, :]
    shuffle = jnp.argsort(order_scores, axis=1)
    listed = jnp.take_along_axis(listed, shuffle, axis=1)
    return (ordered.astype(jnp.int32), listed.astype(jnp.int32))


def draw_depth_order(key, part):
    return tile_layout(key)[0]


def draw_footprints(key, part):
    return tile_layout(key)[1]


def block_scale(own_key, dims, pieces, least, high):
    def one(dim, parts):
        draws = jax.random.uniform(jax.random.fold_in(jax.random.fold_in(own_key, 6), dim), (parts,), jnp.float32, least / len(pieces), high / len(pieces))
        return jnp.repeat(jnp.exp(draws), dims[dim] // parts).reshape((-1,) + (1,) * (len(dims) - dim - 1))

    gain = one(*pieces[0])
    for cut in pieces[1:]:
        gain = gain * one(*cut)
    return gain


def bell_draw(rng, dims, width, limit, split=(), held_as=jnp.bfloat16):
    drawn = width * jax.random.normal(rng, dims, jnp.float32)
    if split:
        drawn = drawn * block_scale(rng, dims, split, -0.22, 0.18)
    return jnp.clip(drawn, -limit, limit).astype(held_as)


def setup_inputs(seed: int = 0) -> dict:
    seeds = jax.random.split(jax.random.key(seed), 10)
    payload = bell_draw(seeds[0], (BRICKS * FRAGS, TILE_H, CH, TILE_W), 1.0, 6.0, ((0, 128),))
    opacity = jnp.clip(0.049804688 + 0.2998047 * jax.random.uniform(seeds[1], (BRICKS * FRAGS, TILE_H, TILE_W), jnp.float32) ** block_scale(seeds[1], (BRICKS * FRAGS, TILE_H, TILE_W), ((0, 128),), -0.2, 0.2), 0.049804688, 0.34960938).astype(jnp.bfloat16)
    depth_order = draw_depth_order(jax.random.fold_in(seeds[9], 71), 0)
    footprints = draw_footprints(jax.random.fold_in(seeds[9], 71), 0)
    panel_map = jax.random.permutation(seeds[4], N_GY).astype(jnp.int32)
    conv1_weight = bell_draw(seeds[5], (9, FEAT, CH + 1), (9 * (CH + 1)) ** -0.5, 0.3125)
    conv1_bias = bell_draw(seeds[6], (FEAT,), 0.5, 3.0, (), jnp.float32)
    conv2_weight = bell_draw(seeds[7], (9, FEAT, FEAT), (9 * FEAT) ** -0.5, 0.375)
    conv2_bias = bell_draw(seeds[8], (FEAT,), 0.5, 3.0, (), jnp.float32)
    return dict(payload=payload, opacity=opacity, depth_order=depth_order, footprints=footprints, panel_map=panel_map, conv1_weight=conv1_weight, conv1_bias=conv1_bias, conv2_weight=conv2_weight, conv2_bias=conv2_bias)


def conv_layer(field, kernel):
    height = field.shape[0]
    span_cols = field.shape[2]
    padded = jnp.pad(field.astype(jnp.float32), ((1, 1), (0, 0), (1, 1)))
    kernel_wide = kernel.astype(jnp.float32)
    total = jnp.zeros((height, kernel.shape[1], span_cols), jnp.float32)
    for row_shift in range(3):
        for col_shift in range(3):
            window = padded[row_shift:row_shift + height, :, col_shift:col_shift + span_cols]
            total = total + jnp.einsum("oc,hcw->how", kernel_wide[3 * row_shift + col_shift], window)
    return total


def reference(payload, opacity, depth_order, footprints, panel_map, conv1_weight, conv1_bias, conv2_weight, conv2_bias):
    tile_index = jnp.arange(TILES, dtype=jnp.int32)
    frag_index = jnp.arange(FRAGS, dtype=jnp.int32)
    color = jnp.zeros((TILES, TILE_H, CH, TILE_W), jnp.float32)
    transmit = jnp.ones((TILES, TILE_H, TILE_W), jnp.float32)
    for depth_step in range(DEPTH):
        brick = depth_order[:, depth_step]
        foot_rows = footprints[brick]
        position = jnp.sum(jnp.where(foot_rows == tile_index[:, None], frag_index[None, :], 0), axis=1).astype(jnp.int32)
        source = brick * FRAGS + position
        color = color + transmit[:, :, None, :] * payload[source].astype(jnp.float32)
        transmit = transmit * (1.0 - opacity[source].astype(jnp.float32))
    composite = jnp.concatenate([color.astype(jnp.bfloat16), (1.0 - transmit).astype(jnp.bfloat16)[:, :, None, :]], axis=2)
    screen = composite.reshape(N_GX, N_GY, TYD, TXD, TILE_H, CH + 1, TILE_W)
    screen = screen.transpose(0, 2, 4, 5, 1, 3, 6).reshape(SCREEN_H, CH + 1, SCREEN_W)
    hidden = jax.nn.silu(conv_layer(screen, conv1_weight) + conv1_bias[None, :, None]).astype(jnp.bfloat16)
    shaded = conv_layer(hidden, conv2_weight) + conv2_bias[None, :, None] + screen[:, :FEAT, :].astype(jnp.float32)
    shaded = shaded.astype(jnp.bfloat16)
    strips = shaded.reshape(N_GX, N_GY, STRIP, FEAT, SCREEN_W)
    panel_range = jnp.arange(N_GY, dtype=jnp.int32)
    inverse = jnp.sum(jnp.where(panel_map[:, None] == panel_range[None, :], panel_range[:, None], 0), axis=0).astype(jnp.int32)
    return strips[:, inverse]
```

```python
import functools

import jax
import jax.numpy as jnp
import numpy as np
from jax import lax
from jax.experimental import pallas as pl
from jax.experimental.pallas import tpu as pltpu
from jax.sharding import PartitionSpec as P

MESH = pl.DeviceIdType.MESH
TYD = 4
TXD = 2
TILES = 8
DEPTH = 16
CH = 35
ROWS = 4
COLS = 128
NX = 8
NY = 16
SIDE = 4
TSTEP = DEPTH + 2
MASKS = ((4, 12, 1, 3), (12, 4, 3, 1), (1, 3, 4, 12), (3, 1, 12, 4))


def kappa(q, k):
    m = MASKS[q]
    return (m[1] if k & 4 else 0) ^ (m[2] if k & 2 else 0) ^ (m[3] if k & 1 else 0)


def flip4(p, d):
    if d == 0:
        return p
    if d == 1:
        return p + 1 - 2 * (p % 2)
    if d == 2:
        return (p + 2) % SIDE
    return 3 - p


def paired(c, mask):
    return flip4(c // SIDE, mask // SIDE) * SIDE + flip4(c % SIDE, mask % SIDE)


def tables(footprints, depth_order, gx, gy):
    own = lax.dynamic_slice_in_dim(footprints, gx * NY + gy, 1, 0)[0]
    local = own % TILES
    slot = (own // TILES) % NY * TILES + local
    base = np.zeros((2, 4, 8, 2), np.int32)
    rest = np.zeros((2, 4, 8, 2), np.int32)
    for role in range(2):
        for q in range(4):
            for k in range(8):
                for f in range(2):
                    j, g = q % 2, q // 2
                    jy = (1 + g) if f else (3 if g else 0)
                    base[role, q, k, f] = kappa(q, k) ^ (MASKS[q][0] if role else 0)
                    rest[role, q, k, f] = jy * TXD + j
    owner = jnp.bitwise_xor(jnp.asarray(base.reshape(-1)), gy)
    target = jnp.concatenate(
        [jnp.arange(128, dtype=jnp.int32), owner * TILES + jnp.asarray(rest.reshape(-1))]
    )
    order = jnp.arange(128, dtype=jnp.int32)
    pos = jnp.sum(jnp.where(target[:, None] == slot[None, :], order[None, :], 0), axis=1)

    tile = np.arange(TILES, dtype=np.int32)[:, None]
    part = (gx - depth_order // NY) % NX
    source = (part * NY + depth_order % NY) * 6 + (tile // TXD - 1 + part) * TXD + tile % TXD

    mask = np.zeros((4, 8, 3, 2), np.int32)
    back = np.zeros((4, 8, 3, 2), np.int32)
    which = np.zeros((4, 8, 3, 2), np.int32)
    for q in range(4):
        for k in range(8):
            for e in range(3):
                for s in range(2):
                    j, g = q % 2, q // 2
                    jy = (1 + g) if e != 1 else (3 if g else 0)
                    back[q, k, e, s] = (0, 1 - g, 1)[e]
                    mask[q, k, e, s] = kappa(q, k) ^ (MASKS[q][0] if s else 0)
                    which[q, k, e, s] = jy * TXD + j
    brick = (gx - jnp.asarray(back.reshape(-1))) % NX * NY + jnp.bitwise_xor(
        jnp.asarray(mask.reshape(-1)), gy
    )
    which = jnp.asarray(which.reshape(-1))
    listed = (depth_order + 128 * tile).reshape(-1)
    steps = jnp.tile(jnp.arange(DEPTH, dtype=jnp.int32), TILES)
    hit = (brick + 128 * which)[:, None] == listed[None, :]
    depth = jnp.sum(jnp.where(hit, steps[None, :] - (DEPTH + 1), 0), axis=1) + DEPTH + 1
    return jnp.concatenate([pos, source.reshape(-1), which * TSTEP + depth])


POS_A = 0
POS_K = 128
POS_S = 192
SRC = 256
RET = 384


def reduce_kernel(
    tab, pay_h, opa_h, comp, cov,
    pay, opa, asend, abuf, tb, tsend, trecv, s1, r1, s2, acc, r2, s3, r3, s4, r4, ys, yr,
    lsem, a_s, a_r, t_s, t_r, m_s, m_r, y_s, y_r,
):
    gx = lax.axis_index("gx")
    me = lax.axis_index("gy")
    up = (gx + 1) % NX
    down = (gx + NX - 1) % NX
    loads = [pltpu.make_async_copy(opa_h, opa, lsem.at[4])]
    for i in range(4):
        part = pl.ds(32 * i, 32)
        loads.append(pltpu.make_async_copy(pay_h.at[part], pay.at[part], lsem.at[i]))
    for load in loads:
        load.start()

    barrier = pltpu.get_barrier_semaphore()

    def greet_row(i, _):
        pl.semaphore_signal(barrier, inc=1, device_id=(gx, (me + i) % NY), device_id_type=MESH)
        return 0

    def greet_next(i, _):
        pl.semaphore_signal(barrier, inc=1, device_id=(up, i), device_id_type=MESH)
        pl.semaphore_signal(barrier, inc=1, device_id=(down, i), device_id_type=MESH)
        return 0

    lax.fori_loop(1, NY, greet_row, 0)
    lax.fori_loop(0, NY, greet_next, 0)

    loads[0].wait()

    def pack_alpha(i, _):
        asend[i] = opa[tab[POS_A + i]]
        return 0

    lax.fori_loop(0, 128, pack_alpha, 0, unroll=8)
    for e in range(6):
        abuf[me * 6 + e] = asend[me * TILES + 2 + e]
    pl.semaphore_wait(barrier, 47)

    def alpha_copy(i, back):
        return pltpu.make_async_remote_copy(
            src_ref=asend.at[pl.ds(i * TILES + 2 - 2 * back, 6)],
            dst_ref=abuf.at[pl.ds((back * NY + me) * 6, 6)],
            send_sem=a_s.at[back * NY + i],
            recv_sem=a_r.at[back * NY + me],
            device_id=(up if back else gx, i),
            device_id_type=MESH,
        )

    def alpha_start(n, _):
        alpha_copy((me + n) % NY, 0).start()
        alpha_copy((me + n) % NY, 1).start()
        return 0

    lax.fori_loop(1, NY, alpha_start, 0)
    alpha_copy(me, 1).start()

    for load in loads[1:]:
        load.wait()

    def pack_raw(q, lo, hi):
        def body(k, _):
            for f in range(2):
                s1[q, k, f] = pay[tab[POS_S + (q * 8 + k) * 2 + f]]
            return 0

        lax.fori_loop(lo, hi, body, 0)

    groups = ((4, 8), (2, 4), (1, 2), (0, 1))

    def raw_copy(q, n):
        lo, hi = groups[n]
        part = pl.ds(lo, hi - lo)
        return pltpu.make_async_remote_copy(
            src_ref=s1.at[q, part],
            dst_ref=r1.at[q, part],
            send_sem=m_s.at[q, n],
            recv_sem=m_r.at[q, n],
            device_id=(gx, paired(me, MASKS[q][0])),
            device_id_type=MESH,
        )

    raw = [[raw_copy(q, n) for n in range(4)] for q in range(4)]
    for q in range(4):
        pack_raw(q, 4, 8)
        raw[q][0].start()
    for q in range(4):
        pack_raw(q, 0, 4)

    def alpha_wait(n, _):
        col = (me + n) % NY
        for back in range(2):
            pltpu.make_async_remote_copy(
                src_ref=asend.at[pl.ds(0, 6)],
                dst_ref=abuf.at[pl.ds((back * NY + col) * 6, 6)],
                send_sem=a_s.at[back * NY + col],
                recv_sem=a_r.at[back * NY + col],
                device_id=(gx, col),
                device_id_type=MESH,
            ).wait_recv()
        return 0

    lax.fori_loop(1, NY, alpha_wait, 0)
    alpha_copy(me, 1).wait_recv()

    for t in range(TILES):
        tb[t * TSTEP + DEPTH + 1] = jnp.zeros((ROWS, COLS), jnp.float32)

    def through(d, passed):
        out = []
        for t in range(TILES):
            tb[t * TSTEP + d] = passed[t]
            alpha = abuf[tab[SRC + t * DEPTH + d]].astype(jnp.float32)
            out.append(passed[t] * (1.0 - alpha))
        return tuple(out)

    last = lax.fori_loop(
        0, DEPTH, through, tuple(jnp.ones((ROWS, COLS), jnp.float32) for _ in range(TILES))
    )
    for t in range(TILES):
        cov[t] = (1.0 - last[t]).astype(jnp.bfloat16)

    def fill(i, _):
        tsend[i] = tb[tab[RET + i]]
        return 0

    lax.fori_loop(0, 192, fill, 0, unroll=8)

    def weight_range(q, k, back):
        g = q // 2
        start, size = ((0, 4 if g else 2), (4 if g else 2, 2 if g else 4))[back]
        return pl.ds((q * 8 + k) * 6 + start, size)

    def weight_copy(q, k, back):
        part = weight_range(q, k, back)
        return pltpu.make_async_remote_copy(
            src_ref=tsend.at[part],
            dst_ref=trecv.at[part],
            send_sem=t_s.at[q, k, back],
            recv_sem=t_r.at[q, k, back],
            device_id=(down if back else gx, paired(me, kappa(q, k))),
            device_id_type=MESH,
        )

    weights = {}
    for k in (7, 6, 5, 4, 3, 2, 1, 0):
        for q in range(4):
            for back in range(2):
                if k == 0 and back == 0:
                    g = q // 2
                    for e in range(4 if g else 2):
                        trecv[q * 48 + e] = tsend[q * 48 + e]
                else:
                    weights[q, k, back] = weight_copy(q, k, back)
                    weights[q, k, back].start()
    for q in range(4):
        for n in range(1, 4):
            raw[q][n].start()

    def weighed(q, k):
        own = (q * 8 + k) * 2
        lead = (q * 8 + k) * 6
        own_f = pay[tab[POS_K + own]].astype(jnp.float32)
        got_f = r1[q, k, 0].astype(jnp.float32)
        mid = trecv[lead + 2][None] * own_f + trecv[lead + 3][None] * got_f
        own_a = pay[tab[POS_K + own + 1]].astype(jnp.float32)
        got_a = r1[q, k, 1].astype(jnp.float32)
        first = trecv[lead][None] * own_a + trecv[lead + 1][None] * got_a
        third = trecv[lead + 4][None] * own_a + trecv[lead + 5][None] * got_a
        return first, mid, third

    def merge_sent(q, lo, hi):
        def body(k, _):
            for e, v in enumerate(weighed(q, k)):
                s2[q, k - 4, e] = v.astype(jnp.bfloat16)
            return 0

        lax.fori_loop(lo, hi, body, 0)

    def merge_kept(q, lo, hi):
        def body(k, _):
            for e, v in enumerate(weighed(q, k)):
                acc[q, k, e] = v
            return 0

        lax.fori_loop(lo, hi, body, 0)

    def step_copy(src, dst, q, lo, hi, step, sem):
        part = pl.ds(lo, hi - lo)
        return pltpu.make_async_remote_copy(
            src_ref=src.at[q, part],
            dst_ref=dst.at[q, part],
            send_sem=m_s.at[q, sem],
            recv_sem=m_r.at[q, sem],
            device_id=(gx, paired(me, MASKS[q][step - 1])),
            device_id_type=MESH,
        )

    def wait_weights(q, lo, hi):
        for k in range(lo, hi):
            for back in range(2):
                if (q, k, back) in weights:
                    weights[q, k, back].wait_recv()

    two = [[step_copy(s2, r2, q, lo, hi, 2, 4 + n) for n, (lo, hi) in enumerate(groups[1:])] for q in range(4)]
    three = [[step_copy(s3, r3, q, lo, hi, 3, 7 + n) for n, (lo, hi) in enumerate(groups[2:])] for q in range(4)]
    four = [step_copy(s4, r4, q, 0, 1, 4, 9) for q in range(4)]

    for q in range(4):
        wait_weights(q, 4, 8)
        raw[q][0].wait_recv()
        merge_sent(q, 6, 8)
        two[q][0].start()
    for q in range(4):
        merge_sent(q, 4, 6)
        two[q][1].start()
        two[q][2].start()
    for q in range(4):
        wait_weights(q, 0, 4)
        for n in range(1, 4):
            raw[q][n].wait_recv()
        merge_kept(q, 0, 4)

    def added(src, q, k):
        return [acc[q, k, e] + src[q, k, e].astype(jnp.float32) for e in range(3)]

    def forward(dst, src, q, k, to):
        for e, v in enumerate(added(src, q, k)):
            dst[q, to, e] = v.astype(jnp.bfloat16)

    def keep(src, q, k):
        for e, v in enumerate(added(src, q, k)):
            acc[q, k, e] = v

    for q in range(4):
        two[q][0].wait_recv()
        forward(s3, r2, q, 3, 1)
        three[q][0].start()
        forward(s3, r2, q, 2, 0)
        three[q][1].start()
    for q in range(4):
        two[q][1].wait_recv()
        keep(r2, q, 1)
        two[q][2].wait_recv()
        keep(r2, q, 0)
    for q in range(4):
        three[q][0].wait_recv()
        forward(s4, r3, q, 1, 0)
        four[q].start()
    for q in range(4):
        three[q][1].wait_recv()
        keep(r3, q, 0)

    def cross_copy(q):
        part = pl.ds(q // 2, 2 - q // 2)
        return pltpu.make_async_remote_copy(
            src_ref=ys.at[q, part],
            dst_ref=yr.at[q, part],
            send_sem=y_s.at[q],
            recv_sem=y_r.at[q],
            device_id=(up, me),
            device_id_type=MESH,
        )

    cross = [cross_copy(q) for q in range(4)]
    for q in range(4):
        g, j = q // 2, q % 2
        four[q].wait_recv()
        first, mid, third = added(r4, q, 0)
        ys[q, 1] = third.astype(jnp.bfloat16)
        if g == 0:
            ys[q, 0] = mid.astype(jnp.bfloat16)
        else:
            comp[3 * TXD + j] = mid.astype(jnp.bfloat16)
        cross[q].start()
        acc[q, 0, 0] = first
    for q in range(4):
        g, j = q // 2, q % 2
        cross[q].wait_recv()
        comp[(1 + g) * TXD + j] = (acc[q, 0, 0] + yr[q, 1].astype(jnp.float32)).astype(jnp.bfloat16)
        if g == 0:
            comp[j] = yr[q, 0]

    def alpha_sent(n, _):
        alpha_copy((me + n) % NY, 0).wait_send()
        alpha_copy((me + n) % NY, 1).wait_send()
        return 0

    lax.fori_loop(1, NY, alpha_sent, 0)
    alpha_copy(me, 1).wait_send()
    for copy in weights.values():
        copy.wait_send()
    for q in range(4):
        for copy in raw[q] + two[q] + three[q] + [four[q], cross[q]]:
            copy.wait_send()


def reduce_fragments(tab, payload, opacity):
    unit = (CH, ROWS, COLS)
    bf16, f32 = jnp.bfloat16, jnp.float32
    vmem = pltpu.VMEM
    dma = pltpu.SemaphoreType.DMA
    return pl.pallas_call(
        reduce_kernel,
        name="reduce_fragments",
        out_shape=(
            jax.ShapeDtypeStruct((TILES,) + unit, bf16),
            jax.ShapeDtypeStruct((TILES, ROWS, COLS), bf16),
        ),
        in_specs=[
            pl.BlockSpec(memory_space=pltpu.SMEM),
            pl.BlockSpec(memory_space=pl.ANY),
            pl.BlockSpec(memory_space=pl.ANY),
        ],
        out_specs=(pl.BlockSpec(memory_space=vmem), pl.BlockSpec(memory_space=vmem)),
        scratch_shapes=[
            vmem((128,) + unit, bf16),
            vmem((128, ROWS, COLS), bf16),
            vmem((128, ROWS, COLS), bf16),
            vmem((192, ROWS, COLS), bf16),
            vmem((TILES * TSTEP, ROWS, COLS), f32),
            vmem((192, ROWS, COLS), f32),
            vmem((192, ROWS, COLS), f32),
            vmem((4, 8, 2) + unit, bf16),
            vmem((4, 8, 2) + unit, bf16),
            vmem((4, 4, 3) + unit, bf16),
            vmem((4, 4, 3) + unit, f32),
            vmem((4, 4, 3) + unit, bf16),
            vmem((4, 2, 3) + unit, bf16),
            vmem((4, 2, 3) + unit, bf16),
            vmem((4, 1, 3) + unit, bf16),
            vmem((4, 1, 3) + unit, bf16),
            vmem((4, 2) + unit, bf16),
            vmem((4, 2) + unit, bf16),
            dma((5,)),
            dma((32,)),
            dma((32,)),
            dma((4, 8, 2)),
            dma((4, 8, 2)),
            dma((4, 10)),
            dma((4, 10)),
            dma((4,)),
            dma((4,)),
        ],
        compiler_params=pltpu.CompilerParams(
            collective_id=0, has_side_effects=True, vmem_limit_bytes=48 << 20
        ),
    )(tab, payload, opacity)


def with_halo(block, sides, width):
    for axis, dim in sides:
        count = lax.axis_size(axis)
        forward = [(i, i + 1) for i in range(count - 1)]
        backward = [(target, source) for source, target in forward]
        low = lax.ppermute(
            lax.slice_in_dim(block, block.shape[dim] - width, None, axis=dim), axis, forward
        )
        high = lax.ppermute(lax.slice_in_dim(block, 0, width, axis=dim), axis, backward)
        block = jnp.concatenate([low, block, high], axis=dim)
    return block


def conv_valid(padded, kernel):
    height = padded.shape[0] - 2
    span_cols = padded.shape[2] - 2
    total = jnp.zeros((height, kernel.shape[1], span_cols), jnp.float32)
    for row_shift in range(3):
        for col_shift in range(3):
            window = padded[row_shift : row_shift + height, :, col_shift : col_shift + span_cols]
            total = total + jnp.einsum(
                "oc,hcw->how",
                kernel[3 * row_shift + col_shift],
                window,
                preferred_element_type=jnp.float32,
            )
    return total


def rimmed(field):
    return with_halo(field, (("gx", 0), ("gy", 2)), 1)


def composited(payload, opacity, depth_order, footprints):
    gx = lax.axis_index("gx")
    gy = lax.axis_index("gy")
    tab = tables(footprints, depth_order, gx, gy)
    color, cover = reduce_fragments(tab, payload.transpose(0, 2, 1, 3), opacity)
    composite = jnp.concatenate([color, cover[:, None]], axis=1)
    region = composite.reshape(TYD, TXD, CH + 1, ROWS, COLS).transpose(0, 3, 2, 1, 4)
    return region.reshape(TYD * ROWS, CH + 1, TXD * COLS)


def shards(
    payload, opacity, depth_order, footprints, panel_map,
    conv1_weight, conv1_bias, conv2_weight, conv2_bias,
):
    col_groups = lax.axis_size("gy")
    region = composited(payload, opacity, depth_order, footprints)
    band_rows = region.shape[0]
    region_cols = region.shape[2]
    bias_one = conv1_bias[None, :, None]
    bias_two = conv2_bias[None, :, None]
    hidden = jax.nn.silu(conv_valid(rimmed(region), conv1_weight) + bias_one).astype(jnp.bfloat16)
    shaded = conv_valid(rimmed(hidden), conv2_weight)
    feature_count = conv2_weight.shape[1]
    shaded = (shaded + bias_two + region[:, :feature_count, :].astype(jnp.float32)).astype(
        jnp.bfloat16
    )
    strip_rows = band_rows // col_groups
    panel_range = jnp.arange(col_groups, dtype=jnp.int32)
    inverse = jnp.sum(
        jnp.where(panel_map[:, None] == panel_range[None, :], panel_range[:, None], 0), axis=0
    )
    pieces = shaded.reshape(col_groups, strip_rows, feature_count, region_cols)[inverse]
    pieces = pieces.reshape(band_rows, feature_count, region_cols)
    shown = lax.all_to_all(pieces, "gy", split_axis=0, concat_axis=2, tiled=True)
    return shown[None, None]


SPECS = (
    P(("gx", "gy"), None, None, None),
    P(("gx", "gy"), None, None),
    P(("gx", "gy"), None),
    P(),
    P(),
    P(),
    P(),
    P(),
    P(),
)


def solution(mesh):
    return jax.shard_map(
        shards,
        mesh=mesh,
        in_specs=SPECS,
        out_specs=P("gx", "gy", None, None, None),
        check_vma=False,
    )
```

```python
import functools

import jax
import jax.numpy as jnp
import numpy as np
from jax import lax
from jax.experimental import pallas as pl
from jax.experimental.pallas import tpu as pltpu
from jax.sharding import PartitionSpec as P

MESH = pl.DeviceIdType.MESH
TYD = 4
TXD = 2
TILES = 8
DEPTH = 16
CH = 35
ROWS = 4
COLS = 128
NX = 8
NY = 16
SIDE = 4
TSTEP = DEPTH + 2
MASKS = ((4, 12, 1, 3), (12, 4, 3, 1), (1, 3, 4, 12), (3, 1, 12, 4))


def kappa(q, k):
    m = MASKS[q]
    return (m[1] if k & 4 else 0) ^ (m[2] if k & 2 else 0) ^ (m[3] if k & 1 else 0)


def flip4(p, d):
    if d == 0:
        return p
    if d == 1:
        return p + 1 - 2 * (p % 2)
    if d == 2:
        return (p + 2) % SIDE
    return 3 - p


def paired(c, mask):
    return flip4(c // SIDE, mask // SIDE) * SIDE + flip4(c % SIDE, mask % SIDE)


def tables(footprints, depth_order, panel_map, gx, gy):
    own = lax.dynamic_slice_in_dim(footprints, gx * NY + gy, 1, 0)[0]
    local = own % TILES
    slot = (own // TILES) % NY * TILES + local
    base = np.zeros((2, 4, 8, 2), np.int32)
    rest = np.zeros((2, 4, 8, 2), np.int32)
    for role in range(2):
        for q in range(4):
            for k in range(8):
                for f in range(2):
                    j, g = q % 2, q // 2
                    jy = (1 + g) if f else (3 if g else 0)
                    base[role, q, k, f] = kappa(q, k) ^ (MASKS[q][0] if role else 0)
                    rest[role, q, k, f] = jy * TXD + j
    owner = jnp.bitwise_xor(jnp.asarray(base.reshape(-1)), gy)
    target = jnp.concatenate(
        [jnp.arange(128, dtype=jnp.int32), owner * TILES + jnp.asarray(rest.reshape(-1))]
    )
    order = jnp.arange(128, dtype=jnp.int32)
    pos = jnp.sum(jnp.where(target[:, None] == slot[None, :], order[None, :], 0), axis=1)

    tile = np.arange(TILES, dtype=np.int32)[:, None]
    part = (gx - depth_order // NY) % NX
    source = (part * NY + depth_order % NY) * 6 + (tile // TXD - 1 + part) * TXD + tile % TXD

    mask = np.zeros((4, 8, 3, 2), np.int32)
    back = np.zeros((4, 8, 3, 2), np.int32)
    which = np.zeros((4, 8, 3, 2), np.int32)
    for q in range(4):
        for k in range(8):
            for e in range(3):
                for s in range(2):
                    j, g = q % 2, q // 2
                    jy = (1 + g) if e != 1 else (3 if g else 0)
                    back[q, k, e, s] = (0, 1 - g, 1)[e]
                    mask[q, k, e, s] = kappa(q, k) ^ (MASKS[q][0] if s else 0)
                    which[q, k, e, s] = jy * TXD + j
    brick = (gx - jnp.asarray(back.reshape(-1))) % NX * NY + jnp.bitwise_xor(
        jnp.asarray(mask.reshape(-1)), gy
    )
    which = jnp.asarray(which.reshape(-1))
    listed = (depth_order + 128 * tile).reshape(-1)
    steps = jnp.tile(jnp.arange(DEPTH, dtype=jnp.int32), TILES)
    hit = (brick + 128 * which)[:, None] == listed[None, :]
    depth = jnp.sum(jnp.where(hit, steps[None, :] - (DEPTH + 1), 0), axis=1) + DEPTH + 1
    panels = jnp.arange(NY, dtype=jnp.int32)
    inverse = jnp.sum(jnp.where(panel_map[:, None] == panels[None, :], panels[:, None], 0), axis=0)
    return jnp.concatenate([pos, source.reshape(-1), which * TSTEP + depth, inverse])


POS_A = 0
POS_K = 128
POS_S = 192
SRC = 256
RET = 384
INV = 576
OUT = 32
WIDE = 3 * COLS
DEEP1 = (CH + 1) * ROWS
DEEP2 = OUT * ROWS


def frame_kernel(
    tab, pay_h, opa_h, w1, b1, w2, b2, shown,
    pay, opa, asend, abuf, tb, tsend, trecv, s1, r1, s2, acc, r2, s3, r3, s4, r4, ys, yr,
    cov, stage, v1, pack, side, corner, band1, band2, h_acc, v2, v2_top, v2_low, o_acc, shaded, strips, got,
    lsem, a_s, a_r, t_s, t_r, m_s, m_r, y_s, y_r, h_s, h_r, d_s, d_r,
):
    gx = lax.axis_index("gx")
    me = lax.axis_index("gy")
    up = (gx + 1) % NX
    down = (gx + NX - 1) % NX
    loads = [pltpu.make_async_copy(opa_h, opa, lsem.at[4])]
    for i in range(4):
        part = pl.ds(32 * i, 32)
        loads.append(pltpu.make_async_copy(pay_h.at[part], pay.at[part], lsem.at[i]))
    for load in loads:
        load.start()

    barrier = pltpu.get_barrier_semaphore()

    def greet_row(i, _):
        pl.semaphore_signal(barrier, inc=1, device_id=(gx, (me + i) % NY), device_id_type=MESH)
        return 0

    def greet_next(i, _):
        pl.semaphore_signal(barrier, inc=1, device_id=(up, i), device_id_type=MESH)
        pl.semaphore_signal(barrier, inc=1, device_id=(down, i), device_id_type=MESH)
        return 0

    lax.fori_loop(1, NY, greet_row, 0)
    lax.fori_loop(0, NY, greet_next, 0)

    loads[0].wait()

    def pack_alpha(i, _):
        asend[i] = opa[tab[POS_A + i]]
        return 0

    lax.fori_loop(0, 128, pack_alpha, 0, unroll=8)
    for e in range(6):
        abuf[me * 6 + e] = asend[me * TILES + 2 + e]
    pl.semaphore_wait(barrier, 47)

    def alpha_copy(i, back):
        return pltpu.make_async_remote_copy(
            src_ref=asend.at[pl.ds(i * TILES + 2 - 2 * back, 6)],
            dst_ref=abuf.at[pl.ds((back * NY + me) * 6, 6)],
            send_sem=a_s.at[back * NY + i],
            recv_sem=a_r.at[back * NY + me],
            device_id=(up if back else gx, i),
            device_id_type=MESH,
        )

    def alpha_start(n, _):
        alpha_copy((me + n) % NY, 0).start()
        alpha_copy((me + n) % NY, 1).start()
        return 0

    lax.fori_loop(1, NY, alpha_start, 0)
    alpha_copy(me, 1).start()

    for load in loads[1:]:
        load.wait()

    def pack_raw(q, lo, hi):
        def body(k, _):
            for f in range(2):
                s1[q, k, f] = pay[tab[POS_S + (q * 8 + k) * 2 + f]]
            return 0

        lax.fori_loop(lo, hi, body, 0)

    groups = ((4, 8), (2, 4), (1, 2), (0, 1))

    def raw_copy(q, n):
        lo, hi = groups[n]
        part = pl.ds(lo, hi - lo)
        return pltpu.make_async_remote_copy(
            src_ref=s1.at[q, part],
            dst_ref=r1.at[q, part],
            send_sem=m_s.at[q, n],
            recv_sem=m_r.at[q, n],
            device_id=(gx, paired(me, MASKS[q][0])),
            device_id_type=MESH,
        )

    raw = [[raw_copy(q, n) for n in range(4)] for q in range(4)]
    for q in range(4):
        pack_raw(q, 4, 8)
        raw[q][0].start()
    for q in range(4):
        pack_raw(q, 0, 4)

    spread_weights(w1, w2, band1, band2)

    def alpha_wait(n, _):
        col = (me + n) % NY
        for back in range(2):
            pltpu.make_async_remote_copy(
                src_ref=asend.at[pl.ds(0, 6)],
                dst_ref=abuf.at[pl.ds((back * NY + col) * 6, 6)],
                send_sem=a_s.at[back * NY + col],
                recv_sem=a_r.at[back * NY + col],
                device_id=(gx, col),
                device_id_type=MESH,
            ).wait_recv()
        return 0

    lax.fori_loop(1, NY, alpha_wait, 0)
    alpha_copy(me, 1).wait_recv()

    for t in range(TILES):
        tb[t * TSTEP + DEPTH + 1] = jnp.zeros((ROWS, COLS), jnp.float32)

    def through(d, passed):
        out = []
        for t in range(TILES):
            tb[t * TSTEP + d] = passed[t]
            alpha = abuf[tab[SRC + t * DEPTH + d]].astype(jnp.float32)
            out.append(passed[t] * (1.0 - alpha))
        return tuple(out)

    last = lax.fori_loop(
        0, DEPTH, through, tuple(jnp.ones((ROWS, COLS), jnp.float32) for _ in range(TILES))
    )
    for t in range(TILES):
        cov[t] = 1.0 - last[t]

    def fill(i, _):
        tsend[i] = tb[tab[RET + i]]
        return 0

    lax.fori_loop(0, 192, fill, 0, unroll=8)

    def weight_range(q, k, back):
        g = q // 2
        start, size = ((0, 4 if g else 2), (4 if g else 2, 2 if g else 4))[back]
        return pl.ds((q * 8 + k) * 6 + start, size)

    def weight_copy(q, k, back):
        part = weight_range(q, k, back)
        return pltpu.make_async_remote_copy(
            src_ref=tsend.at[part],
            dst_ref=trecv.at[part],
            send_sem=t_s.at[q, k, back],
            recv_sem=t_r.at[q, k, back],
            device_id=(down if back else gx, paired(me, kappa(q, k))),
            device_id_type=MESH,
        )

    weights = {}
    for k in (7, 6, 5, 4, 3, 2, 1, 0):
        for q in range(4):
            for back in range(2):
                if k == 0 and back == 0:
                    g = q // 2
                    for e in range(4 if g else 2):
                        trecv[q * 48 + e] = tsend[q * 48 + e]
                else:
                    weights[q, k, back] = weight_copy(q, k, back)
                    weights[q, k, back].start()
    for q in range(4):
        for n in range(1, 4):
            raw[q][n].start()

    def weighed(q, k):
        own = (q * 8 + k) * 2
        lead = (q * 8 + k) * 6
        own_f = pay[tab[POS_K + own]].astype(jnp.float32)
        got_f = r1[q, k, 0].astype(jnp.float32)
        mid = trecv[lead + 2][None] * own_f + trecv[lead + 3][None] * got_f
        own_a = pay[tab[POS_K + own + 1]].astype(jnp.float32)
        got_a = r1[q, k, 1].astype(jnp.float32)
        first = trecv[lead][None] * own_a + trecv[lead + 1][None] * got_a
        third = trecv[lead + 4][None] * own_a + trecv[lead + 5][None] * got_a
        return first, mid, third

    def merge_sent(q, lo, hi):
        def body(k, _):
            for e, v in enumerate(weighed(q, k)):
                s2[q, k - 4, e] = v.astype(jnp.bfloat16)
            return 0

        lax.fori_loop(lo, hi, body, 0)

    def merge_kept(q, lo, hi):
        def body(k, _):
            for e, v in enumerate(weighed(q, k)):
                acc[q, k, e] = v
            return 0

        lax.fori_loop(lo, hi, body, 0)

    def step_copy(src, dst, q, lo, hi, step, sem):
        part = pl.ds(lo, hi - lo)
        return pltpu.make_async_remote_copy(
            src_ref=src.at[q, part],
            dst_ref=dst.at[q, part],
            send_sem=m_s.at[q, sem],
            recv_sem=m_r.at[q, sem],
            device_id=(gx, paired(me, MASKS[q][step - 1])),
            device_id_type=MESH,
        )

    def wait_weights(q, lo, hi):
        for k in range(lo, hi):
            for back in range(2):
                if (q, k, back) in weights:
                    weights[q, k, back].wait_recv()

    two = [[step_copy(s2, r2, q, lo, hi, 2, 4 + n) for n, (lo, hi) in enumerate(groups[1:])] for q in range(4)]
    three = [[step_copy(s3, r3, q, lo, hi, 3, 7 + n) for n, (lo, hi) in enumerate(groups[2:])] for q in range(4)]
    four = [step_copy(s4, r4, q, 0, 1, 4, 9) for q in range(4)]

    for q in range(4):
        wait_weights(q, 4, 8)
        raw[q][0].wait_recv()
        merge_sent(q, 6, 8)
        two[q][0].start()
    for q in range(4):
        merge_sent(q, 4, 6)
        two[q][1].start()
        two[q][2].start()
    for q in range(4):
        wait_weights(q, 0, 4)
        for n in range(1, 4):
            raw[q][n].wait_recv()
        merge_kept(q, 0, 4)

    def added(src, q, k):
        return [acc[q, k, e] + src[q, k, e].astype(jnp.float32) for e in range(3)]

    def forward(dst, src, q, k, to):
        for e, v in enumerate(added(src, q, k)):
            dst[q, to, e] = v.astype(jnp.bfloat16)

    def keep(src, q, k):
        for e, v in enumerate(added(src, q, k)):
            acc[q, k, e] = v

    for q in range(4):
        two[q][0].wait_recv()
        forward(s3, r2, q, 3, 1)
        three[q][0].start()
        forward(s3, r2, q, 2, 0)
        three[q][1].start()
    for q in range(4):
        two[q][1].wait_recv()
        keep(r2, q, 1)
        two[q][2].wait_recv()
        keep(r2, q, 0)
    for q in range(4):
        three[q][0].wait_recv()
        forward(s4, r3, q, 1, 0)
        four[q].start()
    for q in range(4):
        three[q][1].wait_recv()
        keep(r3, q, 0)

    def cross_copy(q):
        part = pl.ds(q // 2, 2 - q // 2)
        return pltpu.make_async_remote_copy(
            src_ref=ys.at[q, part],
            dst_ref=yr.at[q, part],
            send_sem=y_s.at[q],
            recv_sem=y_r.at[q],
            device_id=(up, me),
            device_id_type=MESH,
        )

    cross = [cross_copy(q) for q in range(4)]
    right = (me + 1) % NY
    left = (me + NY - 1) % NY

    def place(jy, j, v):
        lanes = pl.ds(j * COLS, COLS)
        for c in range(CH):
            stage[jy, j, pl.ds(c * ROWS, ROWS), :] = v[c]
        stage[jy, j, pl.ds(CH * ROWS, ROWS), :] = cov[jy * TXD + j]
        v1[jy + 1, :, lanes] = stage[jy, j].astype(jnp.bfloat16)

    def edge_copy(src, dst, n, row, col):
        return pltpu.make_async_remote_copy(
            src_ref=src,
            dst_ref=dst,
            send_sem=h_s.at[n],
            recv_sem=h_r.at[n],
            device_id=(row, col),
            device_id_type=MESH,
        )

    mine = pl.ds(0, TXD * COLS)
    low = pl.ds(0, COLS)
    high = pl.ds(COLS, COLS)
    edges = (
        edge_copy(v1.at[4, :, mine], v1.at[0, :, mine], 0, up, me),
        edge_copy(v1.at[4, :, high], corner.at[0], 1, up, right),
        edge_copy(v1.at[4, :, low], corner.at[1], 2, up, left),
        edge_copy(v1.at[1, :, mine], v1.at[5, :, mine], 3, down, me),
        edge_copy(v1.at[1, :, high], corner.at[2], 4, down, right),
        edge_copy(v1.at[1, :, low], corner.at[3], 5, down, left),
        edge_copy(pack.at[0], side.at[0], 6, gx, right),
        edge_copy(pack.at[1], side.at[1], 7, gx, left),
    )

    for q in range(4):
        g, j = q // 2, q % 2
        four[q].wait_recv()
        first, mid, third = added(r4, q, 0)
        ys[q, 1] = third.astype(jnp.bfloat16)
        if g == 0:
            ys[q, 0] = mid.astype(jnp.bfloat16)
        cross[q].start()
        acc[q, 0, 0] = first
        if g:
            place(3, j, mid)
    for n in range(3):
        edges[n].start()
    for q in range(4):
        g, j = q // 2, q % 2
        cross[q].wait_recv()
        if g == 0:
            place(0, j, yr[q, 0].astype(jnp.float32))
        place(1 + g, j, acc[q, 0, 0] + yr[q, 1].astype(jnp.float32))
        if q == 1:
            for n in range(3, 6):
                edges[n].start()

    lane = lax.broadcasted_iota(jnp.int32, (DEEP1, COLS), 1)
    to_right = stage[0, 1]
    to_left = stage[0, 0]
    for jy in range(1, TYD):
        spot = (lane // 2) == (COLS // 2 - 1 - jy)
        to_right = jnp.where(spot, pltpu.roll(stage[jy, 1], COLS - 2 * jy, 1), to_right)
        spot = (lane // 2) == jy
        to_left = jnp.where(spot, pltpu.roll(stage[jy, 0], 2 * jy, 1), to_left)
    pack[0] = to_right.astype(jnp.bfloat16)
    pack[1] = to_left.astype(jnp.bfloat16)
    edges[6].start()
    edges[7].start()
    for copy in edges:
        copy.wait_recv()

    on_right = jnp.logical_and(lane < COLS // 2, me < NY - 1)
    on_left = jnp.logical_and(lane >= COLS // 2, me > 0)
    last_tile = pl.ds(2 * COLS, COLS)
    zero = jnp.zeros((DEEP1, COLS), jnp.float32)
    from_left = side[0].astype(jnp.float32)
    from_right = side[1].astype(jnp.float32)
    for jy in range(TYD):
        r_part = pltpu.roll(from_right, COLS - 2 * jy, 1) if jy else from_right
        l_part = pltpu.roll(from_left, 2 * jy, 1) if jy else from_left
        rim = jnp.where(on_right, r_part, jnp.where(on_left, l_part, zero))
        v1[jy + 1, :, last_tile] = rim.astype(jnp.bfloat16)
    wide_zero = jnp.zeros((DEEP1, TXD * COLS), jnp.bfloat16)
    for blk, base, inside in ((0, 0, gx > 0), (5, 2, gx < NX - 1)):
        l_part = corner[base].astype(jnp.float32)
        r_part = corner[base + 1].astype(jnp.float32)
        rim = jnp.where(on_right, r_part, jnp.where(on_left, l_part, zero))
        rim = jnp.where(inside, rim, zero)
        v1[blk, :, last_tile] = rim.astype(jnp.bfloat16)

        @pl.when(jnp.logical_not(inside))
        def _(blk=blk):
            v1[blk, :, mine] = wide_zero

    def product(band, rows, field):
        total = None
        for dx in range(3):
            z = jnp.dot(band(dx, rows), field, preferred_element_type=jnp.float32)
            if dx != 1:
                z = pltpu.roll(z, (1 - dx) % WIDE, 1)
            total = z if total is None else total + z
        return total

    def band_one(dx, rows):
        return band1[dx, rows, :]

    def band_two(dx, rows):
        return band2[dx, rows, :]

    def column(ref):
        eye = lax.broadcasted_iota(jnp.int32, (OUT, OUT), 0) == lax.broadcasted_iota(jnp.int32, (OUT, OUT), 1)
        return jnp.sum(jnp.where(eye, ref[...], 0.0), axis=1, keepdims=True)

    every = pl.ds(0, 6 * OUT)
    head = product(band_one, pl.ds(4 * OUT, 2 * OUT), v1[0])
    h_acc[0] = head[:OUT]
    h_acc[1] = head[OUT:]
    for blk in range(TYD):
        s = product(band_one, every, v1[blk + 1])
        y = 4 * blk
        for n in range(6):
            piece = s[n * OUT : (n + 1) * OUT]
            h_acc[y + n] = piece + h_acc[y + n] if n < 2 else piece
    tail = product(band_one, pl.ds(0, 2 * OUT), v1[5])
    bias_one = column(b1)
    far = lax.broadcasted_iota(jnp.int32, (OUT, WIDE), 1)
    cut = jnp.logical_or(
        jnp.logical_and(far >= 2 * COLS + COLS // 2, me == 0),
        jnp.logical_and(
            jnp.logical_and(far >= 2 * COLS, far < 2 * COLS + COLS // 2), me == NY - 1
        ),
    )
    for n in range(18):
        raw_sum = h_acc[n]
        if n >= 16:
            raw_sum = raw_sum + tail[(n - 16) * OUT : (n - 15) * OUT]
        pre = raw_sum + bias_one
        h = pre * lax.logistic(pre)
        h = jnp.where(cut, 0.0, h)
        if n == 0:
            v2_top[...] = jnp.where(gx > 0, h, 0.0).astype(jnp.bfloat16)
        elif n == 17:
            v2_low[...] = jnp.where(gx < NX - 1, h, 0.0).astype(jnp.bfloat16)
        else:
            v2[(n - 1) // 4, pl.ds((n - 1) % 4 * OUT, OUT), :] = h.astype(jnp.bfloat16)

    o_acc[0] = product(lambda dx, rows: w2[dx], every, v2_top[...])[:, : TXD * COLS]
    for blk in range(TYD):
        s = product(band_two, every, v2[blk])[:, : TXD * COLS]
        y = 4 * blk - 1
        for n in range(6):
            piece = s[n * OUT : (n + 1) * OUT]
            if 0 <= y + n < 16:
                o_acc[y + n] = piece + o_acc[y + n] if n < 2 else piece
    tail = product(lambda dx, rows: w2[6 + dx], every, v2_low[...])[:, : TXD * COLS]
    bias_two = column(b2)
    for n in range(16):
        rows = pl.ds(n % 4, OUT, stride=ROWS)
        base = jnp.concatenate([stage[n // 4, j, rows, :] for j in range(TXD)], axis=1)
        value = o_acc[n] + bias_two + base.astype(jnp.bfloat16).astype(jnp.float32)
        if n == 15:
            value = value + tail
        shaded[n] = value.astype(jnp.bfloat16)

    def strip_copy(g):
        return pltpu.make_async_remote_copy(
            src_ref=strips.at[g],
            dst_ref=got.at[me],
            send_sem=d_s.at[g],
            recv_sem=d_r.at[me],
            device_id=(gx, g),
            device_id_type=MESH,
        )

    def strip_start(n, _):
        g = (me + n) % NY
        strips[g] = shaded[tab[INV + g]]
        strip_copy(g).start()
        return 0

    lax.fori_loop(1, NY, strip_start, 0)
    got[me] = shaded[tab[INV + me]]

    def strip_wait(n, _):
        col = (me + n) % NY
        pltpu.make_async_remote_copy(
            src_ref=strips.at[col],
            dst_ref=got.at[col],
            send_sem=d_s.at[col],
            recv_sem=d_r.at[col],
            device_id=(gx, col),
            device_id_type=MESH,
        ).wait_recv()
        return 0

    lax.fori_loop(1, NY, strip_wait, 0)
    for col in range(NY):
        shown[:, pl.ds(col * TXD * COLS, TXD * COLS)] = got[col]

    def strip_sent(n, _):
        strip_copy((me + n) % NY).wait_send()
        return 0

    lax.fori_loop(1, NY, strip_sent, 0)
    for copy in edges:
        copy.wait_send()

    def alpha_sent(n, _):
        alpha_copy((me + n) % NY, 0).wait_send()
        alpha_copy((me + n) % NY, 1).wait_send()
        return 0

    lax.fori_loop(1, NY, alpha_sent, 0)
    alpha_copy(me, 1).wait_send()
    for copy in weights.values():
        copy.wait_send()
    for q in range(4):
        for copy in raw[q] + two[q] + three[q] + [four[q], cross[q]]:
            copy.wait_send()


def spread_weights(w1, w2, band1, band2):
    for ref, band, ins, wide, step in ((w1, band1, CH + 1, DEEP1, 4), (w2, band2, OUT, DEEP2, 1)):
        chan = lax.broadcasted_iota(jnp.int32, (ins, wide), 0)
        spot = lax.broadcasted_iota(jnp.int32, (ins, wide), 1)
        pick = []
        for r in range(ROWS):
            where = chan * ROWS + r if step == 4 else chan + OUT * r
            pick.append(jnp.where(spot == where, 1.0, 0.0).astype(jnp.bfloat16))
        for dx in range(3):
            for n in range(6):
                total = None
                for dy in range(3):
                    r = n - 1 + dy - 1
                    if 0 <= r < ROWS:
                        term = jnp.dot(
                            ref[3 * dy + dx], pick[r], preferred_element_type=jnp.float32
                        )
                        total = term if total is None else total + term
                band[dx, pl.ds(n * OUT, OUT), :] = total.astype(jnp.bfloat16)


def frame(tab, payload, opacity, w1, b1, w2, b2):
    unit = (CH, ROWS, COLS)
    bf16, f32 = jnp.bfloat16, jnp.float32
    vmem = pltpu.VMEM
    dma = pltpu.SemaphoreType.DMA
    return pl.pallas_call(
        frame_kernel,
        name="frame",
        out_shape=jax.ShapeDtypeStruct((OUT, NY * TXD * COLS), bf16),
        in_specs=[
            pl.BlockSpec(memory_space=pltpu.SMEM),
            pl.BlockSpec(memory_space=pl.ANY),
            pl.BlockSpec(memory_space=pl.ANY),
        ]
        + [pl.BlockSpec(memory_space=vmem)] * 4,
        out_specs=pl.BlockSpec(memory_space=vmem),
        scratch_shapes=[
            vmem((128,) + unit, bf16),
            vmem((128, ROWS, COLS), bf16),
            vmem((128, ROWS, COLS), bf16),
            vmem((192, ROWS, COLS), bf16),
            vmem((TILES * TSTEP, ROWS, COLS), f32),
            vmem((192, ROWS, COLS), f32),
            vmem((192, ROWS, COLS), f32),
            vmem((4, 8, 2) + unit, bf16),
            vmem((4, 8, 2) + unit, bf16),
            vmem((4, 4, 3) + unit, bf16),
            vmem((4, 4, 3) + unit, f32),
            vmem((4, 4, 3) + unit, bf16),
            vmem((4, 2, 3) + unit, bf16),
            vmem((4, 2, 3) + unit, bf16),
            vmem((4, 1, 3) + unit, bf16),
            vmem((4, 1, 3) + unit, bf16),
            vmem((4, 2) + unit, bf16),
            vmem((4, 2) + unit, bf16),
            vmem((TILES, ROWS, COLS), f32),
            vmem((TYD, TXD, DEEP1, COLS), f32),
            vmem((TYD + 2, DEEP1, WIDE), bf16),
            vmem((2, DEEP1, COLS), bf16),
            vmem((2, DEEP1, COLS), bf16),
            vmem((4, DEEP1, COLS), bf16),
            vmem((3, 6 * OUT, DEEP1), bf16),
            vmem((3, 6 * OUT, DEEP2), bf16),
            vmem((18, OUT, WIDE), f32),
            vmem((TYD, DEEP2, WIDE), bf16),
            vmem((OUT, WIDE), bf16),
            vmem((OUT, WIDE), bf16),
            vmem((16, OUT, TXD * COLS), f32),
            vmem((16, OUT, TXD * COLS), bf16),
            vmem((NY, OUT, TXD * COLS), bf16),
            vmem((NY, OUT, TXD * COLS), bf16),
            dma((5,)),
            dma((32,)),
            dma((32,)),
            dma((4, 8, 2)),
            dma((4, 8, 2)),
            dma((4, 10)),
            dma((4, 10)),
            dma((4,)),
            dma((4,)),
            dma((8,)),
            dma((8,)),
            dma((NY,)),
            dma((NY,)),
        ],
        compiler_params=pltpu.CompilerParams(
            collective_id=0, has_side_effects=True, vmem_limit_bytes=48 << 20
        ),
    )(tab, payload, opacity, w1, b1, w2, b2)


def shards(
    payload, opacity, depth_order, footprints, panel_map,
    conv1_weight, conv1_bias, conv2_weight, conv2_bias,
):
    tab = tables(footprints, depth_order, panel_map, lax.axis_index("gx"), lax.axis_index("gy"))
    shown = frame(
        tab,
        payload.transpose(0, 2, 1, 3),
        opacity,
        conv1_weight,
        conv1_bias[None],
        conv2_weight,
        conv2_bias[None],
    )
    return shown[None, None, None]


SPECS = (
    P(("gx", "gy"), None, None, None),
    P(("gx", "gy"), None, None),
    P(("gx", "gy"), None),
    P(),
    P(),
    P(),
    P(),
    P(),
    P(),
)


def solution(mesh):
    return jax.shard_map(
        shards,
        mesh=mesh,
        in_specs=SPECS,
        out_specs=P("gx", "gy", None, None, None),
        check_vma=False,
    )
```

```python
import functools

import jax
import jax.numpy as jnp
import numpy as np
from jax import lax
from jax.experimental import pallas as pl
from jax.experimental.pallas import tpu as pltpu
from jax.sharding import PartitionSpec as P

MESH = pl.DeviceIdType.MESH
TYD = 4
TXD = 2
TILES = 8
DEPTH = 16
CH = 35
ROWS = 4
COLS = 128
NX = 8
NY = 16
SIDE = 4
TSTEP = DEPTH + 2
MASKS = ((4, 12, 1, 3), (12, 4, 3, 1), (1, 3, 4, 12), (3, 1, 12, 4))


def kappa(q, k):
    m = MASKS[q]
    return (m[1] if k & 4 else 0) ^ (m[2] if k & 2 else 0) ^ (m[3] if k & 1 else 0)


def flip4(p, d):
    if d == 0:
        return p
    if d == 1:
        return p + 1 - 2 * (p % 2)
    if d == 2:
        return (p + 2) % SIDE
    return 3 - p


def paired(c, mask):
    return flip4(c // SIDE, mask // SIDE) * SIDE + flip4(c % SIDE, mask % SIDE)


def patterns():
    base = np.zeros((2, 4, 8, 2), np.int32)
    rest = np.zeros((2, 4, 8, 2), np.int32)
    mask = np.zeros((4, 8, 3, 2), np.int32)
    which = np.zeros((4, 8, 3, 2), np.int32)
    for q in range(4):
        j, g = q % 2, q // 2
        for k in range(8):
            for s in range(2):
                flip = kappa(q, k) ^ (MASKS[q][0] if s else 0)
                for f in range(2):
                    jy = (1 + g) if f else (3 if g else 0)
                    base[s, q, k, f] = flip
                    rest[s, q, k, f] = jy * TXD + j
                for e in range(3):
                    jy = (1 + g) if e != 1 else (3 if g else 0)
                    mask[q, k, e, s] = flip
                    which[q, k, e, s] = jy * TXD + j + TILES * (0, 1 - g, 1)[e]
    rows = np.zeros((8, 128), np.int32)
    rows[0] = base.reshape(-1)
    rows[1] = rest.reshape(-1)
    rows[2:4].reshape(-1)[:192] = mask.reshape(-1)
    rows[4:6].reshape(-1)[:192] = which.reshape(-1)
    return rows


def fill_tables(rows, foot, order, out, gx, gy):
    i32 = jnp.int32
    own = foot[pl.ds(gx * NY + gy, 1), :]
    slot = ((own >> 3) & (NY - 1)) * TILES + (own & (TILES - 1))
    across = lax.broadcasted_iota(i32, (128, 128), 1)
    along = lax.broadcasted_iota(i32, (128, 128), 0)
    slots = jnp.sum(jnp.where(across == along, slot, 0), axis=1, keepdims=True)
    target = (rows[0:1] ^ gy) * TILES + rows[1:2]
    out[0:1] = jnp.max(jnp.where(slots == across, along, 0), axis=0, keepdims=True)
    out[1:2] = jnp.max(jnp.where(slots == target, along, 0), axis=0, keepdims=True)

    listed = order[...]
    tile = lax.broadcasted_iota(i32, (TILES, 128), 0)
    for n in range(2):
        which = rows[4 + n : 5 + n]
        local = which & (TILES - 1)
        brick = ((gx - (which >> 3)) & (NX - 1)) * NY + (rows[2 + n : 3 + n] ^ gy)
        rank = jnp.zeros((TILES, 128), i32)
        for d in range(DEPTH):
            hit = jnp.logical_and(listed[:, d : d + 1] == brick, tile == local)
            rank = jnp.minimum(rank, jnp.where(hit, d - (DEPTH + 1), 0))
        rank = jnp.min(rank, axis=0, keepdims=True)
        out[2 + n : 3 + n] = local * TSTEP + DEPTH + 1 + rank

    tile = lax.broadcasted_iota(i32, (TILES, DEPTH), 0)
    part = jnp.minimum((gx - (listed >> 4)) & (NX - 1), 1)
    spot = ((tile >> 1) - 1 + part) * TXD + (tile & 1)
    out[8:16, 0:DEPTH] = jnp.maximum((part * NY + (listed & (NY - 1))) * 6 + spot, 0)


OUT = 32
VMEM_BYTES = 62 << 20
WIDE = 3 * COLS
DEEP1 = (CH + 1) * ROWS
DEEP2 = OUT * ROWS


def frame_kernel(
    pay_h, opa_h, rows_h, foot_h, order_h, panel_h, w1_h, b1_h, w2_h, b2_h, shown,
    rows, foot, order, tabv, tab, panel, inv, w1, b1, w2, b2, tsem,
    pay, opa, asend, abuf, tb, tsend, trecv, s1, r1, s2, acc, r2, s3, r3, s4, r4, ys, yr,
    cov, stage, v1, pack, side, corner, band1, band2, h_acc, v2, v2_top, v2_low, o_acc, shaded, strips, got,
    lsem, a_s, a_r, t_s, t_r, m_s, m_r, y_s, y_r, h_s, h_r, d_s, d_r,
):
    gx = lax.axis_index("gx")
    me = lax.axis_index("gy")
    up = (gx + 1) % NX
    down = (gx + NX - 1) % NX
    early = [
        pltpu.make_async_copy(src, dst, tsem.at[n])
        for n, (src, dst) in enumerate(
            ((rows_h, rows), (foot_h, foot), (order_h, order), (opa_h, opa), (panel_h, panel),
             (w1_h, w1), (b1_h, b1), (w2_h, w2), (b2_h, b2))
        )
    ]
    loads = []
    for i in range(4):
        part = pl.ds(32 * i, 32)
        loads.append(pltpu.make_async_copy(pay_h.at[part], pay.at[part], lsem.at[i]))
    for load in early[:4] + loads + early[4:]:
        load.start()

    barrier = pltpu.get_barrier_semaphore()

    def greet_row(i, _):
        pl.semaphore_signal(barrier, inc=1, device_id=(gx, (me + i) % NY), device_id_type=MESH)
        return 0

    def greet_next(i, _):
        pl.semaphore_signal(barrier, inc=1, device_id=(up, i), device_id_type=MESH)
        pl.semaphore_signal(barrier, inc=1, device_id=(down, i), device_id_type=MESH)
        return 0

    lax.fori_loop(1, NY, greet_row, 0)
    lax.fori_loop(0, NY, greet_next, 0)

    for load in early[:3]:
        load.wait()
    fill_tables(rows, foot, order, tabv, gx, me)
    to_smem = pltpu.make_async_copy(tabv, tab, tsem.at[9])
    early[3].wait()
    to_smem.start()
    to_smem.wait()

    def pack_alpha(i, _):
        asend[i] = opa[tab[0, i]]
        return 0

    lax.fori_loop(0, 128, pack_alpha, 0, unroll=8)
    for e in range(6):
        abuf[me * 6 + e] = asend[me * TILES + 2 + e]
    for load in loads:
        load.wait()

    def pack_raw(q, lo, hi):
        def body(k, _):
            for f in range(2):
                s1[q, k, f] = pay[tab[1, 64 + (q * 8 + k) * 2 + f]]
            return 0

        lax.fori_loop(lo, hi, body, 0)

    for q in range(4):
        pack_raw(q, 2, 8)
    pl.semaphore_wait(barrier, 47)

    def alpha_copy(i, back):
        return pltpu.make_async_remote_copy(
            src_ref=asend.at[pl.ds(i * TILES + 2 - 2 * back, 6)],
            dst_ref=abuf.at[pl.ds((back * NY + me) * 6, 6)],
            send_sem=a_s.at[back * NY + i],
            recv_sem=a_r.at[back * NY + me],
            device_id=(up if back else gx, i),
            device_id_type=MESH,
        )

    def alpha_start(n, _):
        alpha_copy((me + n) % NY, 0).start()
        alpha_copy((me + n) % NY, 1).start()
        return 0

    lax.fori_loop(1, NY, alpha_start, 0)
    alpha_copy(me, 1).start()

    groups = ((4, 8), (2, 4), (1, 2), (0, 1))

    def raw_copy(q, n):
        lo, hi = groups[n]
        part = pl.ds(lo, hi - lo)
        return pltpu.make_async_remote_copy(
            src_ref=s1.at[q, part],
            dst_ref=r1.at[q, part],
            send_sem=m_s.at[q, n],
            recv_sem=m_r.at[q, n],
            device_id=(gx, paired(me, MASKS[q][0])),
            device_id_type=MESH,
        )

    raw = [[raw_copy(q, n) for n in range(4)] for q in range(4)]
    for n in range(2):
        for q in range(4):
            raw[q][n].start()
    for q in range(4):
        pack_raw(q, 0, 2)
    for load in early[4:]:
        load.wait()

    def invert(g, _):
        at = 0
        for strip in range(NY):
            at = jnp.where(panel[strip] == g, strip, at)
        inv[g] = at
        return 0

    lax.fori_loop(0, NY, invert, 0)

    spread_weights(w1, w2, band1, band2)

    def alpha_wait(n, _):
        col = (me + n) % NY
        for back in range(2):
            pltpu.make_async_remote_copy(
                src_ref=asend.at[pl.ds(0, 6)],
                dst_ref=abuf.at[pl.ds((back * NY + col) * 6, 6)],
                send_sem=a_s.at[back * NY + col],
                recv_sem=a_r.at[back * NY + col],
                device_id=(gx, col),
                device_id_type=MESH,
            ).wait_recv()
        return 0

    lax.fori_loop(1, NY, alpha_wait, 0)
    alpha_copy(me, 1).wait_recv()

    for t in range(TILES):
        tb[t * TSTEP + DEPTH + 1] = jnp.zeros((ROWS, COLS), jnp.float32)

    def through(d, passed):
        out = []
        for t in range(TILES):
            tb[t * TSTEP + d] = passed[t]
            alpha = abuf[tab[8 + t, d]].astype(jnp.float32)
            out.append(passed[t] * (1.0 - alpha))
        return tuple(out)

    last = lax.fori_loop(
        0, DEPTH, through, tuple(jnp.ones((ROWS, COLS), jnp.float32) for _ in range(TILES))
    )
    for t in range(TILES):
        cov[t] = 1.0 - last[t]

    def fill(i, _):
        tsend[i] = tb[tab[2 + i // 128, i % 128]]
        return 0

    lax.fori_loop(0, 192, fill, 0, unroll=8)

    def weight_range(q, k, back):
        g = q // 2
        start, size = ((0, 4 if g else 2), (4 if g else 2, 2 if g else 4))[back]
        return pl.ds((q * 8 + k) * 6 + start, size)

    def weight_copy(q, k, back):
        part = weight_range(q, k, back)
        return pltpu.make_async_remote_copy(
            src_ref=tsend.at[part],
            dst_ref=trecv.at[part],
            send_sem=t_s.at[q, k, back],
            recv_sem=t_r.at[q, k, back],
            device_id=(down if back else gx, paired(me, kappa(q, k))),
            device_id_type=MESH,
        )

    weights = {}
    for k in (7, 6, 5, 4, 3, 2, 1, 0):
        for q in range(4):
            for back in range(2):
                if k == 0 and back == 0:
                    g = q // 2
                    for e in range(4 if g else 2):
                        trecv[q * 48 + e] = tsend[q * 48 + e]
                else:
                    weights[q, k, back] = weight_copy(q, k, back)
                    weights[q, k, back].start()
    for n in range(2, 4):
        for q in range(4):
            raw[q][n].start()

    def weighed(q, k):
        own = (q * 8 + k) * 2
        lead = (q * 8 + k) * 6
        own_f = pay[tab[1, own]].astype(jnp.float32)
        got_f = r1[q, k, 0].astype(jnp.float32)
        mid = trecv[lead + 2][None] * own_f + trecv[lead + 3][None] * got_f
        own_a = pay[tab[1, own + 1]].astype(jnp.float32)
        got_a = r1[q, k, 1].astype(jnp.float32)
        first = trecv[lead][None] * own_a + trecv[lead + 1][None] * got_a
        third = trecv[lead + 4][None] * own_a + trecv[lead + 5][None] * got_a
        return first, mid, third

    def merge_sent(q, lo, hi):
        def body(k, _):
            for e, v in enumerate(weighed(q, k)):
                s2[q, k - 4, e] = v.astype(jnp.bfloat16)
            return 0

        lax.fori_loop(lo, hi, body, 0)

    def merge_kept(q, lo, hi):
        def body(k, _):
            for e, v in enumerate(weighed(q, k)):
                acc[q, k, e] = v
            return 0

        lax.fori_loop(lo, hi, body, 0)

    def step_copy(src, dst, q, lo, hi, step, sem):
        part = pl.ds(lo, hi - lo)
        return pltpu.make_async_remote_copy(
            src_ref=src.at[q, part],
            dst_ref=dst.at[q, part],
            send_sem=m_s.at[q, sem],
            recv_sem=m_r.at[q, sem],
            device_id=(gx, paired(me, MASKS[q][step - 1])),
            device_id_type=MESH,
        )

    def wait_weights(q, lo, hi):
        for k in range(lo, hi):
            for back in range(2):
                if (q, k, back) in weights:
                    weights[q, k, back].wait_recv()

    two = [[step_copy(s2, r2, q, lo, hi, 2, 4 + n) for n, (lo, hi) in enumerate(groups[1:])] for q in range(4)]
    three = [[step_copy(s3, r3, q, lo, hi, 3, 7 + n) for n, (lo, hi) in enumerate(groups[2:])] for q in range(4)]
    four = [step_copy(s4, r4, q, 0, 1, 4, 9) for q in range(4)]

    for q in range(4):
        wait_weights(q, 4, 8)
        raw[q][0].wait_recv()
        merge_sent(q, 6, 8)
        two[q][0].start()
    for q in range(4):
        merge_sent(q, 4, 6)
        two[q][1].start()
        two[q][2].start()
    for q in range(4):
        wait_weights(q, 0, 4)
        for n in range(1, 4):
            raw[q][n].wait_recv()
        merge_kept(q, 0, 4)

    def added(src, q, k):
        return [acc[q, k, e] + src[q, k, e].astype(jnp.float32) for e in range(3)]

    def forward(dst, src, q, k, to):
        for e, v in enumerate(added(src, q, k)):
            dst[q, to, e] = v.astype(jnp.bfloat16)

    def keep(src, q, k):
        for e, v in enumerate(added(src, q, k)):
            acc[q, k, e] = v

    for q in range(4):
        two[q][0].wait_recv()
        forward(s3, r2, q, 3, 1)
        three[q][0].start()
        forward(s3, r2, q, 2, 0)
        three[q][1].start()
    for q in range(4):
        two[q][1].wait_recv()
        keep(r2, q, 1)
        two[q][2].wait_recv()
        keep(r2, q, 0)
    for q in range(4):
        three[q][0].wait_recv()
        forward(s4, r3, q, 1, 0)
        four[q].start()
    for q in range(4):
        three[q][1].wait_recv()
        keep(r3, q, 0)

    def cross_copy(q):
        part = pl.ds(q // 2, 2 - q // 2)
        return pltpu.make_async_remote_copy(
            src_ref=ys.at[q, part],
            dst_ref=yr.at[q, part],
            send_sem=y_s.at[q],
            recv_sem=y_r.at[q],
            device_id=(up, me),
            device_id_type=MESH,
        )

    cross = [cross_copy(q) for q in range(4)]
    right = (me + 1) % NY
    left = (me + NY - 1) % NY

    def place(jy, j, v):
        lanes = pl.ds(j * COLS, COLS)
        for c in range(CH):
            stage[jy, j, pl.ds(c * ROWS, ROWS), :] = v[c]
        stage[jy, j, pl.ds(CH * ROWS, ROWS), :] = cov[jy * TXD + j]
        v1[jy + 1, :, lanes] = stage[jy, j].astype(jnp.bfloat16)

    def edge_copy(src, dst, n, row, col):
        return pltpu.make_async_remote_copy(
            src_ref=src,
            dst_ref=dst,
            send_sem=h_s.at[n],
            recv_sem=h_r.at[n],
            device_id=(row, col),
            device_id_type=MESH,
        )

    mine = pl.ds(0, TXD * COLS)
    low = pl.ds(0, COLS)
    high = pl.ds(COLS, COLS)
    edges = (
        edge_copy(v1.at[4, :, mine], v1.at[0, :, mine], 0, up, me),
        edge_copy(v1.at[4, :, high], corner.at[0], 1, up, right),
        edge_copy(v1.at[4, :, low], corner.at[1], 2, up, left),
        edge_copy(v1.at[1, :, mine], v1.at[5, :, mine], 3, down, me),
        edge_copy(v1.at[1, :, high], corner.at[2], 4, down, right),
        edge_copy(v1.at[1, :, low], corner.at[3], 5, down, left),
        edge_copy(pack.at[0], side.at[0], 6, gx, right),
        edge_copy(pack.at[1], side.at[1], 7, gx, left),
    )

    for q in range(4):
        g, j = q // 2, q % 2
        four[q].wait_recv()
        first, mid, third = added(r4, q, 0)
        ys[q, 1] = third.astype(jnp.bfloat16)
        if g == 0:
            ys[q, 0] = mid.astype(jnp.bfloat16)
        cross[q].start()
        acc[q, 0, 0] = first
        if g:
            place(3, j, mid)
    for n in range(3):
        edges[n].start()
    for q in range(4):
        g, j = q // 2, q % 2
        cross[q].wait_recv()
        if g == 0:
            place(0, j, yr[q, 0].astype(jnp.float32))
        place(1 + g, j, acc[q, 0, 0] + yr[q, 1].astype(jnp.float32))
        if q == 1:
            for n in range(3, 6):
                edges[n].start()

    lane = lax.broadcasted_iota(jnp.int32, (DEEP1, COLS), 1)
    to_right = stage[0, 1]
    to_left = stage[0, 0]
    for jy in range(1, TYD):
        spot = (lane // 2) == (COLS // 2 - 1 - jy)
        to_right = jnp.where(spot, pltpu.roll(stage[jy, 1], COLS - 2 * jy, 1), to_right)
        spot = (lane // 2) == jy
        to_left = jnp.where(spot, pltpu.roll(stage[jy, 0], 2 * jy, 1), to_left)
    pack[0] = to_right.astype(jnp.bfloat16)
    pack[1] = to_left.astype(jnp.bfloat16)
    edges[6].start()
    edges[7].start()
    for copy in edges:
        copy.wait_recv()

    on_right = jnp.logical_and(lane < COLS // 2, me < NY - 1)
    on_left = jnp.logical_and(lane >= COLS // 2, me > 0)
    last_tile = pl.ds(2 * COLS, COLS)
    zero = jnp.zeros((DEEP1, COLS), jnp.float32)
    from_left = side[0].astype(jnp.float32)
    from_right = side[1].astype(jnp.float32)
    for jy in range(TYD):
        r_part = pltpu.roll(from_right, COLS - 2 * jy, 1) if jy else from_right
        l_part = pltpu.roll(from_left, 2 * jy, 1) if jy else from_left
        rim = jnp.where(on_right, r_part, jnp.where(on_left, l_part, zero))
        v1[jy + 1, :, last_tile] = rim.astype(jnp.bfloat16)
    wide_zero = jnp.zeros((DEEP1, TXD * COLS), jnp.bfloat16)
    for blk, base, inside in ((0, 0, gx > 0), (5, 2, gx < NX - 1)):
        l_part = corner[base].astype(jnp.float32)
        r_part = corner[base + 1].astype(jnp.float32)
        rim = jnp.where(on_right, r_part, jnp.where(on_left, l_part, zero))
        rim = jnp.where(inside, rim, zero)
        v1[blk, :, last_tile] = rim.astype(jnp.bfloat16)

        @pl.when(jnp.logical_not(inside))
        def _(blk=blk):
            v1[blk, :, mine] = wide_zero

    def product(band, rows, field):
        total = None
        for dx in range(3):
            z = jnp.dot(band(dx, rows), field, preferred_element_type=jnp.float32)
            if dx != 1:
                z = pltpu.roll(z, (1 - dx) % WIDE, 1)
            total = z if total is None else total + z
        return total

    def band_one(dx, rows):
        return band1[dx, rows, :]

    def band_two(dx, rows):
        return band2[dx, rows, :]

    def column(ref):
        eye = lax.broadcasted_iota(jnp.int32, (OUT, OUT), 0) == lax.broadcasted_iota(jnp.int32, (OUT, OUT), 1)
        return jnp.sum(jnp.where(eye, ref[...], 0.0), axis=1, keepdims=True)

    every = pl.ds(0, 6 * OUT)
    head = product(band_one, pl.ds(4 * OUT, 2 * OUT), v1[0])
    h_acc[0] = head[:OUT]
    h_acc[1] = head[OUT:]
    for blk in range(TYD):
        s = product(band_one, every, v1[blk + 1])
        y = 4 * blk
        for n in range(6):
            piece = s[n * OUT : (n + 1) * OUT]
            h_acc[y + n] = piece + h_acc[y + n] if n < 2 else piece
    tail = product(band_one, pl.ds(0, 2 * OUT), v1[5])
    bias_one = column(b1)
    far = lax.broadcasted_iota(jnp.int32, (OUT, WIDE), 1)
    cut = jnp.logical_or(
        jnp.logical_and(far >= 2 * COLS + COLS // 2, me == 0),
        jnp.logical_and(
            jnp.logical_and(far >= 2 * COLS, far < 2 * COLS + COLS // 2), me == NY - 1
        ),
    )
    for n in range(18):
        raw_sum = h_acc[n]
        if n >= 16:
            raw_sum = raw_sum + tail[(n - 16) * OUT : (n - 15) * OUT]
        pre = raw_sum + bias_one
        h = pre * lax.logistic(pre)
        h = jnp.where(cut, 0.0, h)
        if n == 0:
            v2_top[...] = jnp.where(gx > 0, h, 0.0).astype(jnp.bfloat16)
        elif n == 17:
            v2_low[...] = jnp.where(gx < NX - 1, h, 0.0).astype(jnp.bfloat16)
        else:
            v2[(n - 1) // 4, pl.ds((n - 1) % 4 * OUT, OUT), :] = h.astype(jnp.bfloat16)

    o_acc[0] = product(lambda dx, rows: w2[dx], every, v2_top[...])[:, : TXD * COLS]
    for blk in range(TYD):
        s = product(band_two, every, v2[blk])[:, : TXD * COLS]
        y = 4 * blk - 1
        for n in range(6):
            piece = s[n * OUT : (n + 1) * OUT]
            if 0 <= y + n < 16:
                o_acc[y + n] = piece + o_acc[y + n] if n < 2 else piece
    tail = product(lambda dx, rows: w2[6 + dx], every, v2_low[...])[:, : TXD * COLS]
    bias_two = column(b2)
    for n in range(16):
        rows = pl.ds(n % 4, OUT, stride=ROWS)
        base = jnp.concatenate([stage[n // 4, j, rows, :] for j in range(TXD)], axis=1)
        value = o_acc[n] + bias_two + base.astype(jnp.bfloat16).astype(jnp.float32)
        if n == 15:
            value = value + tail
        shaded[n] = value.astype(jnp.bfloat16)

    def strip_copy(g):
        return pltpu.make_async_remote_copy(
            src_ref=strips.at[g],
            dst_ref=got.at[me],
            send_sem=d_s.at[g],
            recv_sem=d_r.at[me],
            device_id=(gx, g),
            device_id_type=MESH,
        )

    def strip_start(n, _):
        g = (me + n) % NY
        strips[g] = shaded[inv[g]]
        strip_copy(g).start()
        return 0

    lax.fori_loop(1, NY, strip_start, 0)
    got[me] = shaded[inv[me]]

    def strip_wait(n, _):
        col = (me + n) % NY
        pltpu.make_async_remote_copy(
            src_ref=strips.at[col],
            dst_ref=got.at[col],
            send_sem=d_s.at[col],
            recv_sem=d_r.at[col],
            device_id=(gx, col),
            device_id_type=MESH,
        ).wait_recv()
        return 0

    lax.fori_loop(1, NY, strip_wait, 0)
    for col in range(NY):
        shown[:, pl.ds(col * TXD * COLS, TXD * COLS)] = got[col]

    def strip_sent(n, _):
        strip_copy((me + n) % NY).wait_send()
        return 0

    lax.fori_loop(1, NY, strip_sent, 0)
    for copy in edges:
        copy.wait_send()

    def alpha_sent(n, _):
        alpha_copy((me + n) % NY, 0).wait_send()
        alpha_copy((me + n) % NY, 1).wait_send()
        return 0

    lax.fori_loop(1, NY, alpha_sent, 0)
    alpha_copy(me, 1).wait_send()
    for copy in weights.values():
        copy.wait_send()
    for q in range(4):
        for copy in raw[q] + two[q] + three[q] + [four[q], cross[q]]:
            copy.wait_send()


def spread_weights(w1, w2, band1, band2):
    for ref, band, ins, wide, step in ((w1, band1, CH + 1, DEEP1, 4), (w2, band2, OUT, DEEP2, 1)):
        chan = lax.broadcasted_iota(jnp.int32, (ins, wide), 0)
        spot = lax.broadcasted_iota(jnp.int32, (ins, wide), 1)
        pick = []
        for r in range(ROWS):
            where = chan * ROWS + r if step == 4 else chan + OUT * r
            pick.append(jnp.where(spot == where, 1.0, 0.0).astype(jnp.bfloat16))
        for dx in range(3):
            for n in range(6):
                total = None
                for dy in range(3):
                    r = n - 1 + dy - 1
                    if 0 <= r < ROWS:
                        term = jnp.dot(
                            ref[3 * dy + dx], pick[r], preferred_element_type=jnp.float32
                        )
                        total = term if total is None else total + term
                band[dx, pl.ds(n * OUT, OUT), :] = total.astype(jnp.bfloat16)


def frame(*operands):
    unit = (CH, ROWS, COLS)
    bf16, f32 = jnp.bfloat16, jnp.float32
    vmem = pltpu.VMEM
    dma = pltpu.SemaphoreType.DMA
    return pl.pallas_call(
        frame_kernel,
        name="frame",
        out_shape=jax.ShapeDtypeStruct((OUT, NY * TXD * COLS), bf16),
        in_specs=[pl.BlockSpec(memory_space=pl.ANY)] * len(operands),
        out_specs=pl.BlockSpec(memory_space=vmem),
        scratch_shapes=[
            vmem((8, 128), jnp.int32),
            vmem((128, 128), jnp.int32),
            vmem((TILES, DEPTH), jnp.int32),
            vmem((16, 128), jnp.int32),
            pltpu.SMEM((16, 128), jnp.int32),
            pltpu.SMEM((NY,), jnp.int32),
            pltpu.SMEM((NY,), jnp.int32),
            vmem((9, OUT, CH + 1), bf16),
            vmem((1, OUT), f32),
            vmem((9, OUT, OUT), bf16),
            vmem((1, OUT), f32),
            dma((10,)),
            vmem((128,) + unit, bf16),
            vmem((128, ROWS, COLS), bf16),
            vmem((128, ROWS, COLS), bf16),
            vmem((192, ROWS, COLS), bf16),
            vmem((TILES * TSTEP, ROWS, COLS), f32),
            vmem((192, ROWS, COLS), f32),
            vmem((192, ROWS, COLS), f32),
            vmem((4, 8, 2) + unit, bf16),
            vmem((4, 8, 2) + unit, bf16),
            vmem((4, 4, 3) + unit, bf16),
            vmem((4, 4, 3) + unit, f32),
            vmem((4, 4, 3) + unit, bf16),
            vmem((4, 2, 3) + unit, bf16),
            vmem((4, 2, 3) + unit, bf16),
            vmem((4, 1, 3) + unit, bf16),
            vmem((4, 1, 3) + unit, bf16),
            vmem((4, 2) + unit, bf16),
            vmem((4, 2) + unit, bf16),
            vmem((TILES, ROWS, COLS), f32),
            vmem((TYD, TXD, DEEP1, COLS), f32),
            vmem((TYD + 2, DEEP1, WIDE), bf16),
            vmem((2, DEEP1, COLS), bf16),
            vmem((2, DEEP1, COLS), bf16),
            vmem((4, DEEP1, COLS), bf16),
            vmem((3, 6 * OUT, DEEP1), bf16),
            vmem((3, 6 * OUT, DEEP2), bf16),
            vmem((18, OUT, WIDE), f32),
            vmem((TYD, DEEP2, WIDE), bf16),
            vmem((OUT, WIDE), bf16),
            vmem((OUT, WIDE), bf16),
            vmem((16, OUT, TXD * COLS), f32),
            vmem((16, OUT, TXD * COLS), bf16),
            vmem((NY, OUT, TXD * COLS), bf16),
            vmem((NY, OUT, TXD * COLS), bf16),
            dma((4,)),
            dma((32,)),
            dma((32,)),
            dma((4, 8, 2)),
            dma((4, 8, 2)),
            dma((4, 10)),
            dma((4, 10)),
            dma((4,)),
            dma((4,)),
            dma((8,)),
            dma((8,)),
            dma((NY,)),
            dma((NY,)),
        ],
        compiler_params=pltpu.CompilerParams(
            collective_id=0, has_side_effects=True, vmem_limit_bytes=VMEM_BYTES
        ),
    )(*operands)


def shards(
    payload, opacity, depth_order, footprints, panel_map,
    conv1_weight, conv1_bias, conv2_weight, conv2_bias,
):
    shown = frame(
        payload.transpose(0, 2, 1, 3),
        opacity,
        jnp.asarray(patterns()),
        footprints,
        depth_order,
        panel_map,
        conv1_weight,
        conv1_bias[None],
        conv2_weight,
        conv2_bias[None],
    )
    return shown[None, None, None]


SPECS = (
    P(("gx", "gy"), None, None, None),
    P(("gx", "gy"), None, None),
    P(("gx", "gy"), None),
    P(),
    P(),
    P(),
    P(),
    P(),
    P(),
)


def solution(mesh):
    return jax.shard_map(
        shards,
        mesh=mesh,
        in_specs=SPECS,
        out_specs=P("gx", "gy", None, None, None),
        check_vma=False,
    )
```

```python
import functools

import jax
import jax.numpy as jnp
import numpy as np
from jax import lax
from jax.experimental import pallas as pl
from jax.experimental.pallas import tpu as pltpu
from jax.sharding import PartitionSpec as P

MESH = pl.DeviceIdType.MESH
TYD = 4
TXD = 2
TILES = 8
DEPTH = 16
CH = 35
ROWS = 4
COLS = 128
NX = 8
NY = 16
SIDE = 4
TSTEP = DEPTH + 2
MASKS = ((4, 12, 1, 3), (12, 4, 3, 1), (1, 3, 4, 12), (3, 1, 12, 4))


def kappa(q, k):
    m = MASKS[q]
    return (m[1] if k & 4 else 0) ^ (m[2] if k & 2 else 0) ^ (m[3] if k & 1 else 0)


def flip4(p, d):
    if d == 0:
        return p
    if d == 1:
        return p + 1 - 2 * (p % 2)
    if d == 2:
        return (p + 2) % SIDE
    return 3 - p


def paired(c, mask):
    return flip4(c // SIDE, mask // SIDE) * SIDE + flip4(c % SIDE, mask % SIDE)


def patterns():
    base = np.zeros((2, 4, 8, 2), np.int32)
    rest = np.zeros((2, 4, 8, 2), np.int32)
    mask = np.zeros((4, 8, 3, 2), np.int32)
    which = np.zeros((4, 8, 3, 2), np.int32)
    for q in range(4):
        j, g = q % 2, q // 2
        for k in range(8):
            for s in range(2):
                flip = kappa(q, k) ^ (MASKS[q][0] if s else 0)
                for f in range(2):
                    jy = (1 + g) if f else (3 if g else 0)
                    base[s, q, k, f] = flip
                    rest[s, q, k, f] = jy * TXD + j
                for e in range(3):
                    jy = (1 + g) if e != 1 else (3 if g else 0)
                    mask[q, k, e, s] = flip
                    which[q, k, e, s] = jy * TXD + j + TILES * (0, 1 - g, 1)[e]
    rows = np.zeros((8, 128), np.int32)
    rows[0] = base.reshape(-1)
    rows[1] = rest.reshape(-1)
    rows[2:4].reshape(-1)[:192] = mask.reshape(-1)
    rows[4:6].reshape(-1)[:192] = which.reshape(-1)
    return rows


def fill_tables(rows, foot, order, out, gx, gy):
    i32 = jnp.int32
    own = foot[pl.ds(gx * NY + gy, 1), :]
    slot = ((own >> 3) & (NY - 1)) * TILES + (own & (TILES - 1))
    across = lax.broadcasted_iota(i32, (128, 128), 1)
    along = lax.broadcasted_iota(i32, (128, 128), 0)
    slots = jnp.sum(jnp.where(across == along, slot, 0), axis=1, keepdims=True)
    target = (rows[0:1] ^ gy) * TILES + rows[1:2]
    out[0:1] = jnp.max(jnp.where(slots == across, along, 0), axis=0, keepdims=True)
    out[1:2] = jnp.max(jnp.where(slots == target, along, 0), axis=0, keepdims=True)

    listed = order[...]
    tile = lax.broadcasted_iota(i32, (TILES, 128), 0)
    for n in range(2):
        which = rows[4 + n : 5 + n]
        local = which & (TILES - 1)
        brick = ((gx - (which >> 3)) & (NX - 1)) * NY + (rows[2 + n : 3 + n] ^ gy)
        rank = jnp.zeros((TILES, 128), i32)
        for d in range(DEPTH):
            hit = jnp.logical_and(listed[:, d : d + 1] == brick, tile == local)
            rank = jnp.minimum(rank, jnp.where(hit, d - (DEPTH + 1), 0))
        rank = jnp.min(rank, axis=0, keepdims=True)
        out[2 + n : 3 + n] = local * TSTEP + DEPTH + 1 + rank

    tile = lax.broadcasted_iota(i32, (TILES, DEPTH), 0)
    part = jnp.minimum((gx - (listed >> 4)) & (NX - 1), 1)
    spot = ((tile >> 1) - 1 + part) * TXD + (tile & 1)
    out[8:16, 0:DEPTH] = jnp.maximum((part * NY + (listed & (NY - 1))) * 6 + spot, 0)


OUT = 32
VMEM_BYTES = 62 << 20
WIDE = 3 * COLS
DEEP1 = (CH + 1) * ROWS
DEEP2 = OUT * ROWS


def frame_kernel(
    pay_h, opa_h, rows_h, foot_h, order_h, panel_h, w1_h, b1_h, w2_h, b2_h, shown,
    rows, foot, order, tabv, tab, panel, inv, w1, b1, w2, b2, tsem,
    pay, opa, asend, abuf, tb, tsend, trecv, s1, r1, s2, acc, r2, s3, r3, s4, r4, ys, yr,
    cov, cov_side, cov_over, cov_under, stage, stage_y, v1, pack, rim, edge, band1, band2, h_acc, v2, v2_top, v2_low, o_acc, shaded, strips, got,
    lsem, a_s, a_r, t_s, t_r, m_s, m_r, y_s, y_r, c_s, c_r, h_s, h_r, d_s, d_r,
):
    gx = lax.axis_index("gx")
    me = lax.axis_index("gy")
    up = (gx + 1) % NX
    down = (gx + NX - 1) % NX
    early = [
        pltpu.make_async_copy(src, dst, tsem.at[n])
        for n, (src, dst) in enumerate(
            ((rows_h, rows), (foot_h, foot), (order_h, order), (opa_h, opa), (panel_h, panel),
             (w1_h, w1), (b1_h, b1), (w2_h, w2), (b2_h, b2))
        )
    ]
    loads = []
    for i in range(4):
        part = pl.ds(32 * i, 32)
        loads.append(pltpu.make_async_copy(pay_h.at[part], pay.at[part], lsem.at[i]))
    for load in early[:4] + loads + early[4:]:
        load.start()

    barrier = pltpu.get_barrier_semaphore()

    def greet_row(i, _):
        pl.semaphore_signal(barrier, inc=1, device_id=(gx, (me + i) % NY), device_id_type=MESH)
        return 0

    def greet_next(i, _):
        pl.semaphore_signal(barrier, inc=1, device_id=(up, i), device_id_type=MESH)
        pl.semaphore_signal(barrier, inc=1, device_id=(down, i), device_id_type=MESH)
        return 0

    lax.fori_loop(1, NY, greet_row, 0)
    lax.fori_loop(0, NY, greet_next, 0)

    for load in early[:3]:
        load.wait()
    fill_tables(rows, foot, order, tabv, gx, me)
    to_smem = pltpu.make_async_copy(tabv, tab, tsem.at[9])
    early[3].wait()
    to_smem.start()
    to_smem.wait()

    def pack_alpha(i, _):
        asend[i] = opa[tab[0, i]]
        return 0

    lax.fori_loop(0, 128, pack_alpha, 0, unroll=8)
    for e in range(6):
        abuf[me * 6 + e] = asend[me * TILES + 2 + e]
    for load in loads:
        load.wait()

    def pack_raw(q, lo, hi):
        def body(k, _):
            for f in range(2):
                s1[q, k, f] = pay[tab[1, 64 + (q * 8 + k) * 2 + f]]
            return 0

        lax.fori_loop(lo, hi, body, 0)

    for q in range(4):
        pack_raw(q, 2, 8)
    pl.semaphore_wait(barrier, 47)

    def alpha_copy(i, back):
        return pltpu.make_async_remote_copy(
            src_ref=asend.at[pl.ds(i * TILES + 2 - 2 * back, 6)],
            dst_ref=abuf.at[pl.ds((back * NY + me) * 6, 6)],
            send_sem=a_s.at[back * NY + i],
            recv_sem=a_r.at[back * NY + me],
            device_id=(up if back else gx, i),
            device_id_type=MESH,
        )

    def alpha_start(n, _):
        alpha_copy((me + n) % NY, 0).start()
        alpha_copy((me + n) % NY, 1).start()
        return 0

    lax.fori_loop(1, NY, alpha_start, 0)
    alpha_copy(me, 1).start()

    groups = ((4, 8), (2, 4), (1, 2), (0, 1))

    def raw_copy(q, n):
        lo, hi = groups[n]
        part = pl.ds(lo, hi - lo)
        return pltpu.make_async_remote_copy(
            src_ref=s1.at[q, part],
            dst_ref=r1.at[q, part],
            send_sem=m_s.at[q, n],
            recv_sem=m_r.at[q, n],
            device_id=(gx, paired(me, MASKS[q][0])),
            device_id_type=MESH,
        )

    raw = [[raw_copy(q, n) for n in range(4)] for q in range(4)]
    for n in range(2):
        for q in range(4):
            raw[q][n].start()
    for q in range(4):
        pack_raw(q, 0, 2)
    for load in early[4:]:
        load.wait()

    def invert(g, _):
        at = 0
        for strip in range(NY):
            at = jnp.where(panel[strip] == g, strip, at)
        inv[g] = at
        return 0

    lax.fori_loop(0, NY, invert, 0)

    spread_weights(w1, w2, band1, band2)

    def alpha_wait(n, _):
        col = (me + n) % NY
        for back in range(2):
            pltpu.make_async_remote_copy(
                src_ref=asend.at[pl.ds(0, 6)],
                dst_ref=abuf.at[pl.ds((back * NY + col) * 6, 6)],
                send_sem=a_s.at[back * NY + col],
                recv_sem=a_r.at[back * NY + col],
                device_id=(gx, col),
                device_id_type=MESH,
            ).wait_recv()
        return 0

    lax.fori_loop(1, NY, alpha_wait, 0)
    alpha_copy(me, 1).wait_recv()

    for t in range(TILES):
        tb[t * TSTEP + DEPTH + 1] = jnp.zeros((ROWS, COLS), jnp.float32)

    def through(d, passed):
        out = []
        for t in range(TILES):
            tb[t * TSTEP + d] = passed[t]
            alpha = abuf[tab[8 + t, d]].astype(jnp.float32)
            out.append(passed[t] * (1.0 - alpha))
        return tuple(out)

    last = lax.fori_loop(
        0, DEPTH, through, tuple(jnp.ones((ROWS, COLS), jnp.float32) for _ in range(TILES))
    )
    for t in range(TILES):
        cov[t] = (1.0 - last[t]).astype(jnp.bfloat16)

    def fill(i, _):
        tsend[i] = tb[tab[2, i]]
        return 0

    def fill_rest(i, _):
        tsend[128 + i] = tb[tab[3, i]]
        return 0

    lax.fori_loop(0, 128, fill, 0, unroll=8)
    lax.fori_loop(0, 64, fill_rest, 0, unroll=8)

    def weight_range(q, k, back):
        g = q // 2
        start, size = ((0, 4 if g else 2), (4 if g else 2, 2 if g else 4))[back]
        return pl.ds((q * 8 + k) * 6 + start, size)

    def weight_copy(q, k, back):
        part = weight_range(q, k, back)
        return pltpu.make_async_remote_copy(
            src_ref=tsend.at[part],
            dst_ref=trecv.at[part],
            send_sem=t_s.at[q, k, back],
            recv_sem=t_r.at[q, k, back],
            device_id=(down if back else gx, paired(me, kappa(q, k))),
            device_id_type=MESH,
        )

    weights = {}
    for k in (7, 6, 5, 4, 3, 2, 1, 0):
        for q in range(4):
            for back in range(2):
                if k == 0 and back == 0:
                    g = q // 2
                    for e in range(4 if g else 2):
                        trecv[q * 48 + e] = tsend[q * 48 + e]
                else:
                    weights[q, k, back] = weight_copy(q, k, back)
                    weights[q, k, back].start()
    right = (me + 1) % NY
    left = (me + NY - 1) % NY
    first_row = pl.ds(0, TXD)
    last_row = pl.ds((TYD - 1) * TXD, TXD)
    covers = [
        pltpu.make_async_remote_copy(
            src_ref=src,
            dst_ref=dst,
            send_sem=c_s.at[n],
            recv_sem=c_r.at[n],
            device_id=(row, col),
            device_id_type=MESH,
        )
        for n, (src, dst, row, col) in enumerate(
            (
                (cov, cov_side.at[0], gx, right),
                (cov, cov_side.at[1], gx, left),
                (cov.at[last_row], cov_over.at[0], up, right),
                (cov.at[last_row], cov_over.at[1], up, left),
                (cov.at[first_row], cov_under.at[0], down, right),
                (cov.at[first_row], cov_under.at[1], down, left),
                (cov.at[first_row], cov_under.at[2], down, me),
            )
        )
    ]
    for copy in covers:
        copy.start()
    for n in range(2, 4):
        for q in range(4):
            raw[q][n].start()

    def weighed(q, k):
        own = (q * 8 + k) * 2
        lead = (q * 8 + k) * 6
        own_f = pay[tab[1, own]].astype(jnp.float32)
        got_f = r1[q, k, 0].astype(jnp.float32)
        mid = trecv[lead + 2][None] * own_f + trecv[lead + 3][None] * got_f
        own_a = pay[tab[1, own + 1]].astype(jnp.float32)
        got_a = r1[q, k, 1].astype(jnp.float32)
        first = trecv[lead][None] * own_a + trecv[lead + 1][None] * got_a
        third = trecv[lead + 4][None] * own_a + trecv[lead + 5][None] * got_a
        return first, mid, third

    def merge_sent(q, lo, hi):
        def body(k, _):
            for e, v in enumerate(weighed(q, k)):
                s2[q, k - 4, e] = v.astype(jnp.bfloat16)
            return 0

        lax.fori_loop(lo, hi, body, 0)

    def merge_kept(q, lo, hi):
        def body(k, _):
            for e, v in enumerate(weighed(q, k)):
                acc[q, k, e] = v
            return 0

        lax.fori_loop(lo, hi, body, 0)

    def step_copy(src, dst, q, lo, hi, step, sem):
        part = pl.ds(lo, hi - lo)
        return pltpu.make_async_remote_copy(
            src_ref=src.at[q, part],
            dst_ref=dst.at[q, part],
            send_sem=m_s.at[q, sem],
            recv_sem=m_r.at[q, sem],
            device_id=(gx, paired(me, MASKS[q][step - 1])),
            device_id_type=MESH,
        )

    def wait_weights(q, lo, hi):
        for k in range(lo, hi):
            for back in range(2):
                if (q, k, back) in weights:
                    weights[q, k, back].wait_recv()

    two = [[step_copy(s2, r2, q, lo, hi, 2, 4 + n) for n, (lo, hi) in enumerate(groups[1:])] for q in range(4)]
    three = [[step_copy(s3, r3, q, lo, hi, 3, 7 + n) for n, (lo, hi) in enumerate(groups[2:])] for q in range(4)]

    def last_copy(q, crossing):
        size = 2 - q // 2 if crossing else 1 + q // 2
        part = pl.ds(1 + q // 2 if crossing else 0, size)
        return pltpu.make_async_remote_copy(
            src_ref=s4.at[q, 0, part],
            dst_ref=r4.at[q, 0, part],
            send_sem=m_s.at[q, 9 + crossing],
            recv_sem=m_r.at[q, 9 + crossing],
            device_id=(gx, paired(me, MASKS[q][3])),
            device_id_type=MESH,
        )

    four = [[last_copy(q, crossing) for crossing in range(2)] for q in range(4)]

    for q in range(4):
        wait_weights(q, 4, 8)
        raw[q][0].wait_recv()
        merge_sent(q, 6, 8)
        two[q][0].start()
    for q in range(4):
        merge_sent(q, 4, 6)
        two[q][1].start()
        two[q][2].start()
    for q in range(4):
        wait_weights(q, 0, 4)
        for n in range(1, 4):
            raw[q][n].wait_recv()
        merge_kept(q, 0, 4)

    def added(src, q, k):
        return [acc[q, k, e] + src[q, k, e].astype(jnp.float32) for e in range(3)]

    def forward(dst, src, q, k, to):
        for e, v in enumerate(added(src, q, k)):
            dst[q, to, e] = v.astype(jnp.bfloat16)

    def keep(src, q, k):
        for e, v in enumerate(added(src, q, k)):
            acc[q, k, e] = v

    for q in range(4):
        two[q][0].wait_recv()
        forward(s3, r2, q, 3, 1)
        three[q][0].start()
        forward(s3, r2, q, 2, 0)
        three[q][1].start()
    for q in range(4):
        two[q][1].wait_recv()
        keep(r2, q, 1)
        two[q][2].wait_recv()
        keep(r2, q, 0)
    for q in range(4):
        three[q][0].wait_recv()
        forward(s4, r3, q, 1, 0)
        four[q][1].start()
        four[q][0].start()
    for q in range(4):
        three[q][1].wait_recv()
        keep(r3, q, 0)

    def cross_copy(q):
        part = pl.ds(q // 2, 2 - q // 2)
        return pltpu.make_async_remote_copy(
            src_ref=ys.at[q, part],
            dst_ref=yr.at[q, part],
            send_sem=y_s.at[q],
            recv_sem=y_r.at[q],
            device_id=(up, me),
            device_id_type=MESH,
        )

    cross = [cross_copy(q) for q in range(4)]

    def spread(ref, v):
        for c in range(CH):
            ref[pl.ds(c * ROWS, ROWS), :] = v[c]

    def place(jy, j, v):
        spread(stage.at[jy, j], v)
        stage[jy, j, pl.ds(CH * ROWS, ROWS), :] = cov[jy * TXD + j].astype(jnp.float32)
        v1[jy + 1, :, pl.ds(j * COLS, COLS)] = stage[jy, j].astype(jnp.bfloat16)

    def final(q, e):
        return acc[q, 0, e] + r4[q, 0, e].astype(jnp.float32)

    for q in range(4):
        g, j = q // 2, q % 2
        four[q][1].wait_recv()
        ys[q, 1] = final(q, 2).astype(jnp.bfloat16)
        if g == 0:
            ys[q, 0] = final(q, 1).astype(jnp.bfloat16)
        cross[q].start()
    for q in range(4):
        g, j = q // 2, q % 2
        spread(stage_y.at[1 + g, j], ys[q, 1].astype(jnp.float32))
        if g == 0:
            spread(stage_y.at[0, j], ys[q, 0].astype(jnp.float32))
    for q in range(4):
        g, j = q // 2, q % 2
        four[q][0].wait_recv()
        own = final(q, 0)
        acc[q, 0, 0] = own
        spread(stage.at[1 + g, j], own)
        if g:
            place(3, j, final(q, 1))

    def edge_copy(src, dst, n, row, col):
        return pltpu.make_async_remote_copy(
            src_ref=src,
            dst_ref=dst,
            send_sem=h_s.at[n],
            recv_sem=h_r.at[n],
            device_id=(row, col),
            device_id_type=MESH,
        )

    mine = pl.ds(0, TXD * COLS)
    edges = (
        edge_copy(v1.at[4, :, mine], v1.at[0, :, mine], 0, up, me),
        edge_copy(pack.at[0, 0], rim.at[0, 0], 1, gx, right),
        edge_copy(pack.at[0, 1], rim.at[0, 1], 2, gx, left),
        edge_copy(pack.at[1, 0], rim.at[1, 0], 3, up, right),
        edge_copy(pack.at[1, 1], rim.at[1, 1], 4, up, left),
    )
    edges[0].start()

    lane = lax.broadcasted_iota(jnp.int32, (8, COLS), 1)
    groups_of = DEEP1 // 8

    def packed(ref, side):
        total = jnp.zeros((8, COLS), jnp.float32)
        for i in range(groups_of):
            v = ref[pl.ds(8 * i, 8), :]
            if i:
                v = pltpu.roll(v, 4 * i, 1)
            pair = (COLS // 2 - 1 + 2 * i) % (COLS // 2) if side == 0 else 2 * i
            total = jnp.where((lane >> 1) == pair, v, total)
        return total

    for side in range(2):
        j = 1 - side
        for n, ref in enumerate((stage.at[1, j], stage.at[2, j], stage.at[3, j], stage_y.at[0, j])):
            pack[0, side, pl.ds(8 * n, 8), :] = packed(ref, side)
        for n, ref in enumerate((stage.at[3, j], stage_y.at[0, j], stage_y.at[1, j], stage_y.at[2, j])):
            pack[1, side, pl.ds(8 * n, 8), :] = packed(ref, side)
        edges[1 + side].start()
        edges[3 + side].start()

    for copy in covers:
        copy.wait_recv()
    for j in range(TXD):
        stage_y[0, j, pl.ds(CH * ROWS, ROWS), :] = cov_under[2, j].astype(jnp.float32)
        low = jnp.where(gx < NX - 1, stage_y[0, j], 0.0)
        v1[5, :, pl.ds(j * COLS, COLS)] = low.astype(jnp.bfloat16)
    for q in range(4):
        g, j = q // 2, q % 2
        cross[q].wait_recv()
        if g == 0:
            place(0, j, yr[q, 0].astype(jnp.float32))
        place(1 + g, j, acc[q, 0, 0] + yr[q, 1].astype(jnp.float32))
    for copy in edges:
        copy.wait_recv()

    last_tile = pl.ds(2 * COLS, COLS)
    cover_lane = lax.broadcasted_iota(jnp.int32, (ROWS, COLS), 1)
    has = (me > 0, me < NY - 1)
    for blk in range(-1, TYD + 1):
        total = None
        for side in range(2):
            part = None
            if blk >= 1:
                part = rim[0, side, pl.ds(8 * (blk - 1), 8), :]
            if blk <= 2:
                more = rim[1, side, pl.ds(8 * (blk + 1), 8), :]
                part = more if part is None else part + more
            part = jnp.where(has[side], part, 0.0)
            total = part if total is None else total + part
        if blk < 0:
            sides = cov_over[0, 1], cov_over[1, 0]
            inside = gx > 0
        elif blk == TYD:
            sides = cov_under[0, 1], cov_under[1, 0]
            inside = gx < NX - 1
        else:
            sides = cov_side[0, blk * TXD + 1], cov_side[1, blk * TXD]
            inside = None
        covered = jnp.where(
            cover_lane >= COLS // 2,
            jnp.where(has[0], sides[0].astype(jnp.float32), 0.0),
            jnp.where(has[1], sides[1].astype(jnp.float32), 0.0),
        )
        for i in range(groups_of):
            edge[blk + 1, pl.ds(8 * i, 8), :] = pltpu.roll(total, COLS - 4 * i, 1) if i else total
        edge[blk + 1, pl.ds(CH * ROWS, ROWS), :] = covered
        value = edge[blk + 1]
        if inside is not None:
            value = jnp.where(inside, value, 0.0)
        v1[blk + 1, :, last_tile] = value.astype(jnp.bfloat16)
    wide_zero = jnp.zeros((DEEP1, TXD * COLS), jnp.bfloat16)

    @pl.when(gx == 0)
    def _():
        v1[0, :, mine] = wide_zero

    def product(band, rows, field):
        total = None
        for dx in range(3):
            z = jnp.dot(band(dx, rows), field, preferred_element_type=jnp.float32)
            if dx != 1:
                z = pltpu.roll(z, (1 - dx) % WIDE, 1)
            total = z if total is None else total + z
        return total

    def band_one(dx, rows):
        return band1[dx, rows, :]

    def band_two(dx, rows):
        return band2[dx, rows, :]

    def column(ref):
        eye = lax.broadcasted_iota(jnp.int32, (OUT, OUT), 0) == lax.broadcasted_iota(jnp.int32, (OUT, OUT), 1)
        return jnp.sum(jnp.where(eye, ref[...], 0.0), axis=1, keepdims=True)

    every = pl.ds(0, 6 * OUT)
    head = product(band_one, pl.ds(4 * OUT, 2 * OUT), v1[0])
    h_acc[0] = head[:OUT]
    h_acc[1] = head[OUT:]
    for blk in range(TYD):
        s = product(band_one, every, v1[blk + 1])
        y = 4 * blk
        for n in range(6):
            piece = s[n * OUT : (n + 1) * OUT]
            h_acc[y + n] = piece + h_acc[y + n] if n < 2 else piece
    tail = product(band_one, pl.ds(0, 2 * OUT), v1[5])
    bias_one = column(b1)
    far = lax.broadcasted_iota(jnp.int32, (OUT, WIDE), 1)
    cut = jnp.logical_or(
        jnp.logical_and(far >= 2 * COLS + COLS // 2, me == 0),
        jnp.logical_and(
            jnp.logical_and(far >= 2 * COLS, far < 2 * COLS + COLS // 2), me == NY - 1
        ),
    )
    for n in range(18):
        raw_sum = h_acc[n]
        if n >= 16:
            raw_sum = raw_sum + tail[(n - 16) * OUT : (n - 15) * OUT]
        pre = raw_sum + bias_one
        h = pre * lax.logistic(pre)
        h = jnp.where(cut, 0.0, h)
        if n == 0:
            v2_top[...] = jnp.where(gx > 0, h, 0.0).astype(jnp.bfloat16)
        elif n == 17:
            v2_low[...] = jnp.where(gx < NX - 1, h, 0.0).astype(jnp.bfloat16)
        else:
            v2[(n - 1) // 4, pl.ds((n - 1) % 4 * OUT, OUT), :] = h.astype(jnp.bfloat16)

    o_acc[0] = product(lambda dx, rows: w2[dx], every, v2_top[...])[:, : TXD * COLS]
    for blk in range(TYD):
        s = product(band_two, every, v2[blk])[:, : TXD * COLS]
        y = 4 * blk - 1
        for n in range(6):
            piece = s[n * OUT : (n + 1) * OUT]
            if 0 <= y + n < 16:
                o_acc[y + n] = piece + o_acc[y + n] if n < 2 else piece
    tail = product(lambda dx, rows: w2[6 + dx], every, v2_low[...])[:, : TXD * COLS]
    bias_two = column(b2)
    for n in range(16):
        rows = pl.ds(n % 4, OUT, stride=ROWS)
        base = jnp.concatenate([stage[n // 4, j, rows, :] for j in range(TXD)], axis=1)
        value = o_acc[n] + bias_two + base.astype(jnp.bfloat16).astype(jnp.float32)
        if n == 15:
            value = value + tail
        shaded[n] = value.astype(jnp.bfloat16)

    def strip_copy(g):
        return pltpu.make_async_remote_copy(
            src_ref=strips.at[g],
            dst_ref=got.at[me],
            send_sem=d_s.at[g],
            recv_sem=d_r.at[me],
            device_id=(gx, g),
            device_id_type=MESH,
        )

    def strip_start(n, _):
        g = (me + n) % NY
        strips[g] = shaded[inv[g]]
        strip_copy(g).start()
        return 0

    lax.fori_loop(1, NY, strip_start, 0)
    got[me] = shaded[inv[me]]

    def strip_wait(n, _):
        col = (me + n) % NY
        pltpu.make_async_remote_copy(
            src_ref=strips.at[col],
            dst_ref=got.at[col],
            send_sem=d_s.at[col],
            recv_sem=d_r.at[col],
            device_id=(gx, col),
            device_id_type=MESH,
        ).wait_recv()
        return 0

    lax.fori_loop(1, NY, strip_wait, 0)
    for col in range(NY):
        shown[:, pl.ds(col * TXD * COLS, TXD * COLS)] = got[col]

    def strip_sent(n, _):
        strip_copy((me + n) % NY).wait_send()
        return 0

    lax.fori_loop(1, NY, strip_sent, 0)
    for copy in edges:
        copy.wait_send()
    for copy in covers:
        copy.wait_send()

    def alpha_sent(n, _):
        alpha_copy((me + n) % NY, 0).wait_send()
        alpha_copy((me + n) % NY, 1).wait_send()
        return 0

    lax.fori_loop(1, NY, alpha_sent, 0)
    alpha_copy(me, 1).wait_send()
    for copy in weights.values():
        copy.wait_send()
    for q in range(4):
        for copy in raw[q] + two[q] + three[q] + four[q] + [cross[q]]:
            copy.wait_send()


def spread_weights(w1, w2, band1, band2):
    for ref, band, ins, wide, step in ((w1, band1, CH + 1, DEEP1, 4), (w2, band2, OUT, DEEP2, 1)):
        chan = lax.broadcasted_iota(jnp.int32, (ins, wide), 0)
        spot = lax.broadcasted_iota(jnp.int32, (ins, wide), 1)
        pick = []
        for r in range(ROWS):
            where = chan * ROWS + r if step == 4 else chan + OUT * r
            pick.append(jnp.where(spot == where, 1.0, 0.0).astype(jnp.bfloat16))
        for dx in range(3):
            for n in range(6):
                total = None
                for dy in range(3):
                    r = n - 1 + dy - 1
                    if 0 <= r < ROWS:
                        term = jnp.dot(
                            ref[3 * dy + dx], pick[r], preferred_element_type=jnp.float32
                        )
                        total = term if total is None else total + term
                band[dx, pl.ds(n * OUT, OUT), :] = total.astype(jnp.bfloat16)


def frame(*operands):
    unit = (CH, ROWS, COLS)
    bf16, f32 = jnp.bfloat16, jnp.float32
    vmem = pltpu.VMEM
    dma = pltpu.SemaphoreType.DMA
    return pl.pallas_call(
        frame_kernel,
        name="frame",
        out_shape=jax.ShapeDtypeStruct((OUT, NY * TXD * COLS), bf16),
        in_specs=[pl.BlockSpec(memory_space=pl.ANY)] * len(operands),
        out_specs=pl.BlockSpec(memory_space=vmem),
        scratch_shapes=[
            vmem((8, 128), jnp.int32),
            vmem((128, 128), jnp.int32),
            vmem((TILES, DEPTH), jnp.int32),
            vmem((16, 128), jnp.int32),
            pltpu.SMEM((16, 128), jnp.int32),
            pltpu.SMEM((NY,), jnp.int32),
            pltpu.SMEM((NY,), jnp.int32),
            vmem((9, OUT, CH + 1), bf16),
            vmem((1, OUT), f32),
            vmem((9, OUT, OUT), bf16),
            vmem((1, OUT), f32),
            dma((10,)),
            vmem((128,) + unit, bf16),
            vmem((128, ROWS, COLS), bf16),
            vmem((128, ROWS, COLS), bf16),
            vmem((192, ROWS, COLS), bf16),
            vmem((TILES * TSTEP, ROWS, COLS), f32),
            vmem((192, ROWS, COLS), f32),
            vmem((192, ROWS, COLS), f32),
            vmem((4, 8, 2) + unit, bf16),
            vmem((4, 8, 2) + unit, bf16),
            vmem((4, 4, 3) + unit, bf16),
            vmem((4, 4, 3) + unit, f32),
            vmem((4, 4, 3) + unit, bf16),
            vmem((4, 2, 3) + unit, bf16),
            vmem((4, 2, 3) + unit, bf16),
            vmem((4, 1, 3) + unit, bf16),
            vmem((4, 1, 3) + unit, bf16),
            vmem((4, 2) + unit, bf16),
            vmem((4, 2) + unit, bf16),
            vmem((TILES, ROWS, COLS), bf16),
            vmem((2, TILES, ROWS, COLS), bf16),
            vmem((2, TXD, ROWS, COLS), bf16),
            vmem((3, TXD, ROWS, COLS), bf16),
            vmem((TYD, TXD, DEEP1, COLS), f32),
            vmem((3, TXD, DEEP1, COLS), f32),
            vmem((TYD + 2, DEEP1, WIDE), bf16),
            vmem((2, 2, 32, COLS), f32),
            vmem((2, 2, 32, COLS), f32),
            vmem((TYD + 2, DEEP1, COLS), f32),
            vmem((3, 6 * OUT, DEEP1), bf16),
            vmem((3, 6 * OUT, DEEP2), bf16),
            vmem((18, OUT, WIDE), f32),
            vmem((TYD, DEEP2, WIDE), bf16),
            vmem((OUT, WIDE), bf16),
            vmem((OUT, WIDE), bf16),
            vmem((16, OUT, TXD * COLS), f32),
            vmem((16, OUT, TXD * COLS), bf16),
            vmem((NY, OUT, TXD * COLS), bf16),
            vmem((NY, OUT, TXD * COLS), bf16),
            dma((4,)),
            dma((32,)),
            dma((32,)),
            dma((4, 8, 2)),
            dma((4, 8, 2)),
            dma((4, 11)),
            dma((4, 11)),
            dma((4,)),
            dma((4,)),
            dma((7,)),
            dma((7,)),
            dma((5,)),
            dma((5,)),
            dma((NY,)),
            dma((NY,)),
        ],
        compiler_params=pltpu.CompilerParams(
            collective_id=0, has_side_effects=True, vmem_limit_bytes=VMEM_BYTES
        ),
    )(*operands)


def shards(
    payload, opacity, depth_order, footprints, panel_map,
    conv1_weight, conv1_bias, conv2_weight, conv2_bias,
):
    shown = frame(
        payload.transpose(0, 2, 1, 3),
        opacity,
        jnp.asarray(patterns()),
        footprints,
        depth_order,
        panel_map,
        conv1_weight,
        conv1_bias[None],
        conv2_weight,
        conv2_bias[None],
    )
    return shown[None, None, None]


SPECS = (
    P(("gx", "gy"), None, None, None),
    P(("gx", "gy"), None, None),
    P(("gx", "gy"), None),
    P(),
    P(),
    P(),
    P(),
    P(),
    P(),
)


def solution(mesh):
    return jax.shard_map(
        shards,
        mesh=mesh,
        in_specs=SPECS,
        out_specs=P("gx", "gy", None, None, None),
        check_vma=False,
    )
```

```python
import functools

import jax
import jax.numpy as jnp
import numpy as np
from jax import lax
from jax.experimental import pallas as pl
from jax.experimental.pallas import tpu as pltpu
from jax.sharding import PartitionSpec as P

MESH = pl.DeviceIdType.MESH
TYD = 4
TXD = 2
TILES = 8
DEPTH = 16
CH = 35
ROWS = 4
COLS = 128
NX = 8
NY = 16
SIDE = 4
TSTEP = DEPTH + 2
MASKS = ((4, 12, 1, 3), (12, 4, 3, 1), (1, 3, 4, 12), (3, 1, 12, 4))


def kappa(q, k):
    m = MASKS[q]
    return (m[1] if k & 4 else 0) ^ (m[2] if k & 2 else 0) ^ (m[3] if k & 1 else 0)


def hops(offset):
    return sum(min(d, SIDE - d) for d in offset)


OTHERS = sorted(
    ((dx, dz) for dx in range(SIDE) for dz in range(SIDE) if dx or dz), key=hops, reverse=True
)


def shifted(c, offset):
    return (c // SIDE + offset[0]) % SIDE * SIDE + (c % SIDE + offset[1]) % SIDE


def flip4(p, d):
    if d == 0:
        return p
    if d == 1:
        return p + 1 - 2 * (p % 2)
    if d == 2:
        return (p + 2) % SIDE
    return 3 - p


def paired(c, mask):
    return flip4(c // SIDE, mask // SIDE) * SIDE + flip4(c % SIDE, mask % SIDE)


def patterns():
    base = np.zeros((2, 4, 8, 2), np.int32)
    rest = np.zeros((2, 4, 8, 2), np.int32)
    mask = np.zeros((4, 8, 3, 2), np.int32)
    which = np.zeros((4, 8, 3, 2), np.int32)
    for q in range(4):
        j, g = q % 2, q // 2
        for k in range(8):
            for s in range(2):
                flip = kappa(q, k) ^ (MASKS[q][0] if s else 0)
                for f in range(2):
                    jy = (1 + g) if f else (3 if g else 0)
                    base[s, q, k, f] = flip
                    rest[s, q, k, f] = jy * TXD + j
                for e in range(3):
                    jy = (1 + g) if e != 1 else (3 if g else 0)
                    mask[q, k, e, s] = flip
                    which[q, k, e, s] = jy * TXD + j + TILES * (0, 1 - g, 1)[e]
    rows = np.zeros((8, 128), np.int32)
    rows[0] = base.reshape(-1)
    rows[1] = rest.reshape(-1)
    rows[2:4].reshape(-1)[:192] = mask.reshape(-1)
    rows[4:6].reshape(-1)[:192] = which.reshape(-1)
    return rows


def fill_tables(rows, foot, order, out, gx, gy):
    i32 = jnp.int32
    own = foot[pl.ds(gx * NY + gy, 1), :]
    slot = ((own >> 3) & (NY - 1)) * TILES + (own & (TILES - 1))
    across = lax.broadcasted_iota(i32, (128, 128), 1)
    along = lax.broadcasted_iota(i32, (128, 128), 0)
    slots = jnp.sum(jnp.where(across == along, slot, 0), axis=1, keepdims=True)
    target = (rows[0:1] ^ gy) * TILES + rows[1:2]
    out[0:1] = jnp.max(jnp.where(slots == across, along, 0), axis=0, keepdims=True)
    out[1:2] = jnp.max(jnp.where(slots == target, along, 0), axis=0, keepdims=True)

    listed = order[...]
    tile = lax.broadcasted_iota(i32, (TILES, 128), 0)
    for n in range(2):
        which = rows[4 + n : 5 + n]
        local = which & (TILES - 1)
        brick = ((gx - (which >> 3)) & (NX - 1)) * NY + (rows[2 + n : 3 + n] ^ gy)
        rank = jnp.zeros((TILES, 128), i32)
        for d in range(DEPTH):
            hit = jnp.logical_and(listed[:, d : d + 1] == brick, tile == local)
            rank = jnp.minimum(rank, jnp.where(hit, d - (DEPTH + 1), 0))
        rank = jnp.min(rank, axis=0, keepdims=True)
        out[2 + n : 3 + n] = local * TSTEP + DEPTH + 1 + rank

    tile = lax.broadcasted_iota(i32, (TILES, DEPTH), 0)
    part = jnp.minimum((gx - (listed >> 4)) & (NX - 1), 1)
    spot = ((tile >> 1) - 1 + part) * TXD + (tile & 1)
    out[8:16, 0:DEPTH] = jnp.maximum((part * NY + (listed & (NY - 1))) * 6 + spot, 0)


OUT = 32
VMEM_BYTES = 62 << 20
WIDE = 3 * COLS
DEEP1 = (CH + 1) * ROWS
DEEP2 = OUT * ROWS


def frame_kernel(
    pay_h, opa_h, rows_h, foot_h, order_h, panel_h, w1_h, b1_h, w2_h, b2_h, shown,
    rows, foot, order, tabv, tab, panel, inv, w1, b1, w2, b2, tsem,
    pay, opa, asend, abuf, tb, tsend, trecv, s1, r1, s2, acc, r2, s3, r3, s4, r4, ys, yr,
    cov, cov_side, cov_over, cov_under, stage, stage_y, v1, pack, rim, edge, band1, band2, h_acc, v2, v2_top, v2_low, o_acc, shaded, strips, got,
    lsem, a_s, a_r, t_s, t_r, m_s, m_r, y_s, y_r, c_s, c_r, h_s, h_r, d_s, d_r,
):
    gx = lax.axis_index("gx")
    me = lax.axis_index("gy")
    up = (gx + 1) % NX
    down = (gx + NX - 1) % NX
    early = [
        pltpu.make_async_copy(src, dst, tsem.at[n])
        for n, (src, dst) in enumerate(
            ((rows_h, rows), (foot_h, foot), (order_h, order), (opa_h, opa), (panel_h, panel),
             (w1_h, w1), (b1_h, b1), (w2_h, w2), (b2_h, b2))
        )
    ]
    loads = []
    for i in range(8):
        part = pl.ds(16 * i, 16)
        loads.append(pltpu.make_async_copy(pay_h.at[part], pay.at[part], lsem.at[i]))
    for load in early[:4] + loads + early[4:]:
        load.start()

    barrier = pltpu.get_barrier_semaphore()

    def greet_row(i, _):
        pl.semaphore_signal(barrier, inc=1, device_id=(gx, (me + i) % NY), device_id_type=MESH)
        return 0

    def greet_next(i, _):
        pl.semaphore_signal(barrier, inc=1, device_id=(up, i), device_id_type=MESH)
        pl.semaphore_signal(barrier, inc=1, device_id=(down, i), device_id_type=MESH)
        return 0

    lax.fori_loop(1, NY, greet_row, 0)
    lax.fori_loop(0, NY, greet_next, 0)

    for load in early[:3]:
        load.wait()
    fill_tables(rows, foot, order, tabv, gx, me)
    to_smem = pltpu.make_async_copy(tabv, tab, tsem.at[9])
    early[3].wait()
    to_smem.start()
    to_smem.wait()

    def pack_alpha(i, _):
        asend[i] = opa[tab[0, i]]
        return 0

    lax.fori_loop(0, 128, pack_alpha, 0, unroll=8)
    for e in range(6):
        abuf[me * 6 + e] = asend[me * TILES + 2 + e]
    for load in loads:
        load.wait()

    def pack_raw(q, lo, hi):
        def body(k, _):
            for f in range(2):
                s1[q, k, f] = pay[tab[1, 64 + (q * 8 + k) * 2 + f]]
            return 0

        lax.fori_loop(lo, hi, body, 0)

    for q in range(4):
        pack_raw(q, 2, 8)
    pl.semaphore_wait(barrier, 47)

    def alpha_copy(i, back):
        return pltpu.make_async_remote_copy(
            src_ref=asend.at[pl.ds(i * TILES + 2 - 2 * back, 6)],
            dst_ref=abuf.at[pl.ds((back * NY + me) * 6, 6)],
            send_sem=a_s.at[back * NY + i],
            recv_sem=a_r.at[back * NY + me],
            device_id=(up if back else gx, i),
            device_id_type=MESH,
        )

    for offset in OTHERS:
        alpha_copy(shifted(me, offset), 1).start()
        alpha_copy(shifted(me, offset), 0).start()
    alpha_copy(me, 1).start()

    groups = ((4, 8), (2, 4), (1, 2), (0, 1))

    def raw_copy(q, n):
        lo, hi = groups[n]
        part = pl.ds(lo, hi - lo)
        return pltpu.make_async_remote_copy(
            src_ref=s1.at[q, part],
            dst_ref=r1.at[q, part],
            send_sem=m_s.at[q, n],
            recv_sem=m_r.at[q, n],
            device_id=(gx, paired(me, MASKS[q][0])),
            device_id_type=MESH,
        )

    raw = [[raw_copy(q, n) for n in range(4)] for q in range(4)]
    for n in range(2):
        for q in range(4):
            raw[q][n].start()
    for q in range(4):
        pack_raw(q, 0, 2)
    for load in early[4:]:
        load.wait()

    def invert(g, _):
        at = 0
        for strip in range(NY):
            at = jnp.where(panel[strip] == g, strip, at)
        inv[g] = at
        return 0

    lax.fori_loop(0, NY, invert, 0)

    spread_weights(w1, w2, band1, band2)

    def alpha_wait(n, _):
        col = (me + n) % NY
        for back in range(2):
            pltpu.make_async_remote_copy(
                src_ref=asend.at[pl.ds(0, 6)],
                dst_ref=abuf.at[pl.ds((back * NY + col) * 6, 6)],
                send_sem=a_s.at[back * NY + col],
                recv_sem=a_r.at[back * NY + col],
                device_id=(gx, col),
                device_id_type=MESH,
            ).wait_recv()
        return 0

    lax.fori_loop(1, NY, alpha_wait, 0)
    alpha_copy(me, 1).wait_recv()

    for t in range(TILES):
        tb[t * TSTEP + DEPTH + 1] = jnp.zeros((ROWS, COLS), jnp.float32)

    def through(d, passed):
        out = []
        for t in range(TILES):
            tb[t * TSTEP + d] = passed[t]
            alpha = abuf[tab[8 + t, d]].astype(jnp.float32)
            out.append(passed[t] * (1.0 - alpha))
        return tuple(out)

    last = lax.fori_loop(
        0, DEPTH, through, tuple(jnp.ones((ROWS, COLS), jnp.float32) for _ in range(TILES))
    )
    for t in range(TILES):
        cov[t] = (1.0 - last[t]).astype(jnp.bfloat16)

    def fill(i, _):
        tsend[i] = tb[tab[2, i]].astype(jnp.bfloat16)
        return 0

    def fill_rest(i, _):
        tsend[128 + i] = tb[tab[3, i]].astype(jnp.bfloat16)
        return 0

    lax.fori_loop(0, 128, fill, 0, unroll=8)
    lax.fori_loop(0, 64, fill_rest, 0, unroll=8)

    def weight_range(q, k, back):
        g = q // 2
        start, size = ((0, 4 if g else 2), (4 if g else 2, 2 if g else 4))[back]
        return pl.ds((q * 8 + k) * 6 + start, size)

    def weight_copy(q, k, back):
        part = weight_range(q, k, back)
        return pltpu.make_async_remote_copy(
            src_ref=tsend.at[part],
            dst_ref=trecv.at[part],
            send_sem=t_s.at[q, k, back],
            recv_sem=t_r.at[q, k, back],
            device_id=(down if back else gx, paired(me, kappa(q, k))),
            device_id_type=MESH,
        )

    weights = {}
    for k in (7, 6, 5, 4, 3, 2, 1, 0):
        for q in range(4):
            for back in range(2):
                if k == 0 and back == 0:
                    g = q // 2
                    for e in range(4 if g else 2):
                        trecv[q * 48 + e] = tsend[q * 48 + e]
                else:
                    weights[q, k, back] = weight_copy(q, k, back)
                    weights[q, k, back].start()
    right = (me + 1) % NY
    left = (me + NY - 1) % NY
    first_row = pl.ds(0, TXD)
    last_row = pl.ds((TYD - 1) * TXD, TXD)
    covers = [
        pltpu.make_async_remote_copy(
            src_ref=src,
            dst_ref=dst,
            send_sem=c_s.at[n],
            recv_sem=c_r.at[n],
            device_id=(row, col),
            device_id_type=MESH,
        )
        for n, (src, dst, row, col) in enumerate(
            (
                (cov, cov_side.at[0], gx, right),
                (cov, cov_side.at[1], gx, left),
                (cov.at[last_row], cov_over.at[0], up, right),
                (cov.at[last_row], cov_over.at[1], up, left),
                (cov.at[first_row], cov_under.at[0], down, right),
                (cov.at[first_row], cov_under.at[1], down, left),
                (cov.at[first_row], cov_under.at[2], down, me),
            )
        )
    ]
    for copy in covers:
        copy.start()
    for n in range(2, 4):
        for q in range(4):
            raw[q][n].start()

    def weighed(q, k):
        own = (q * 8 + k) * 2
        lead = (q * 8 + k) * 6
        w = [trecv[lead + n].astype(jnp.float32)[None] for n in range(6)]
        own_f = pay[tab[1, own]].astype(jnp.float32)
        got_f = r1[q, k, 0].astype(jnp.float32)
        mid = w[2] * own_f + w[3] * got_f
        own_a = pay[tab[1, own + 1]].astype(jnp.float32)
        got_a = r1[q, k, 1].astype(jnp.float32)
        first = w[0] * own_a + w[1] * got_a
        third = w[4] * own_a + w[5] * got_a
        return first, mid, third

    def merge_sent(q, lo, hi):
        def body(k, _):
            for e, v in enumerate(weighed(q, k)):
                s2[q, k - 4, e] = v.astype(jnp.bfloat16)
            return 0

        lax.fori_loop(lo, hi, body, 0)

    def merge_kept(q, lo, hi):
        def body(k, _):
            for e, v in enumerate(weighed(q, k)):
                acc[q, k, e] = v
            return 0

        lax.fori_loop(lo, hi, body, 0)

    def step_copy(src, dst, q, lo, hi, step, sem):
        part = pl.ds(lo, hi - lo)
        return pltpu.make_async_remote_copy(
            src_ref=src.at[q, part],
            dst_ref=dst.at[q, part],
            send_sem=m_s.at[q, sem],
            recv_sem=m_r.at[q, sem],
            device_id=(gx, paired(me, MASKS[q][step - 1])),
            device_id_type=MESH,
        )

    def wait_weights(q, lo, hi):
        for k in range(lo, hi):
            for back in range(2):
                if (q, k, back) in weights:
                    weights[q, k, back].wait_recv()

    two = [[step_copy(s2, r2, q, lo, hi, 2, 4 + n) for n, (lo, hi) in enumerate(groups[1:])] for q in range(4)]
    three = [[step_copy(s3, r3, q, lo, hi, 3, 7 + n) for n, (lo, hi) in enumerate(groups[2:])] for q in range(4)]

    def last_copy(q, crossing):
        size = 2 - q // 2 if crossing else 1 + q // 2
        part = pl.ds(1 + q // 2 if crossing else 0, size)
        return pltpu.make_async_remote_copy(
            src_ref=s4.at[q, 0, part],
            dst_ref=r4.at[q, 0, part],
            send_sem=m_s.at[q, 9 + crossing],
            recv_sem=m_r.at[q, 9 + crossing],
            device_id=(gx, paired(me, MASKS[q][3])),
            device_id_type=MESH,
        )

    four = [[last_copy(q, crossing) for crossing in range(2)] for q in range(4)]

    for q in range(4):
        wait_weights(q, 4, 8)
        raw[q][0].wait_recv()
        merge_sent(q, 6, 8)
        two[q][0].start()
    for q in range(4):
        merge_sent(q, 4, 6)
        two[q][1].start()
        two[q][2].start()
    for q in range(4):
        wait_weights(q, 0, 4)
        for n in range(1, 4):
            raw[q][n].wait_recv()
        merge_kept(q, 0, 4)

    def added(src, q, k):
        return [acc[q, k, e] + src[q, k, e].astype(jnp.float32) for e in range(3)]

    def forward(dst, src, q, k, to):
        for e, v in enumerate(added(src, q, k)):
            dst[q, to, e] = v.astype(jnp.bfloat16)

    def keep(src, q, k):
        for e, v in enumerate(added(src, q, k)):
            acc[q, k, e] = v

    for q in range(4):
        two[q][0].wait_recv()
        forward(s3, r2, q, 3, 1)
        three[q][0].start()
        forward(s3, r2, q, 2, 0)
        three[q][1].start()
    for q in range(4):
        two[q][1].wait_recv()
        keep(r2, q, 1)
        two[q][2].wait_recv()
        keep(r2, q, 0)
    for q in range(4):
        three[q][0].wait_recv()
        forward(s4, r3, q, 1, 0)
        four[q][1].start()
        four[q][0].start()
    for q in range(4):
        three[q][1].wait_recv()
        keep(r3, q, 0)

    def cross_copy(q):
        part = pl.ds(q // 2, 2 - q // 2)
        return pltpu.make_async_remote_copy(
            src_ref=ys.at[q, part],
            dst_ref=yr.at[q, part],
            send_sem=y_s.at[q],
            recv_sem=y_r.at[q],
            device_id=(up, me),
            device_id_type=MESH,
        )

    cross = [cross_copy(q) for q in range(4)]

    def spread(ref, v):
        for c in range(CH):
            ref[pl.ds(c * ROWS, ROWS), :] = v[c]

    def place(jy, j, v):
        spread(stage.at[jy, j], v)
        stage[jy, j, pl.ds(CH * ROWS, ROWS), :] = cov[jy * TXD + j].astype(jnp.float32)
        v1[jy + 1, :, pl.ds(j * COLS, COLS)] = stage[jy, j].astype(jnp.bfloat16)

    def final(q, e):
        return acc[q, 0, e] + r4[q, 0, e].astype(jnp.float32)

    for q in range(4):
        g, j = q // 2, q % 2
        four[q][1].wait_recv()
        ys[q, 1] = final(q, 2).astype(jnp.bfloat16)
        if g == 0:
            ys[q, 0] = final(q, 1).astype(jnp.bfloat16)
        cross[q].start()
    for q in range(4):
        g, j = q // 2, q % 2
        spread(stage_y.at[1 + g, j], ys[q, 1].astype(jnp.float32))
        if g == 0:
            spread(stage_y.at[0, j], ys[q, 0].astype(jnp.float32))
    for q in range(4):
        g, j = q // 2, q % 2
        four[q][0].wait_recv()
        own = final(q, 0)
        acc[q, 0, 0] = own
        spread(stage.at[1 + g, j], own)
        if g:
            place(3, j, final(q, 1))

    def edge_copy(src, dst, n, row, col):
        return pltpu.make_async_remote_copy(
            src_ref=src,
            dst_ref=dst,
            send_sem=h_s.at[n],
            recv_sem=h_r.at[n],
            device_id=(row, col),
            device_id_type=MESH,
        )

    mine = pl.ds(0, TXD * COLS)
    edges = (
        edge_copy(v1.at[4, :, mine], v1.at[0, :, mine], 0, up, me),
        edge_copy(pack.at[0, 0], rim.at[0, 0], 1, gx, right),
        edge_copy(pack.at[0, 1], rim.at[0, 1], 2, gx, left),
        edge_copy(pack.at[1, 0], rim.at[1, 0], 3, up, right),
        edge_copy(pack.at[1, 1], rim.at[1, 1], 4, up, left),
    )
    edges[0].start()

    lane = lax.broadcasted_iota(jnp.int32, (8, COLS), 1)
    groups_of = DEEP1 // 8

    def packed(ref, side):
        total = jnp.zeros((8, COLS), jnp.float32)
        for i in range(groups_of):
            v = ref[pl.ds(8 * i, 8), :]
            if i:
                v = pltpu.roll(v, 4 * i, 1)
            pair = (COLS // 2 - 1 + 2 * i) % (COLS // 2) if side == 0 else 2 * i
            total = jnp.where((lane >> 1) == pair, v, total)
        return total

    for side in range(2):
        j = 1 - side
        for n, ref in enumerate((stage.at[1, j], stage.at[2, j], stage.at[3, j], stage_y.at[0, j])):
            pack[0, side, pl.ds(8 * n, 8), :] = packed(ref, side)
        for n, ref in enumerate((stage.at[3, j], stage_y.at[0, j], stage_y.at[1, j], stage_y.at[2, j])):
            pack[1, side, pl.ds(8 * n, 8), :] = packed(ref, side)
        edges[1 + side].start()
        edges[3 + side].start()

    for copy in covers:
        copy.wait_recv()
    for j in range(TXD):
        stage_y[0, j, pl.ds(CH * ROWS, ROWS), :] = cov_under[2, j].astype(jnp.float32)
        low = jnp.where(gx < NX - 1, stage_y[0, j], 0.0)
        v1[5, :, pl.ds(j * COLS, COLS)] = low.astype(jnp.bfloat16)
    for q in range(4):
        g, j = q // 2, q % 2
        cross[q].wait_recv()
        if g == 0:
            place(0, j, yr[q, 0].astype(jnp.float32))
        place(1 + g, j, acc[q, 0, 0] + yr[q, 1].astype(jnp.float32))
    for copy in edges:
        copy.wait_recv()

    last_tile = pl.ds(2 * COLS, COLS)
    cover_lane = lax.broadcasted_iota(jnp.int32, (ROWS, COLS), 1)
    has = (me > 0, me < NY - 1)
    for blk in range(-1, TYD + 1):
        total = None
        for side in range(2):
            part = None
            if blk >= 1:
                part = rim[0, side, pl.ds(8 * (blk - 1), 8), :]
            if blk <= 2:
                more = rim[1, side, pl.ds(8 * (blk + 1), 8), :]
                part = more if part is None else part + more
            part = jnp.where(has[side], part, 0.0)
            total = part if total is None else total + part
        if blk < 0:
            sides = cov_over[0, 1], cov_over[1, 0]
            inside = gx > 0
        elif blk == TYD:
            sides = cov_under[0, 1], cov_under[1, 0]
            inside = gx < NX - 1
        else:
            sides = cov_side[0, blk * TXD + 1], cov_side[1, blk * TXD]
            inside = None
        covered = jnp.where(
            cover_lane >= COLS // 2,
            jnp.where(has[0], sides[0].astype(jnp.float32), 0.0),
            jnp.where(has[1], sides[1].astype(jnp.float32), 0.0),
        )
        for i in range(groups_of):
            edge[blk + 1, pl.ds(8 * i, 8), :] = pltpu.roll(total, COLS - 4 * i, 1) if i else total
        edge[blk + 1, pl.ds(CH * ROWS, ROWS), :] = covered
        value = edge[blk + 1]
        if inside is not None:
            value = jnp.where(inside, value, 0.0)
        v1[blk + 1, :, last_tile] = value.astype(jnp.bfloat16)
    wide_zero = jnp.zeros((DEEP1, TXD * COLS), jnp.bfloat16)

    @pl.when(gx == 0)
    def _():
        v1[0, :, mine] = wide_zero

    def product(band, rows, field):
        total = None
        for dx in range(3):
            z = jnp.dot(band(dx, rows), field, preferred_element_type=jnp.float32)
            if dx != 1:
                z = pltpu.roll(z, (1 - dx) % WIDE, 1)
            total = z if total is None else total + z
        return total

    def band_one(dx, rows):
        return band1[dx, rows, :]

    def band_two(dx, rows):
        return band2[dx, rows, :]

    def column(ref):
        eye = lax.broadcasted_iota(jnp.int32, (OUT, OUT), 0) == lax.broadcasted_iota(jnp.int32, (OUT, OUT), 1)
        return jnp.sum(jnp.where(eye, ref[...], 0.0), axis=1, keepdims=True)

    every = pl.ds(0, 6 * OUT)
    head = product(band_one, pl.ds(4 * OUT, 2 * OUT), v1[0])
    h_acc[0] = head[:OUT]
    h_acc[1] = head[OUT:]
    for blk in range(TYD):
        s = product(band_one, every, v1[blk + 1])
        y = 4 * blk
        for n in range(6):
            piece = s[n * OUT : (n + 1) * OUT]
            h_acc[y + n] = piece + h_acc[y + n] if n < 2 else piece
    tail = product(band_one, pl.ds(0, 2 * OUT), v1[5])
    bias_one = column(b1)
    far = lax.broadcasted_iota(jnp.int32, (OUT, WIDE), 1)
    cut = jnp.logical_or(
        jnp.logical_and(far >= 2 * COLS + COLS // 2, me == 0),
        jnp.logical_and(
            jnp.logical_and(far >= 2 * COLS, far < 2 * COLS + COLS // 2), me == NY - 1
        ),
    )
    for n in range(18):
        raw_sum = h_acc[n]
        if n >= 16:
            raw_sum = raw_sum + tail[(n - 16) * OUT : (n - 15) * OUT]
        pre = raw_sum + bias_one
        h = pre * lax.logistic(pre)
        h = jnp.where(cut, 0.0, h)
        if n == 0:
            v2_top[...] = jnp.where(gx > 0, h, 0.0).astype(jnp.bfloat16)
        elif n == 17:
            v2_low[...] = jnp.where(gx < NX - 1, h, 0.0).astype(jnp.bfloat16)
        else:
            v2[(n - 1) // 4, pl.ds((n - 1) % 4 * OUT, OUT), :] = h.astype(jnp.bfloat16)

    o_acc[0] = product(lambda dx, rows: w2[dx], every, v2_top[...])[:, : TXD * COLS]
    for blk in range(TYD):
        s = product(band_two, every, v2[blk])[:, : TXD * COLS]
        y = 4 * blk - 1
        for n in range(6):
            piece = s[n * OUT : (n + 1) * OUT]
            if 0 <= y + n < 16:
                o_acc[y + n] = piece + o_acc[y + n] if n < 2 else piece
    tail = product(lambda dx, rows: w2[6 + dx], every, v2_low[...])[:, : TXD * COLS]
    bias_two = column(b2)
    for n in range(16):
        rows = pl.ds(n % 4, OUT, stride=ROWS)
        base = jnp.concatenate([stage[n // 4, j, rows, :] for j in range(TXD)], axis=1)
        value = o_acc[n] + bias_two + base.astype(jnp.bfloat16).astype(jnp.float32)
        if n == 15:
            value = value + tail
        shaded[n] = value.astype(jnp.bfloat16)

    def strip_copy(g):
        return pltpu.make_async_remote_copy(
            src_ref=strips.at[g],
            dst_ref=got.at[me],
            send_sem=d_s.at[g],
            recv_sem=d_r.at[me],
            device_id=(gx, g),
            device_id_type=MESH,
        )

    for offset in OTHERS:
        g = shifted(me, offset)
        strips[g] = shaded[inv[g]]
        strip_copy(g).start()
    got[me] = shaded[inv[me]]

    def strip_wait(n, _):
        col = (me + n) % NY
        pltpu.make_async_remote_copy(
            src_ref=strips.at[col],
            dst_ref=got.at[col],
            send_sem=d_s.at[col],
            recv_sem=d_r.at[col],
            device_id=(gx, col),
            device_id_type=MESH,
        ).wait_recv()
        return 0

    lax.fori_loop(1, NY, strip_wait, 0)
    for col in range(NY):
        shown[:, pl.ds(col * TXD * COLS, TXD * COLS)] = got[col]

    def strip_sent(n, _):
        strip_copy((me + n) % NY).wait_send()
        return 0

    lax.fori_loop(1, NY, strip_sent, 0)
    for copy in edges:
        copy.wait_send()
    for copy in covers:
        copy.wait_send()

    def alpha_sent(n, _):
        alpha_copy((me + n) % NY, 0).wait_send()
        alpha_copy((me + n) % NY, 1).wait_send()
        return 0

    lax.fori_loop(1, NY, alpha_sent, 0)
    alpha_copy(me, 1).wait_send()
    for copy in weights.values():
        copy.wait_send()
    for q in range(4):
        for copy in raw[q] + two[q] + three[q] + four[q] + [cross[q]]:
            copy.wait_send()


def spread_weights(w1, w2, band1, band2):
    for ref, band, ins, wide, step in ((w1, band1, CH + 1, DEEP1, 4), (w2, band2, OUT, DEEP2, 1)):
        chan = lax.broadcasted_iota(jnp.int32, (ins, wide), 0)
        spot = lax.broadcasted_iota(jnp.int32, (ins, wide), 1)
        pick = []
        for r in range(ROWS):
            where = chan * ROWS + r if step == 4 else chan + OUT * r
            pick.append(jnp.where(spot == where, 1.0, 0.0).astype(jnp.bfloat16))
        for dx in range(3):
            for n in range(6):
                total = None
                for dy in range(3):
                    r = n - 1 + dy - 1
                    if 0 <= r < ROWS:
                        term = jnp.dot(
                            ref[3 * dy + dx], pick[r], preferred_element_type=jnp.float32
                        )
                        total = term if total is None else total + term
                band[dx, pl.ds(n * OUT, OUT), :] = total.astype(jnp.bfloat16)


def frame(*operands):
    unit = (CH, ROWS, COLS)
    bf16, f32 = jnp.bfloat16, jnp.float32
    vmem = pltpu.VMEM
    dma = pltpu.SemaphoreType.DMA
    return pl.pallas_call(
        frame_kernel,
        name="frame",
        out_shape=jax.ShapeDtypeStruct((OUT, NY * TXD * COLS), bf16),
        in_specs=[pl.BlockSpec(memory_space=pl.ANY)] * len(operands),
        out_specs=pl.BlockSpec(memory_space=vmem),
        scratch_shapes=[
            vmem((8, 128), jnp.int32),
            vmem((128, 128), jnp.int32),
            vmem((TILES, DEPTH), jnp.int32),
            vmem((16, 128), jnp.int32),
            pltpu.SMEM((16, 128), jnp.int32),
            pltpu.SMEM((NY,), jnp.int32),
            pltpu.SMEM((NY,), jnp.int32),
            vmem((9, OUT, CH + 1), bf16),
            vmem((1, OUT), f32),
            vmem((9, OUT, OUT), bf16),
            vmem((1, OUT), f32),
            dma((10,)),
            vmem((128,) + unit, bf16),
            vmem((128, ROWS, COLS), bf16),
            vmem((128, ROWS, COLS), bf16),
            vmem((192, ROWS, COLS), bf16),
            vmem((TILES * TSTEP, ROWS, COLS), f32),
            vmem((192, ROWS, COLS), bf16),
            vmem((192, ROWS, COLS), bf16),
            vmem((4, 8, 2) + unit, bf16),
            vmem((4, 8, 2) + unit, bf16),
            vmem((4, 4, 3) + unit, bf16),
            vmem((4, 4, 3) + unit, f32),
            vmem((4, 4, 3) + unit, bf16),
            vmem((4, 2, 3) + unit, bf16),
            vmem((4, 2, 3) + unit, bf16),
            vmem((4, 1, 3) + unit, bf16),
            vmem((4, 1, 3) + unit, bf16),
            vmem((4, 2) + unit, bf16),
            vmem((4, 2) + unit, bf16),
            vmem((TILES, ROWS, COLS), bf16),
            vmem((2, TILES, ROWS, COLS), bf16),
            vmem((2, TXD, ROWS, COLS), bf16),
            vmem((3, TXD, ROWS, COLS), bf16),
            vmem((TYD, TXD, DEEP1, COLS), f32),
            vmem((3, TXD, DEEP1, COLS), f32),
            vmem((TYD + 2, DEEP1, WIDE), bf16),
            vmem((2, 2, 32, COLS), f32),
            vmem((2, 2, 32, COLS), f32),
            vmem((TYD + 2, DEEP1, COLS), f32),
            vmem((3, 6 * OUT, DEEP1), bf16),
            vmem((3, 6 * OUT, DEEP2), bf16),
            vmem((18, OUT, WIDE), f32),
            vmem((TYD, DEEP2, WIDE), bf16),
            vmem((OUT, WIDE), bf16),
            vmem((OUT, WIDE), bf16),
            vmem((16, OUT, TXD * COLS), f32),
            vmem((16, OUT, TXD * COLS), bf16),
            vmem((NY, OUT, TXD * COLS), bf16),
            vmem((NY, OUT, TXD * COLS), bf16),
            dma((8,)),
            dma((32,)),
            dma((32,)),
            dma((4, 8, 2)),
            dma((4, 8, 2)),
            dma((4, 11)),
            dma((4, 11)),
            dma((4,)),
            dma((4,)),
            dma((7,)),
            dma((7,)),
            dma((5,)),
            dma((5,)),
            dma((NY,)),
            dma((NY,)),
        ],
        compiler_params=pltpu.CompilerParams(
            collective_id=0, has_side_effects=True, vmem_limit_bytes=VMEM_BYTES
        ),
    )(*operands)


def shards(
    payload, opacity, depth_order, footprints, panel_map,
    conv1_weight, conv1_bias, conv2_weight, conv2_bias,
):
    shown = frame(
        payload.transpose(0, 2, 1, 3),
        opacity,
        jnp.asarray(patterns()),
        footprints,
        depth_order,
        panel_map,
        conv1_weight,
        conv1_bias[None],
        conv2_weight,
        conv2_bias[None],
    )
    return shown[None, None, None]


SPECS = (
    P(("gx", "gy"), None, None, None),
    P(("gx", "gy"), None, None),
    P(("gx", "gy"), None),
    P(),
    P(),
    P(),
    P(),
    P(),
    P(),
)


def solution(mesh):
    return jax.shard_map(
        shards,
        mesh=mesh,
        in_specs=SPECS,
        out_specs=P("gx", "gy", None, None, None),
        check_vma=False,
    )
```

```python
import functools

import jax
import jax.numpy as jnp
import numpy as np
from jax import lax
from jax.experimental import pallas as pl
from jax.experimental.pallas import tpu as pltpu
from jax.sharding import PartitionSpec as P

MESH = pl.DeviceIdType.MESH
TYD = 4
TXD = 2
TILES = 8
DEPTH = 16
CH = 35
ROWS = 4
COLS = 128
NX = 8
NY = 16
SIDE = 4
TSTEP = DEPTH + 2
MASKS = ((4, 12, 1, 3), (12, 4, 3, 1), (1, 3, 4, 12), (3, 1, 12, 4))


def kappa(q, k):
    m = MASKS[q]
    return (m[1] if k & 4 else 0) ^ (m[2] if k & 2 else 0) ^ (m[3] if k & 1 else 0)


def hops(offset):
    return sum(min(d, SIDE - d) for d in offset)


OTHERS = sorted(
    ((dx, dz) for dx in range(SIDE) for dz in range(SIDE) if dx or dz), key=hops, reverse=True
)


def shifted(c, offset):
    return (c // SIDE + offset[0]) % SIDE * SIDE + (c % SIDE + offset[1]) % SIDE


def flip4(p, d):
    if d == 0:
        return p
    if d == 1:
        return p + 1 - 2 * (p % 2)
    if d == 2:
        return (p + 2) % SIDE
    return 3 - p


def paired(c, mask):
    return flip4(c // SIDE, mask // SIDE) * SIDE + flip4(c % SIDE, mask % SIDE)


def patterns():
    base = np.zeros((2, 4, 8, 2), np.int32)
    rest = np.zeros((2, 4, 8, 2), np.int32)
    mask = np.zeros((4, 8, 3, 2), np.int32)
    which = np.zeros((4, 8, 3, 2), np.int32)
    for q in range(4):
        j, g = q % 2, q // 2
        for k in range(8):
            for s in range(2):
                flip = kappa(q, k) ^ (MASKS[q][0] if s else 0)
                for f in range(2):
                    jy = (1 + g) if f else (3 if g else 0)
                    base[s, q, k, f] = flip
                    rest[s, q, k, f] = jy * TXD + j
                for e in range(3):
                    jy = (1 + g) if e != 1 else (3 if g else 0)
                    mask[q, k, e, s] = flip
                    which[q, k, e, s] = jy * TXD + j + TILES * (0, 1 - g, 1)[e]
    rows = np.zeros((8, 128), np.int32)
    rows[0] = base.reshape(-1)
    rows[1] = rest.reshape(-1)
    rows[2:4].reshape(-1)[:192] = mask.reshape(-1)
    rows[4:6].reshape(-1)[:192] = which.reshape(-1)
    return rows


def fill_tables(rows, foot, order, out, gx, gy):
    i32 = jnp.int32
    own = foot[pl.ds(gx * NY + gy, 1), :]
    slot = ((own >> 3) & (NY - 1)) * TILES + (own & (TILES - 1))
    across = lax.broadcasted_iota(i32, (128, 128), 1)
    along = lax.broadcasted_iota(i32, (128, 128), 0)
    slots = jnp.sum(jnp.where(across == along, slot, 0), axis=1, keepdims=True)
    target = (rows[0:1] ^ gy) * TILES + rows[1:2]
    out[0:1] = jnp.max(jnp.where(slots == across, along, 0), axis=0, keepdims=True)
    out[1:2] = jnp.max(jnp.where(slots == target, along, 0), axis=0, keepdims=True)

    listed = order[...]
    tile = lax.broadcasted_iota(i32, (TILES, 128), 0)
    for n in range(2):
        which = rows[4 + n : 5 + n]
        local = which & (TILES - 1)
        brick = ((gx - (which >> 3)) & (NX - 1)) * NY + (rows[2 + n : 3 + n] ^ gy)
        rank = jnp.zeros((TILES, 128), i32)
        for d in range(DEPTH):
            hit = jnp.logical_and(listed[:, d : d + 1] == brick, tile == local)
            rank = jnp.minimum(rank, jnp.where(hit, d - (DEPTH + 1), 0))
        rank = jnp.min(rank, axis=0, keepdims=True)
        out[2 + n : 3 + n] = local * TSTEP + DEPTH + 1 + rank

    tile = lax.broadcasted_iota(i32, (TILES, DEPTH), 0)
    part = jnp.minimum((gx - (listed >> 4)) & (NX - 1), 1)
    out[8:16, 0:DEPTH] = (part * NY + (listed & (NY - 1))) * TILES + tile


OUT = 32
VMEM_BYTES = 62 << 20
WIDE = 3 * COLS
DEEP1 = (CH + 1) * ROWS
DEEP2 = OUT * ROWS


def frame_kernel(
    pay_h, opa_h, rows_h, foot_h, order_h, panel_h, w1_h, b1_h, w2_h, b2_h, shown,
    rows, foot, order, tabv, tab, panel, inv, w1, b1, w2, b2, tsem,
    pay, opa, asend, abuf, tb, tsend, trecv, s1, r1, s2, acc, r2, s3, r3, s4, r4, ys, yr,
    cov, cov_side, cov_over, cov_under, stage, stage_y, v1, pack, rim, edge, band1, band2, h_acc, v2, v2_top, v2_low, o_acc, shaded, strips,
    lsem, a_s, a_r, t_s, t_r, m_s, m_r, y_s, y_r, c_s, c_r, h_s, h_r, d_s, d_r,
):
    gx = lax.axis_index("gx")
    me = lax.axis_index("gy")
    up = (gx + 1) % NX
    down = (gx + NX - 1) % NX
    early = [
        pltpu.make_async_copy(src, dst, tsem.at[n])
        for n, (src, dst) in enumerate(
            ((rows_h, rows), (foot_h, foot), (order_h, order), (opa_h, opa), (panel_h, panel),
             (w1_h, w1), (b1_h, b1), (w2_h, w2), (b2_h, b2))
        )
    ]
    loads = []
    for i in range(8):
        part = pl.ds(16 * i, 16)
        loads.append(pltpu.make_async_copy(pay_h.at[part], pay.at[part], lsem.at[i]))
    for load in early[:4] + loads + early[4:]:
        load.start()

    barrier = pltpu.get_barrier_semaphore()

    def greet_row(i, _):
        pl.semaphore_signal(barrier, inc=1, device_id=(gx, (me + i) % NY), device_id_type=MESH)
        return 0

    def greet_next(i, _):
        pl.semaphore_signal(barrier, inc=1, device_id=(up, i), device_id_type=MESH)
        pl.semaphore_signal(barrier, inc=1, device_id=(down, i), device_id_type=MESH)
        return 0

    lax.fori_loop(1, NY, greet_row, 0)
    lax.fori_loop(0, NY, greet_next, 0)

    for load in early[:3]:
        load.wait()
    fill_tables(rows, foot, order, tabv, gx, me)
    to_smem = pltpu.make_async_copy(tabv, tab, tsem.at[9])
    early[3].wait()
    to_smem.start()
    to_smem.wait()

    def pack_alpha(i, _):
        asend[i] = opa[tab[0, i]]
        return 0

    lax.fori_loop(0, 128, pack_alpha, 0, unroll=8)
    for e in range(TILES):
        abuf[me * TILES + e] = asend[me * TILES + e]
    for load in loads:
        load.wait()

    def pack_raw(q, lo, hi):
        def body(k, _):
            for f in range(2):
                s1[q, k, f] = pay[tab[1, 64 + (q * 8 + k) * 2 + f]]
            return 0

        lax.fori_loop(lo, hi, body, 0)

    for q in range(4):
        pack_raw(q, 2, 8)
    pl.semaphore_wait(barrier, 47)

    def alpha_copy(i):
        return pltpu.make_async_remote_copy(
            src_ref=asend.at[pl.ds(i * TILES, TILES)],
            dst_ref=abuf.at[pl.ds(me * TILES, TILES)],
            send_sem=a_s.at[i],
            recv_sem=a_r.at[me],
            device_id=(gx, i),
            device_id_type=MESH,
        )

    alpha_on = pltpu.make_async_remote_copy(
        src_ref=abuf.at[pl.ds(0, 128)],
        dst_ref=abuf.at[pl.ds(128, 128)],
        send_sem=a_s.at[NY],
        recv_sem=a_r.at[NY],
        device_id=(up, me),
        device_id_type=MESH,
    )

    for offset in OTHERS:
        alpha_copy(shifted(me, offset)).start()

    groups = ((4, 8), (2, 4), (1, 2), (0, 1))

    def raw_copy(q, n):
        lo, hi = groups[n]
        part = pl.ds(lo, hi - lo)
        return pltpu.make_async_remote_copy(
            src_ref=s1.at[q, part],
            dst_ref=r1.at[q, part],
            send_sem=m_s.at[q, n],
            recv_sem=m_r.at[q, n],
            device_id=(gx, paired(me, MASKS[q][0])),
            device_id_type=MESH,
        )

    raw = [[raw_copy(q, n) for n in range(4)] for q in range(4)]
    for n in range(2):
        for q in range(4):
            raw[q][n].start()
    for q in range(4):
        pack_raw(q, 0, 2)
    for load in early[4:]:
        load.wait()

    def invert(g, _):
        at = 0
        for strip in range(NY):
            at = jnp.where(panel[strip] == g, strip, at)
        inv[g] = at
        return 0

    lax.fori_loop(0, NY, invert, 0)

    spread_weights(w1, w2, band1, band2)

    def alpha_wait(n, _):
        col = (me + n) % NY
        pltpu.make_async_remote_copy(
            src_ref=asend.at[pl.ds(0, TILES)],
            dst_ref=abuf.at[pl.ds(col * TILES, TILES)],
            send_sem=a_s.at[col],
            recv_sem=a_r.at[col],
            device_id=(gx, col),
            device_id_type=MESH,
        ).wait_recv()
        return 0

    lax.fori_loop(1, NY, alpha_wait, 0)
    alpha_on.start()
    alpha_on.wait_recv()

    for t in range(TILES):
        tb[t * TSTEP + DEPTH + 1] = jnp.zeros((ROWS, COLS), jnp.float32)

    def through(d, passed):
        out = []
        for t in range(TILES):
            tb[t * TSTEP + d] = passed[t]
            alpha = abuf[tab[8 + t, d]].astype(jnp.float32)
            out.append(passed[t] * (1.0 - alpha))
        return tuple(out)

    last = lax.fori_loop(
        0, DEPTH, through, tuple(jnp.ones((ROWS, COLS), jnp.float32) for _ in range(TILES))
    )
    for t in range(TILES):
        cov[t] = (1.0 - last[t]).astype(jnp.bfloat16)

    def fill(i, _):
        tsend[i] = tb[tab[2, i]].astype(jnp.bfloat16)
        return 0

    def fill_rest(i, _):
        tsend[128 + i] = tb[tab[3, i]].astype(jnp.bfloat16)
        return 0

    lax.fori_loop(0, 128, fill, 0, unroll=8)
    lax.fori_loop(0, 64, fill_rest, 0, unroll=8)

    def weight_range(q, k, back):
        g = q // 2
        start, size = ((0, 4 if g else 2), (4 if g else 2, 2 if g else 4))[back]
        return pl.ds((q * 8 + k) * 6 + start, size)

    def weight_copy(q, k, back):
        part = weight_range(q, k, back)
        return pltpu.make_async_remote_copy(
            src_ref=tsend.at[part],
            dst_ref=trecv.at[part],
            send_sem=t_s.at[q, k, back],
            recv_sem=t_r.at[q, k, back],
            device_id=(down if back else gx, paired(me, kappa(q, k))),
            device_id_type=MESH,
        )

    weights = {}
    for k in (7, 6, 5, 4, 3, 2, 1, 0):
        for q in range(4):
            for back in range(2):
                if k == 0 and back == 0:
                    g = q // 2
                    for e in range(4 if g else 2):
                        trecv[q * 48 + e] = tsend[q * 48 + e]
                else:
                    weights[q, k, back] = weight_copy(q, k, back)
                    weights[q, k, back].start()
    right = (me + 1) % NY
    left = (me + NY - 1) % NY
    first_row = pl.ds(0, TXD)
    last_row = pl.ds((TYD - 1) * TXD, TXD)
    covers = [
        pltpu.make_async_remote_copy(
            src_ref=src,
            dst_ref=dst,
            send_sem=c_s.at[n],
            recv_sem=c_r.at[n],
            device_id=(row, col),
            device_id_type=MESH,
        )
        for n, (src, dst, row, col) in enumerate(
            (
                (cov, cov_side.at[0], gx, right),
                (cov, cov_side.at[1], gx, left),
                (cov.at[last_row], cov_over.at[0], up, right),
                (cov.at[last_row], cov_over.at[1], up, left),
                (cov.at[first_row], cov_under.at[0], down, right),
                (cov.at[first_row], cov_under.at[1], down, left),
                (cov.at[first_row], cov_under.at[2], down, me),
            )
        )
    ]
    for copy in covers:
        copy.start()
    for n in range(2, 4):
        for q in range(4):
            raw[q][n].start()

    def weighed(q, k):
        own = (q * 8 + k) * 2
        lead = (q * 8 + k) * 6
        w = [trecv[lead + n].astype(jnp.float32)[None] for n in range(6)]
        own_f = pay[tab[1, own]].astype(jnp.float32)
        got_f = r1[q, k, 0].astype(jnp.float32)
        mid = w[2] * own_f + w[3] * got_f
        own_a = pay[tab[1, own + 1]].astype(jnp.float32)
        got_a = r1[q, k, 1].astype(jnp.float32)
        first = w[0] * own_a + w[1] * got_a
        third = w[4] * own_a + w[5] * got_a
        return first, mid, third

    def merge_sent(q, lo, hi):
        def body(k, _):
            for e, v in enumerate(weighed(q, k)):
                s2[q, k - 4, e] = v.astype(jnp.bfloat16)
            return 0

        lax.fori_loop(lo, hi, body, 0)

    def merge_kept(q, lo, hi):
        def body(k, _):
            for e, v in enumerate(weighed(q, k)):
                acc[q, k, e] = v
            return 0

        lax.fori_loop(lo, hi, body, 0)

    def step_copy(src, dst, q, lo, hi, step, sem):
        part = pl.ds(lo, hi - lo)
        return pltpu.make_async_remote_copy(
            src_ref=src.at[q, part],
            dst_ref=dst.at[q, part],
            send_sem=m_s.at[q, sem],
            recv_sem=m_r.at[q, sem],
            device_id=(gx, paired(me, MASKS[q][step - 1])),
            device_id_type=MESH,
        )

    def wait_weights(q, lo, hi):
        for k in range(lo, hi):
            for back in range(2):
                if (q, k, back) in weights:
                    weights[q, k, back].wait_recv()

    two = [[step_copy(s2, r2, q, lo, hi, 2, 4 + n) for n, (lo, hi) in enumerate(groups[1:])] for q in range(4)]
    three = [[step_copy(s3, r3, q, lo, hi, 3, 7 + n) for n, (lo, hi) in enumerate(groups[2:])] for q in range(4)]

    def last_copy(q, crossing):
        size = 2 - q // 2 if crossing else 1 + q // 2
        part = pl.ds(1 + q // 2 if crossing else 0, size)
        return pltpu.make_async_remote_copy(
            src_ref=s4.at[q, 0, part],
            dst_ref=r4.at[q, 0, part],
            send_sem=m_s.at[q, 9 + crossing],
            recv_sem=m_r.at[q, 9 + crossing],
            device_id=(gx, paired(me, MASKS[q][3])),
            device_id_type=MESH,
        )

    four = [[last_copy(q, crossing) for crossing in range(2)] for q in range(4)]

    for q in range(4):
        wait_weights(q, 4, 8)
        raw[q][0].wait_recv()
        merge_sent(q, 6, 8)
        two[q][0].start()
    for q in range(4):
        merge_sent(q, 4, 6)
        two[q][1].start()
        two[q][2].start()
    for q in range(4):
        wait_weights(q, 0, 4)
        for n in range(1, 4):
            raw[q][n].wait_recv()
        merge_kept(q, 0, 4)

    def added(src, q, k):
        return [acc[q, k, e] + src[q, k, e].astype(jnp.float32) for e in range(3)]

    def forward(dst, src, q, k, to):
        for e, v in enumerate(added(src, q, k)):
            dst[q, to, e] = v.astype(jnp.bfloat16)

    def keep(src, q, k):
        for e, v in enumerate(added(src, q, k)):
            acc[q, k, e] = v

    for q in range(4):
        two[q][0].wait_recv()
        forward(s3, r2, q, 3, 1)
        three[q][0].start()
        forward(s3, r2, q, 2, 0)
        three[q][1].start()
    for q in range(4):
        two[q][1].wait_recv()
        keep(r2, q, 1)
        two[q][2].wait_recv()
        keep(r2, q, 0)
    for q in range(4):
        three[q][0].wait_recv()
        forward(s4, r3, q, 1, 0)
        four[q][1].start()
        four[q][0].start()
    for q in range(4):
        three[q][1].wait_recv()
        keep(r3, q, 0)

    def cross_copy(q):
        part = pl.ds(q // 2, 2 - q // 2)
        return pltpu.make_async_remote_copy(
            src_ref=ys.at[q, part],
            dst_ref=yr.at[q, part],
            send_sem=y_s.at[q],
            recv_sem=y_r.at[q],
            device_id=(up, me),
            device_id_type=MESH,
        )

    cross = [cross_copy(q) for q in range(4)]

    def spread(ref, v):
        for c in range(CH):
            ref[pl.ds(c * ROWS, ROWS), :] = v[c]

    def place(jy, j, v):
        spread(stage.at[jy, j], v)
        stage[jy, j, pl.ds(CH * ROWS, ROWS), :] = cov[jy * TXD + j].astype(jnp.float32)
        v1[jy + 1, :, pl.ds(j * COLS, COLS)] = stage[jy, j].astype(jnp.bfloat16)

    def final(q, e):
        return acc[q, 0, e] + r4[q, 0, e].astype(jnp.float32)

    for q in range(4):
        g, j = q // 2, q % 2
        four[q][1].wait_recv()
        ys[q, 1] = final(q, 2).astype(jnp.bfloat16)
        if g == 0:
            ys[q, 0] = final(q, 1).astype(jnp.bfloat16)
        cross[q].start()
    for q in range(4):
        g, j = q // 2, q % 2
        spread(stage_y.at[1 + g, j], ys[q, 1].astype(jnp.float32))
        if g == 0:
            spread(stage_y.at[0, j], ys[q, 0].astype(jnp.float32))
    for q in range(4):
        g, j = q // 2, q % 2
        four[q][0].wait_recv()
        own = final(q, 0)
        acc[q, 0, 0] = own
        spread(stage.at[1 + g, j], own)
        if g:
            place(3, j, final(q, 1))

    def edge_copy(src, dst, n, row, col):
        return pltpu.make_async_remote_copy(
            src_ref=src,
            dst_ref=dst,
            send_sem=h_s.at[n],
            recv_sem=h_r.at[n],
            device_id=(row, col),
            device_id_type=MESH,
        )

    mine = pl.ds(0, TXD * COLS)
    edges = (
        edge_copy(v1.at[4, :, mine], v1.at[0, :, mine], 0, up, me),
        edge_copy(pack.at[0, 0], rim.at[0, 0], 1, gx, right),
        edge_copy(pack.at[0, 1], rim.at[0, 1], 2, gx, left),
        edge_copy(pack.at[1, 0], rim.at[1, 0], 3, up, right),
        edge_copy(pack.at[1, 1], rim.at[1, 1], 4, up, left),
    )
    edges[0].start()

    lane = lax.broadcasted_iota(jnp.int32, (8, COLS), 1)
    groups_of = DEEP1 // 8

    def packed(ref, side):
        total = jnp.zeros((8, COLS), jnp.float32)
        for i in range(groups_of):
            v = ref[pl.ds(8 * i, 8), :]
            if i:
                v = pltpu.roll(v, 4 * i, 1)
            pair = (COLS // 2 - 1 + 2 * i) % (COLS // 2) if side == 0 else 2 * i
            total = jnp.where((lane >> 1) == pair, v, total)
        return total

    for side in range(2):
        j = 1 - side
        for n, ref in enumerate((stage.at[1, j], stage.at[2, j], stage.at[3, j], stage_y.at[0, j])):
            pack[0, side, pl.ds(8 * n, 8), :] = packed(ref, side)
        for n, ref in enumerate((stage.at[3, j], stage_y.at[0, j], stage_y.at[1, j], stage_y.at[2, j])):
            pack[1, side, pl.ds(8 * n, 8), :] = packed(ref, side)
        edges[1 + side].start()
        edges[3 + side].start()

    for copy in covers:
        copy.wait_recv()
    for j in range(TXD):
        stage_y[0, j, pl.ds(CH * ROWS, ROWS), :] = cov_under[2, j].astype(jnp.float32)
        low = jnp.where(gx < NX - 1, stage_y[0, j], 0.0)
        v1[5, :, pl.ds(j * COLS, COLS)] = low.astype(jnp.bfloat16)
    for q in range(4):
        g, j = q // 2, q % 2
        cross[q].wait_recv()
        if g == 0:
            place(0, j, yr[q, 0].astype(jnp.float32))
        place(1 + g, j, acc[q, 0, 0] + yr[q, 1].astype(jnp.float32))
    for copy in edges:
        copy.wait_recv()

    last_tile = pl.ds(2 * COLS, COLS)
    cover_lane = lax.broadcasted_iota(jnp.int32, (ROWS, COLS), 1)
    has = (me > 0, me < NY - 1)
    for blk in range(-1, TYD + 1):
        total = None
        for side in range(2):
            part = None
            if blk >= 1:
                part = rim[0, side, pl.ds(8 * (blk - 1), 8), :]
            if blk <= 2:
                more = rim[1, side, pl.ds(8 * (blk + 1), 8), :]
                part = more if part is None else part + more
            part = jnp.where(has[side], part, 0.0)
            total = part if total is None else total + part
        if blk < 0:
            sides = cov_over[0, 1], cov_over[1, 0]
            inside = gx > 0
        elif blk == TYD:
            sides = cov_under[0, 1], cov_under[1, 0]
            inside = gx < NX - 1
        else:
            sides = cov_side[0, blk * TXD + 1], cov_side[1, blk * TXD]
            inside = None
        covered = jnp.where(
            cover_lane >= COLS // 2,
            jnp.where(has[0], sides[0].astype(jnp.float32), 0.0),
            jnp.where(has[1], sides[1].astype(jnp.float32), 0.0),
        )
        for i in range(groups_of):
            edge[blk + 1, pl.ds(8 * i, 8), :] = pltpu.roll(total, COLS - 4 * i, 1) if i else total
        edge[blk + 1, pl.ds(CH * ROWS, ROWS), :] = covered
        value = edge[blk + 1]
        if inside is not None:
            value = jnp.where(inside, value, 0.0)
        v1[blk + 1, :, last_tile] = value.astype(jnp.bfloat16)
    wide_zero = jnp.zeros((DEEP1, TXD * COLS), jnp.bfloat16)

    @pl.when(gx == 0)
    def _():
        v1[0, :, mine] = wide_zero

    def product(band, rows, field):
        total = None
        for dx in range(3):
            z = jnp.dot(band(dx, rows), field, preferred_element_type=jnp.float32)
            if dx != 1:
                z = pltpu.roll(z, (1 - dx) % WIDE, 1)
            total = z if total is None else total + z
        return total

    def band_one(dx, rows):
        return band1[dx, rows, :]

    def band_two(dx, rows):
        return band2[dx, rows, :]

    def column(ref):
        eye = lax.broadcasted_iota(jnp.int32, (OUT, OUT), 0) == lax.broadcasted_iota(jnp.int32, (OUT, OUT), 1)
        return jnp.sum(jnp.where(eye, ref[...], 0.0), axis=1, keepdims=True)

    every = pl.ds(0, 6 * OUT)
    head = product(band_one, pl.ds(4 * OUT, 2 * OUT), v1[0])
    h_acc[0] = head[:OUT]
    h_acc[1] = head[OUT:]
    for blk in range(TYD):
        s = product(band_one, every, v1[blk + 1])
        y = 4 * blk
        for n in range(6):
            piece = s[n * OUT : (n + 1) * OUT]
            h_acc[y + n] = piece + h_acc[y + n] if n < 2 else piece
    tail = product(band_one, pl.ds(0, 2 * OUT), v1[5])
    bias_one = column(b1)
    far = lax.broadcasted_iota(jnp.int32, (OUT, WIDE), 1)
    cut = jnp.logical_or(
        jnp.logical_and(far >= 2 * COLS + COLS // 2, me == 0),
        jnp.logical_and(
            jnp.logical_and(far >= 2 * COLS, far < 2 * COLS + COLS // 2), me == NY - 1
        ),
    )
    for n in range(18):
        raw_sum = h_acc[n]
        if n >= 16:
            raw_sum = raw_sum + tail[(n - 16) * OUT : (n - 15) * OUT]
        pre = raw_sum + bias_one
        h = pre * lax.logistic(pre)
        h = jnp.where(cut, 0.0, h)
        if n == 0:
            v2_top[...] = jnp.where(gx > 0, h, 0.0).astype(jnp.bfloat16)
        elif n == 17:
            v2_low[...] = jnp.where(gx < NX - 1, h, 0.0).astype(jnp.bfloat16)
        else:
            v2[(n - 1) // 4, pl.ds((n - 1) % 4 * OUT, OUT), :] = h.astype(jnp.bfloat16)

    o_acc[0] = product(lambda dx, rows: w2[dx], every, v2_top[...])[:, : TXD * COLS]
    for blk in range(TYD):
        s = product(band_two, every, v2[blk])[:, : TXD * COLS]
        y = 4 * blk - 1
        for n in range(6):
            piece = s[n * OUT : (n + 1) * OUT]
            if 0 <= y + n < 16:
                o_acc[y + n] = piece + o_acc[y + n] if n < 2 else piece
    tail = product(lambda dx, rows: w2[6 + dx], every, v2_low[...])[:, : TXD * COLS]
    bias_two = column(b2)
    for n in range(16):
        rows = pl.ds(n % 4, OUT, stride=ROWS)
        base = jnp.concatenate([stage[n // 4, j, rows, :] for j in range(TXD)], axis=1)
        value = o_acc[n] + bias_two + base.astype(jnp.bfloat16).astype(jnp.float32)
        if n == 15:
            value = value + tail
        shaded[n] = value.astype(jnp.bfloat16)

    def window(col):
        start = pl.multiple_of(col * (TXD * COLS), TXD * COLS)
        return shown.at[:, pl.ds(start, TXD * COLS)]

    def strip_copy(g):
        return pltpu.make_async_remote_copy(
            src_ref=strips.at[g],
            dst_ref=window(me),
            send_sem=d_s.at[g],
            recv_sem=d_r.at[me],
            device_id=(gx, g),
            device_id_type=MESH,
        )

    for offset in OTHERS:
        g = shifted(me, offset)
        strips[g] = shaded[inv[g]]
        strip_copy(g).start()
    strips[me] = shaded[inv[me]]
    own_strip = pltpu.make_async_copy(strips.at[me], window(me), tsem.at[10])
    own_strip.start()

    def strip_wait(n, _):
        col = (me + n) % NY
        pltpu.make_async_remote_copy(
            src_ref=strips.at[col],
            dst_ref=window(col),
            send_sem=d_s.at[col],
            recv_sem=d_r.at[col],
            device_id=(gx, col),
            device_id_type=MESH,
        ).wait_recv()
        return 0

    def strip_sent(n, _):
        strip_copy((me + n) % NY).wait_send()
        return 0

    for copy in edges:
        copy.wait_send()
    for copy in covers:
        copy.wait_send()

    def alpha_sent(n, _):
        alpha_copy((me + n) % NY).wait_send()
        return 0

    lax.fori_loop(1, NY, alpha_sent, 0)
    alpha_on.wait_send()
    for copy in weights.values():
        copy.wait_send()
    for q in range(4):
        for copy in raw[q] + two[q] + three[q] + four[q] + [cross[q]]:
            copy.wait_send()
    lax.fori_loop(1, NY, strip_sent, 0)
    own_strip.wait()
    lax.fori_loop(1, NY, strip_wait, 0)


def spread_weights(w1, w2, band1, band2):
    for ref, band, ins, wide, step in ((w1, band1, CH + 1, DEEP1, 4), (w2, band2, OUT, DEEP2, 1)):
        chan = lax.broadcasted_iota(jnp.int32, (ins, wide), 0)
        spot = lax.broadcasted_iota(jnp.int32, (ins, wide), 1)
        pick = []
        for r in range(ROWS):
            where = chan * ROWS + r if step == 4 else chan + OUT * r
            pick.append(jnp.where(spot == where, 1.0, 0.0).astype(jnp.bfloat16))
        for dx in range(3):
            for n in range(6):
                total = None
                for dy in range(3):
                    r = n - 1 + dy - 1
                    if 0 <= r < ROWS:
                        term = jnp.dot(
                            ref[3 * dy + dx], pick[r], preferred_element_type=jnp.float32
                        )
                        total = term if total is None else total + term
                band[dx, pl.ds(n * OUT, OUT), :] = total.astype(jnp.bfloat16)


def frame(*operands):
    unit = (CH, ROWS, COLS)
    bf16, f32 = jnp.bfloat16, jnp.float32
    vmem = pltpu.VMEM
    dma = pltpu.SemaphoreType.DMA
    return pl.pallas_call(
        frame_kernel,
        name="frame",
        out_shape=jax.ShapeDtypeStruct((OUT, NY * TXD * COLS), bf16),
        in_specs=[pl.BlockSpec(memory_space=pl.ANY)] * len(operands),
        out_specs=pl.BlockSpec(memory_space=pl.ANY),
        scratch_shapes=[
            vmem((8, 128), jnp.int32),
            vmem((128, 128), jnp.int32),
            vmem((TILES, DEPTH), jnp.int32),
            vmem((16, 128), jnp.int32),
            pltpu.SMEM((16, 128), jnp.int32),
            pltpu.SMEM((NY,), jnp.int32),
            pltpu.SMEM((NY,), jnp.int32),
            vmem((9, OUT, CH + 1), bf16),
            vmem((1, OUT), f32),
            vmem((9, OUT, OUT), bf16),
            vmem((1, OUT), f32),
            dma((11,)),
            vmem((128,) + unit, bf16),
            vmem((128, ROWS, COLS), bf16),
            vmem((128, ROWS, COLS), bf16),
            vmem((256, ROWS, COLS), bf16),
            vmem((TILES * TSTEP, ROWS, COLS), f32),
            vmem((192, ROWS, COLS), bf16),
            vmem((192, ROWS, COLS), bf16),
            vmem((4, 8, 2) + unit, bf16),
            vmem((4, 8, 2) + unit, bf16),
            vmem((4, 4, 3) + unit, bf16),
            vmem((4, 4, 3) + unit, f32),
            vmem((4, 4, 3) + unit, bf16),
            vmem((4, 2, 3) + unit, bf16),
            vmem((4, 2, 3) + unit, bf16),
            vmem((4, 1, 3) + unit, bf16),
            vmem((4, 1, 3) + unit, bf16),
            vmem((4, 2) + unit, bf16),
            vmem((4, 2) + unit, bf16),
            vmem((TILES, ROWS, COLS), bf16),
            vmem((2, TILES, ROWS, COLS), bf16),
            vmem((2, TXD, ROWS, COLS), bf16),
            vmem((3, TXD, ROWS, COLS), bf16),
            vmem((TYD, TXD, DEEP1, COLS), f32),
            vmem((3, TXD, DEEP1, COLS), f32),
            vmem((TYD + 2, DEEP1, WIDE), bf16),
            vmem((2, 2, 32, COLS), f32),
            vmem((2, 2, 32, COLS), f32),
            vmem((TYD + 2, DEEP1, COLS), f32),
            vmem((3, 6 * OUT, DEEP1), bf16),
            vmem((3, 6 * OUT, DEEP2), bf16),
            vmem((18, OUT, WIDE), f32),
            vmem((TYD, DEEP2, WIDE), bf16),
            vmem((OUT, WIDE), bf16),
            vmem((OUT, WIDE), bf16),
            vmem((16, OUT, TXD * COLS), f32),
            vmem((16, OUT, TXD * COLS), bf16),
            vmem((NY, OUT, TXD * COLS), bf16),
            dma((8,)),
            dma((NY + 1,)),
            dma((NY + 1,)),
            dma((4, 8, 2)),
            dma((4, 8, 2)),
            dma((4, 11)),
            dma((4, 11)),
            dma((4,)),
            dma((4,)),
            dma((7,)),
            dma((7,)),
            dma((5,)),
            dma((5,)),
            dma((NY,)),
            dma((NY,)),
        ],
        compiler_params=pltpu.CompilerParams(
            collective_id=0, has_side_effects=True, vmem_limit_bytes=VMEM_BYTES
        ),
    )(*operands)


def shards(
    payload, opacity, depth_order, footprints, panel_map,
    conv1_weight, conv1_bias, conv2_weight, conv2_bias,
):
    shown = frame(
        payload.transpose(0, 2, 1, 3),
        opacity,
        jnp.asarray(patterns()),
        footprints,
        depth_order,
        panel_map,
        conv1_weight,
        conv1_bias[None],
        conv2_weight,
        conv2_bias[None],
    )
    return shown[None, None, None]


SPECS = (
    P(("gx", "gy"), None, None, None),
    P(("gx", "gy"), None, None),
    P(("gx", "gy"), None),
    P(),
    P(),
    P(),
    P(),
    P(),
    P(),
)


def solution(mesh):
    return jax.shard_map(
        shards,
        mesh=mesh,
        in_specs=SPECS,
        out_specs=P("gx", "gy", None, None, None),
        check_vma=False,
    )
```

```python
import functools

import jax
import jax.numpy as jnp
import numpy as np
from jax import lax
from jax.experimental import pallas as pl
from jax.experimental.pallas import tpu as pltpu
from jax.sharding import PartitionSpec as P

MESH = pl.DeviceIdType.MESH
TYD = 4
TXD = 2
TILES = 8
DEPTH = 16
CH = 35
ROWS = 4
COLS = 128
NX = 8
NY = 16
SIDE = 4
TSTEP = DEPTH + 2
MASKS = ((4, 12, 1, 3), (12, 4, 3, 1), (1, 3, 4, 12), (3, 1, 12, 4))


def kappa(q, k):
    m = MASKS[q]
    return (m[1] if k & 4 else 0) ^ (m[2] if k & 2 else 0) ^ (m[3] if k & 1 else 0)


def hops(offset):
    return sum(min(d, SIDE - d) for d in offset)


OTHERS = sorted(
    ((dx, dz) for dx in range(SIDE) for dz in range(SIDE) if dx or dz), key=hops, reverse=True
)


def shifted(c, offset):
    return (c // SIDE + offset[0]) % SIDE * SIDE + (c % SIDE + offset[1]) % SIDE


def flip4(p, d):
    if d == 0:
        return p
    if d == 1:
        return p + 1 - 2 * (p % 2)
    if d == 2:
        return (p + 2) % SIDE
    return 3 - p


def paired(c, mask):
    return flip4(c // SIDE, mask // SIDE) * SIDE + flip4(c % SIDE, mask % SIDE)


def patterns():
    base = np.zeros((2, 4, 8, 2), np.int32)
    rest = np.zeros((2, 4, 8, 2), np.int32)
    mask = np.zeros((4, 8, 3, 2), np.int32)
    which = np.zeros((4, 8, 3, 2), np.int32)
    for q in range(4):
        j, g = q % 2, q // 2
        for k in range(8):
            for s in range(2):
                flip = kappa(q, k) ^ (MASKS[q][0] if s else 0)
                for f in range(2):
                    jy = (1 + g) if f else (3 if g else 0)
                    base[s, q, k, f] = flip
                    rest[s, q, k, f] = jy * TXD + j
                for e in range(3):
                    jy = (1 + g) if e != 1 else (3 if g else 0)
                    mask[q, k, e, s] = flip
                    which[q, k, e, s] = jy * TXD + j + TILES * (0, 1 - g, 1)[e]
    rows = np.zeros((8, 128), np.int32)
    rows[0] = base.reshape(-1)
    rows[1] = rest.reshape(-1)
    rows[2:4].reshape(-1)[:192] = mask.reshape(-1)
    rows[4:6].reshape(-1)[:192] = which.reshape(-1)
    return rows


def fill_tables(rows, foot, order, out, gx, gy):
    i32 = jnp.int32
    own = foot[pl.ds(gx * NY + gy, 1), :]
    slot = ((own >> 3) & (NY - 1)) * TILES + (own & (TILES - 1))
    across = lax.broadcasted_iota(i32, (128, 128), 1)
    along = lax.broadcasted_iota(i32, (128, 128), 0)
    slots = jnp.sum(jnp.where(across == along, slot, 0), axis=1, keepdims=True)
    target = (rows[0:1] ^ gy) * TILES + rows[1:2]
    out[0:1] = jnp.max(jnp.where(slots == across, along, 0), axis=0, keepdims=True)
    out[1:2] = jnp.max(jnp.where(slots == target, along, 0), axis=0, keepdims=True)

    listed = order[...]
    tile = lax.broadcasted_iota(i32, (TILES, 128), 0)
    for n in range(2):
        which = rows[4 + n : 5 + n]
        local = which & (TILES - 1)
        brick = ((gx - (which >> 3)) & (NX - 1)) * NY + (rows[2 + n : 3 + n] ^ gy)
        rank = jnp.zeros((TILES, 128), i32)
        for d in range(DEPTH):
            hit = jnp.logical_and(listed[:, d : d + 1] == brick, tile == local)
            rank = jnp.minimum(rank, jnp.where(hit, d - (DEPTH + 1), 0))
        rank = jnp.min(rank, axis=0, keepdims=True)
        out[2 + n : 3 + n] = local * TSTEP + DEPTH + 1 + rank

    tile = lax.broadcasted_iota(i32, (TILES, DEPTH), 0)
    part = jnp.minimum((gx - (listed >> 4)) & (NX - 1), 1)
    out[8:16, 0:DEPTH] = (part * NY + (listed & (NY - 1))) * TILES + tile


OUT = 32
VMEM_BYTES = 62 << 20
WIDE = 3 * COLS
DEEP1 = (CH + 1) * ROWS
DEEP2 = OUT * ROWS


def frame_kernel(
    pay_h, opa_h, rows_h, foot_h, order_h, panel_h, w1_h, b1_h, w2_h, b2_h, shown,
    rows, foot, order, tabv, tab, panel, inv, w1, b1, w2, b2, tsem,
    pay, opa, asend, abuf, tb, tsend, trecv, s1, r1, s2, acc, r2, s3, r3, s4, r4, ys, yr,
    cov, cov_side, cov_over, cov_under, stage, stage_y, v1, pack, rim, edge, band1, band2, h_acc, v2, v2_top, v2_low, o_acc, shaded, strips,
    lsem, a_s, a_r, t_s, t_r, m_s, m_r, y_s, y_r, c_sem, h_s, h_r, d_sem,
):
    gx = lax.axis_index("gx")
    me = lax.axis_index("gy")
    up = (gx + 1) % NX
    down = (gx + NX - 1) % NX
    right = (me + 1) % NY
    left = (me + NY - 1) % NY
    early = [
        pltpu.make_async_copy(src, dst, tsem.at[n])
        for n, (src, dst) in enumerate(
            ((rows_h, rows), (foot_h, foot), (order_h, order), (opa_h, opa), (panel_h, panel),
             (w1_h, w1), (b1_h, b1), (w2_h, w2), (b2_h, b2))
        )
    ]
    loads = []
    for i in range(8):
        part = pl.ds(16 * i, 16)
        loads.append(pltpu.make_async_copy(pay_h.at[part], pay.at[part], lsem))
    for load in early[:4] + loads + early[4:]:
        load.start()

    barrier = pltpu.get_barrier_semaphore()

    def greet_row(i, _):
        pl.semaphore_signal(barrier, inc=1, device_id=(gx, (me + i) % NY), device_id_type=MESH)
        return 0

    def greet_next(i, _):
        pl.semaphore_signal(barrier, inc=1, device_id=(up, i), device_id_type=MESH)
        pl.semaphore_signal(barrier, inc=1, device_id=(down, i), device_id_type=MESH)
        return 0

    lax.fori_loop(1, NY, greet_row, 0)
    lax.fori_loop(0, NY, greet_next, 0)

    for load in early[:3]:
        load.wait()
    fill_tables(rows, foot, order, tabv, gx, me)
    to_smem = pltpu.make_async_copy(tabv, tab, tsem.at[9])
    early[3].wait()
    to_smem.start()
    to_smem.wait()

    def pack_alpha(i, _):
        asend[i] = opa[tab[0, i]]
        return 0

    lax.fori_loop(0, 128, pack_alpha, 0, unroll=8)
    for e in range(TILES):
        abuf[me * TILES + e] = asend[me * TILES + e]
    pltpu.make_async_copy(pay_h, pay, lsem).wait()

    def pack_raw(q, lo, hi):
        def body(k, _):
            for f in range(2):
                s1[q, k, f] = pay[tab[1, 64 + (q * 8 + k) * 2 + f]]
            return 0

        lax.fori_loop(lo, hi, body, 0)

    for q in range(4):
        pack_raw(q, 2, 8)
    pl.semaphore_wait(barrier, 47)

    def alpha_copy(i):
        return pltpu.make_async_remote_copy(
            src_ref=asend.at[pl.ds(i * TILES, TILES)],
            dst_ref=abuf.at[pl.ds(me * TILES, TILES)],
            send_sem=a_s.at[0],
            recv_sem=a_r.at[0],
            device_id=(gx, i),
            device_id_type=MESH,
        )

    alpha_on = pltpu.make_async_remote_copy(
        src_ref=abuf.at[pl.ds(0, 128)],
        dst_ref=abuf.at[pl.ds(128, 128)],
        send_sem=a_s.at[1],
        recv_sem=a_r.at[1],
        device_id=(up, me),
        device_id_type=MESH,
    )

    for offset in OTHERS:
        alpha_copy(shifted(me, offset)).start()

    groups = ((4, 8), (2, 4), (1, 2), (0, 1))

    def raw_copy(q, n):
        lo, hi = groups[n]
        part = pl.ds(lo, hi - lo)
        return pltpu.make_async_remote_copy(
            src_ref=s1.at[q, part],
            dst_ref=r1.at[q, part],
            send_sem=m_s.at[0],
            recv_sem=m_r.at[q, 0 if n == 0 else 1],
            device_id=(gx, paired(me, MASKS[q][0])),
            device_id_type=MESH,
        )

    raw = [[raw_copy(q, n) for n in range(4)] for q in range(4)]
    for n in range(2):
        for q in range(4):
            raw[q][n].start()
    for q in range(4):
        pack_raw(q, 0, 2)
    for load in early[4:]:
        load.wait()

    def invert(g, _):
        at = 0
        for strip in range(NY):
            at = jnp.where(panel[strip] == g, strip, at)
        inv[g] = at
        return 0

    lax.fori_loop(0, NY, invert, 0)

    spread_weights(w1, w2, band1, band2)

    others = pl.ds(0, (NY - 1) * TILES)
    alphas = pltpu.make_async_remote_copy(
        src_ref=asend.at[others],
        dst_ref=abuf.at[others],
        send_sem=a_s.at[0],
        recv_sem=a_r.at[0],
        device_id=(gx, right),
        device_id_type=MESH,
    )
    alphas.wait_recv()
    alpha_on.start()
    alpha_on.wait_recv()

    for t in range(TILES):
        tb[t * TSTEP + DEPTH + 1] = jnp.zeros((ROWS, COLS), jnp.float32)

    def through(d, passed):
        out = []
        for t in range(TILES):
            tb[t * TSTEP + d] = passed[t]
            alpha = abuf[tab[8 + t, d]].astype(jnp.float32)
            out.append(passed[t] * (1.0 - alpha))
        return tuple(out)

    last = lax.fori_loop(
        0, DEPTH, through, tuple(jnp.ones((ROWS, COLS), jnp.float32) for _ in range(TILES))
    )
    for t in range(TILES):
        cov[t] = (1.0 - last[t]).astype(jnp.bfloat16)

    def fill(i, _):
        tsend[i] = tb[tab[2, i]].astype(jnp.bfloat16)
        return 0

    def fill_rest(i, _):
        tsend[128 + i] = tb[tab[3, i]].astype(jnp.bfloat16)
        return 0

    lax.fori_loop(0, 128, fill, 0, unroll=8)
    lax.fori_loop(0, 64, fill_rest, 0, unroll=8)

    def weight_range(q, k, back):
        g = q // 2
        start, size = ((0, 4 if g else 2), (4 if g else 2, 2 if g else 4))[back]
        return pl.ds((q * 8 + k) * 6 + start, size)

    def weight_copy(q, k, back):
        part = weight_range(q, k, back)
        return pltpu.make_async_remote_copy(
            src_ref=tsend.at[part],
            dst_ref=trecv.at[part],
            send_sem=t_s,
            recv_sem=t_r.at[1 if k >= 4 else 0],
            device_id=(down if back else gx, paired(me, kappa(q, k))),
            device_id_type=MESH,
        )

    for k in (7, 6, 5, 4, 3, 2, 1, 0):
        for q in range(4):
            for back in range(2):
                if k == 0 and back == 0:
                    g = q // 2
                    for e in range(4 if g else 2):
                        trecv[q * 48 + e] = tsend[q * 48 + e]
                else:
                    weight_copy(q, k, back).start()

    def weight_group(size, sem):
        part = pl.ds(0, size)
        return pltpu.make_async_remote_copy(
            src_ref=tsend.at[part],
            dst_ref=trecv.at[part],
            send_sem=t_s,
            recv_sem=t_r.at[sem],
            device_id=(gx, right),
            device_id_type=MESH,
        )

    first_row = pl.ds(0, TXD)
    last_row = pl.ds((TYD - 1) * TXD, TXD)
    covers = [
        pltpu.make_async_remote_copy(
            src_ref=src,
            dst_ref=dst,
            send_sem=c_sem.at[0],
            recv_sem=c_sem.at[1],
            device_id=(row, col),
            device_id_type=MESH,
        )
        for src, dst, row, col in (
            (
                (cov, cov_side.at[0], gx, right),
                (cov, cov_side.at[1], gx, left),
                (cov.at[last_row], cov_over.at[0], up, right),
                (cov.at[last_row], cov_over.at[1], up, left),
                (cov.at[first_row], cov_under.at[0], down, right),
                (cov.at[first_row], cov_under.at[1], down, left),
                (cov.at[first_row], cov_under.at[2], down, me),
            )
        )
    ]
    for copy in covers:
        copy.start()
    covered_part = pl.ds(0, 2 * TILES + 5 * TXD)
    all_covers = pltpu.make_async_remote_copy(
        src_ref=asend.at[covered_part],
        dst_ref=abuf.at[covered_part],
        send_sem=c_sem.at[0],
        recv_sem=c_sem.at[1],
        device_id=(gx, right),
        device_id_type=MESH,
    )
    for n in range(2, 4):
        for q in range(4):
            raw[q][n].start()

    def weighed(q, k):
        own = (q * 8 + k) * 2
        lead = (q * 8 + k) * 6
        w = [trecv[lead + n].astype(jnp.float32)[None] for n in range(6)]
        own_f = pay[tab[1, own]].astype(jnp.float32)
        got_f = r1[q, k, 0].astype(jnp.float32)
        mid = w[2] * own_f + w[3] * got_f
        own_a = pay[tab[1, own + 1]].astype(jnp.float32)
        got_a = r1[q, k, 1].astype(jnp.float32)
        first = w[0] * own_a + w[1] * got_a
        third = w[4] * own_a + w[5] * got_a
        return first, mid, third

    def merge_sent(q, lo, hi):
        def body(k, _):
            for e, v in enumerate(weighed(q, k)):
                s2[q, k - 4, e] = v.astype(jnp.bfloat16)
            return 0

        lax.fori_loop(lo, hi, body, 0)

    def merge_kept(q, lo, hi):
        def body(k, _):
            for e, v in enumerate(weighed(q, k)):
                acc[q, k, e] = v
            return 0

        lax.fori_loop(lo, hi, body, 0)

    def step_copy(src, dst, q, lo, hi, step, sem):
        part = pl.ds(lo, hi - lo)
        return pltpu.make_async_remote_copy(
            src_ref=src.at[q, part],
            dst_ref=dst.at[q, part],
            send_sem=m_s.at[step - 1],
            recv_sem=m_r.at[q, sem],
            device_id=(gx, paired(me, MASKS[q][step - 1])),
            device_id_type=MESH,
        )

    def whole(src, dst, part, send, recv):
        return pltpu.make_async_remote_copy(
            src_ref=src.at[part],
            dst_ref=dst.at[part],
            send_sem=send,
            recv_sem=recv,
            device_id=(gx, right),
            device_id_type=MESH,
        )

    two = [[step_copy(s2, r2, q, lo, hi, 2, 2 + n) for n, (lo, hi) in enumerate(groups[1:])] for q in range(4)]
    three = [[step_copy(s3, r3, q, lo, hi, 3, 5 + n) for n, (lo, hi) in enumerate(groups[2:])] for q in range(4)]

    def last_copy(q, crossing):
        size = 2 - q // 2 if crossing else 1 + q // 2
        part = pl.ds(1 + q // 2 if crossing else 0, size)
        return pltpu.make_async_remote_copy(
            src_ref=s4.at[q, 0, part],
            dst_ref=r4.at[q, 0, part],
            send_sem=m_s.at[3],
            recv_sem=m_r.at[q, 7 + crossing],
            device_id=(gx, paired(me, MASKS[q][3])),
            device_id_type=MESH,
        )

    four = [[last_copy(q, crossing) for crossing in range(2)] for q in range(4)]

    weight_group(96, 1).wait_recv()
    for q in range(4):
        raw[q][0].wait_recv()
        merge_sent(q, 6, 8)
        two[q][0].start()
    for q in range(4):
        merge_sent(q, 4, 6)
        two[q][1].start()
        two[q][2].start()
    weight_group(84, 0).wait_recv()
    for q in range(4):
        half = (q, pl.ds(0, 4))
        whole(s1, r1, half, m_s.at[0], m_r.at[q, 1]).wait_recv()
        merge_kept(q, 0, 4)

    def added(src, q, k):
        return [acc[q, k, e] + src[q, k, e].astype(jnp.float32) for e in range(3)]

    def forward(dst, src, q, k, to):
        for e, v in enumerate(added(src, q, k)):
            dst[q, to, e] = v.astype(jnp.bfloat16)

    def keep(src, q, k):
        for e, v in enumerate(added(src, q, k)):
            acc[q, k, e] = v

    for q in range(4):
        two[q][0].wait_recv()
        forward(s3, r2, q, 3, 1)
        three[q][0].start()
        forward(s3, r2, q, 2, 0)
        three[q][1].start()
    for q in range(4):
        two[q][1].wait_recv()
        keep(r2, q, 1)
        two[q][2].wait_recv()
        keep(r2, q, 0)
    for q in range(4):
        three[q][0].wait_recv()
        forward(s4, r3, q, 1, 0)
        four[q][1].start()
        four[q][0].start()
    for q in range(4):
        three[q][1].wait_recv()
        keep(r3, q, 0)

    def cross_copy(q):
        part = pl.ds(q // 2, 2 - q // 2)
        return pltpu.make_async_remote_copy(
            src_ref=ys.at[q, part],
            dst_ref=yr.at[q, part],
            send_sem=y_s,
            recv_sem=y_r.at[q],
            device_id=(up, me),
            device_id_type=MESH,
        )

    cross = [cross_copy(q) for q in range(4)]

    def spread(ref, v):
        for c in range(CH):
            ref[pl.ds(c * ROWS, ROWS), :] = v[c]

    def place(jy, j, v):
        spread(stage.at[jy, j], v)
        stage[jy, j, pl.ds(CH * ROWS, ROWS), :] = cov[jy * TXD + j].astype(jnp.float32)
        v1[jy + 1, :, pl.ds(j * COLS, COLS)] = stage[jy, j].astype(jnp.bfloat16)

    def final(q, e):
        return acc[q, 0, e] + r4[q, 0, e].astype(jnp.float32)

    for q in range(4):
        g, j = q // 2, q % 2
        four[q][1].wait_recv()
        ys[q, 1] = final(q, 2).astype(jnp.bfloat16)
        if g == 0:
            ys[q, 0] = final(q, 1).astype(jnp.bfloat16)
        cross[q].start()
    for q in range(4):
        g, j = q // 2, q % 2
        spread(stage_y.at[1 + g, j], ys[q, 1].astype(jnp.float32))
        if g == 0:
            spread(stage_y.at[0, j], ys[q, 0].astype(jnp.float32))
    for q in range(4):
        g, j = q // 2, q % 2
        four[q][0].wait_recv()
        own = final(q, 0)
        acc[q, 0, 0] = own
        spread(stage.at[1 + g, j], own)
        if g:
            place(3, j, final(q, 1))

    def edge_copy(src, dst, n, row, col):
        n = min(n, 1)
        return pltpu.make_async_remote_copy(
            src_ref=src,
            dst_ref=dst,
            send_sem=h_s.at[n],
            recv_sem=h_r.at[n],
            device_id=(row, col),
            device_id_type=MESH,
        )

    mine = pl.ds(0, TXD * COLS)
    edges = (
        edge_copy(v1.at[4, :, mine], v1.at[0, :, mine], 0, up, me),
        edge_copy(pack.at[0, 0], rim.at[0, 0], 1, gx, right),
        edge_copy(pack.at[0, 1], rim.at[0, 1], 2, gx, left),
        edge_copy(pack.at[1, 0], rim.at[1, 0], 3, up, right),
        edge_copy(pack.at[1, 1], rim.at[1, 1], 4, up, left),
    )
    edges[0].start()

    lane = lax.broadcasted_iota(jnp.int32, (8, COLS), 1)
    groups_of = DEEP1 // 8

    def packed(ref, side):
        total = jnp.zeros((8, COLS), jnp.float32)
        for i in range(groups_of):
            v = ref[pl.ds(8 * i, 8), :]
            if i:
                v = pltpu.roll(v, 4 * i, 1)
            pair = (COLS // 2 - 1 + 2 * i) % (COLS // 2) if side == 0 else 2 * i
            total = jnp.where((lane >> 1) == pair, v, total)
        return total

    for side in range(2):
        j = 1 - side
        for n, ref in enumerate((stage.at[1, j], stage.at[2, j], stage.at[3, j], stage_y.at[0, j])):
            pack[0, side, pl.ds(8 * n, 8), :] = packed(ref, side)
        for n, ref in enumerate((stage.at[3, j], stage_y.at[0, j], stage_y.at[1, j], stage_y.at[2, j])):
            pack[1, side, pl.ds(8 * n, 8), :] = packed(ref, side)
        edges[1 + side].start()
        edges[3 + side].start()

    all_covers.wait_recv()
    for j in range(TXD):
        stage_y[0, j, pl.ds(CH * ROWS, ROWS), :] = cov_under[2, j].astype(jnp.float32)
        low = jnp.where(gx < NX - 1, stage_y[0, j], 0.0)
        v1[5, :, pl.ds(j * COLS, COLS)] = low.astype(jnp.bfloat16)
    for q in range(4):
        g, j = q // 2, q % 2
        cross[q].wait_recv()
        if g == 0:
            place(0, j, yr[q, 0].astype(jnp.float32))
        place(1 + g, j, acc[q, 0, 0] + yr[q, 1].astype(jnp.float32))
    rims = whole(pack, rim, pl.ds(0, 2), h_s.at[1], h_r.at[1])
    edges[0].wait_recv()
    rims.wait_recv()

    last_tile = pl.ds(2 * COLS, COLS)
    cover_lane = lax.broadcasted_iota(jnp.int32, (ROWS, COLS), 1)
    has = (me > 0, me < NY - 1)
    for blk in range(-1, TYD + 1):
        total = None
        for side in range(2):
            part = None
            if blk >= 1:
                part = rim[0, side, pl.ds(8 * (blk - 1), 8), :]
            if blk <= 2:
                more = rim[1, side, pl.ds(8 * (blk + 1), 8), :]
                part = more if part is None else part + more
            part = jnp.where(has[side], part, 0.0)
            total = part if total is None else total + part
        if blk < 0:
            sides = cov_over[0, 1], cov_over[1, 0]
            inside = gx > 0
        elif blk == TYD:
            sides = cov_under[0, 1], cov_under[1, 0]
            inside = gx < NX - 1
        else:
            sides = cov_side[0, blk * TXD + 1], cov_side[1, blk * TXD]
            inside = None
        covered = jnp.where(
            cover_lane >= COLS // 2,
            jnp.where(has[0], sides[0].astype(jnp.float32), 0.0),
            jnp.where(has[1], sides[1].astype(jnp.float32), 0.0),
        )
        for i in range(groups_of):
            edge[blk + 1, pl.ds(8 * i, 8), :] = pltpu.roll(total, COLS - 4 * i, 1) if i else total
        edge[blk + 1, pl.ds(CH * ROWS, ROWS), :] = covered
        value = edge[blk + 1]
        if inside is not None:
            value = jnp.where(inside, value, 0.0)
        v1[blk + 1, :, last_tile] = value.astype(jnp.bfloat16)
    wide_zero = jnp.zeros((DEEP1, TXD * COLS), jnp.bfloat16)

    @pl.when(gx == 0)
    def _():
        v1[0, :, mine] = wide_zero

    def product(band, rows, field):
        total = None
        for dx in range(3):
            z = jnp.dot(band(dx, rows), field, preferred_element_type=jnp.float32)
            if dx != 1:
                z = pltpu.roll(z, (1 - dx) % WIDE, 1)
            total = z if total is None else total + z
        return total

    def band_one(dx, rows):
        return band1[dx, rows, :]

    def band_two(dx, rows):
        return band2[dx, rows, :]

    def column(ref):
        eye = lax.broadcasted_iota(jnp.int32, (OUT, OUT), 0) == lax.broadcasted_iota(jnp.int32, (OUT, OUT), 1)
        return jnp.sum(jnp.where(eye, ref[...], 0.0), axis=1, keepdims=True)

    every = pl.ds(0, 6 * OUT)
    head = product(band_one, pl.ds(4 * OUT, 2 * OUT), v1[0])
    h_acc[0] = head[:OUT]
    h_acc[1] = head[OUT:]
    for blk in range(TYD):
        s = product(band_one, every, v1[blk + 1])
        y = 4 * blk
        for n in range(6):
            piece = s[n * OUT : (n + 1) * OUT]
            h_acc[y + n] = piece + h_acc[y + n] if n < 2 else piece
    tail = product(band_one, pl.ds(0, 2 * OUT), v1[5])
    bias_one = column(b1)
    far = lax.broadcasted_iota(jnp.int32, (OUT, WIDE), 1)
    cut = jnp.logical_or(
        jnp.logical_and(far >= 2 * COLS + COLS // 2, me == 0),
        jnp.logical_and(
            jnp.logical_and(far >= 2 * COLS, far < 2 * COLS + COLS // 2), me == NY - 1
        ),
    )
    for n in range(18):
        raw_sum = h_acc[n]
        if n >= 16:
            raw_sum = raw_sum + tail[(n - 16) * OUT : (n - 15) * OUT]
        pre = raw_sum + bias_one
        h = pre * lax.logistic(pre)
        h = jnp.where(cut, 0.0, h)
        if n == 0:
            v2_top[...] = jnp.where(gx > 0, h, 0.0).astype(jnp.bfloat16)
        elif n == 17:
            v2_low[...] = jnp.where(gx < NX - 1, h, 0.0).astype(jnp.bfloat16)
        else:
            v2[(n - 1) // 4, pl.ds((n - 1) % 4 * OUT, OUT), :] = h.astype(jnp.bfloat16)

    o_acc[0] = product(lambda dx, rows: w2[dx], every, v2_top[...])[:, : TXD * COLS]
    for blk in range(TYD):
        s = product(band_two, every, v2[blk])[:, : TXD * COLS]
        y = 4 * blk - 1
        for n in range(6):
            piece = s[n * OUT : (n + 1) * OUT]
            if 0 <= y + n < 16:
                o_acc[y + n] = piece + o_acc[y + n] if n < 2 else piece
    tail = product(lambda dx, rows: w2[6 + dx], every, v2_low[...])[:, : TXD * COLS]
    bias_two = column(b2)
    for n in range(16):
        rows = pl.ds(n % 4, OUT, stride=ROWS)
        base = jnp.concatenate([stage[n // 4, j, rows, :] for j in range(TXD)], axis=1)
        value = o_acc[n] + bias_two + base.astype(jnp.bfloat16).astype(jnp.float32)
        if n == 15:
            value = value + tail
        shaded[n] = value.astype(jnp.bfloat16)

    def window(col):
        start = pl.multiple_of(col * (TXD * COLS), TXD * COLS)
        return shown.at[:, pl.ds(start, TXD * COLS)]

    def strip_copy(g):
        return pltpu.make_async_remote_copy(
            src_ref=strips.at[g],
            dst_ref=window(me),
            send_sem=d_sem.at[0],
            recv_sem=d_sem.at[1],
            device_id=(gx, g),
            device_id_type=MESH,
        )

    for offset in OTHERS:
        g = shifted(me, offset)
        strips[g] = shaded[inv[g]]
        strip_copy(g).start()
    start = pl.multiple_of(me * (TXD * COLS), TXD * COLS)
    shown[:, pl.ds(start, TXD * COLS)] = shaded[inv[me]]

    edges[0].wait_send()
    rims.wait_send()
    all_covers.wait_send()

    alphas.wait_send()
    alpha_on.wait_send()
    weight_group(180, 0).wait_send()
    every_q = pl.ds(0, 4)
    for n, (src, dst) in enumerate(((s1, r1), (s2, r2), (s3, r3), (s4, r4))):
        whole(src, dst, every_q, m_s.at[n], m_r.at[0, 0]).wait_send()
    whole(ys, yr, pl.ds(0, 3), y_s, y_r.at[0]).wait_send()
    parts = pl.ds(0, NY - 1)
    all_strips = pltpu.make_async_remote_copy(
        src_ref=strips.at[parts],
        dst_ref=shaded.at[parts],
        send_sem=d_sem.at[0],
        recv_sem=d_sem.at[1],
        device_id=(gx, right),
        device_id_type=MESH,
    )
    all_strips.wait_send()
    all_strips.wait_recv()


def spread_weights(w1, w2, band1, band2):
    for ref, band, ins, wide, step in ((w1, band1, CH + 1, DEEP1, 4), (w2, band2, OUT, DEEP2, 1)):
        chan = lax.broadcasted_iota(jnp.int32, (ins, wide), 0)
        spot = lax.broadcasted_iota(jnp.int32, (ins, wide), 1)
        pick = []
        for r in range(ROWS):
            where = chan * ROWS + r if step == 4 else chan + OUT * r
            pick.append(jnp.where(spot == where, 1.0, 0.0).astype(jnp.bfloat16))
        for dx in range(3):
            for n in range(6):
                total = None
                for dy in range(3):
                    r = n - 1 + dy - 1
                    if 0 <= r < ROWS:
                        term = jnp.dot(
                            ref[3 * dy + dx], pick[r], preferred_element_type=jnp.float32
                        )
                        total = term if total is None else total + term
                band[dx, pl.ds(n * OUT, OUT), :] = total.astype(jnp.bfloat16)


def frame(*operands):
    unit = (CH, ROWS, COLS)
    bf16, f32 = jnp.bfloat16, jnp.float32
    vmem = pltpu.VMEM
    dma = pltpu.SemaphoreType.DMA
    return pl.pallas_call(
        frame_kernel,
        name="frame",
        out_shape=jax.ShapeDtypeStruct((OUT, NY * TXD * COLS), bf16),
        in_specs=[pl.BlockSpec(memory_space=pl.ANY)] * len(operands),
        out_specs=pl.BlockSpec(memory_space=vmem),
        scratch_shapes=[
            vmem((8, 128), jnp.int32),
            vmem((128, 128), jnp.int32),
            vmem((TILES, DEPTH), jnp.int32),
            vmem((16, 128), jnp.int32),
            pltpu.SMEM((16, 128), jnp.int32),
            pltpu.SMEM((NY,), jnp.int32),
            pltpu.SMEM((NY,), jnp.int32),
            vmem((9, OUT, CH + 1), bf16),
            vmem((1, OUT), f32),
            vmem((9, OUT, OUT), bf16),
            vmem((1, OUT), f32),
            dma((10,)),
            vmem((128,) + unit, bf16),
            vmem((128, ROWS, COLS), bf16),
            vmem((128, ROWS, COLS), bf16),
            vmem((256, ROWS, COLS), bf16),
            vmem((TILES * TSTEP, ROWS, COLS), f32),
            vmem((192, ROWS, COLS), bf16),
            vmem((192, ROWS, COLS), bf16),
            vmem((4, 8, 2) + unit, bf16),
            vmem((4, 8, 2) + unit, bf16),
            vmem((4, 4, 3) + unit, bf16),
            vmem((4, 4, 3) + unit, f32),
            vmem((4, 4, 3) + unit, bf16),
            vmem((4, 2, 3) + unit, bf16),
            vmem((4, 2, 3) + unit, bf16),
            vmem((4, 1, 3) + unit, bf16),
            vmem((4, 1, 3) + unit, bf16),
            vmem((4, 2) + unit, bf16),
            vmem((4, 2) + unit, bf16),
            vmem((TILES, ROWS, COLS), bf16),
            vmem((2, TILES, ROWS, COLS), bf16),
            vmem((2, TXD, ROWS, COLS), bf16),
            vmem((3, TXD, ROWS, COLS), bf16),
            vmem((TYD, TXD, DEEP1, COLS), f32),
            vmem((3, TXD, DEEP1, COLS), f32),
            vmem((TYD + 2, DEEP1, WIDE), bf16),
            vmem((2, 2, 32, COLS), f32),
            vmem((2, 2, 32, COLS), f32),
            vmem((TYD + 2, DEEP1, COLS), f32),
            vmem((3, 6 * OUT, DEEP1), bf16),
            vmem((3, 6 * OUT, DEEP2), bf16),
            vmem((18, OUT, WIDE), f32),
            vmem((TYD, DEEP2, WIDE), bf16),
            vmem((OUT, WIDE), bf16),
            vmem((OUT, WIDE), bf16),
            vmem((16, OUT, TXD * COLS), f32),
            vmem((16, OUT, TXD * COLS), bf16),
            vmem((NY, OUT, TXD * COLS), bf16),
            dma(()),
            dma((2,)),
            dma((2,)),
            dma(()),
            dma((2,)),
            dma((4,)),
            dma((4, 9)),
            dma(()),
            dma((4,)),
            dma((2,)),
            dma((2,)),
            dma((2,)),
            dma((2,)),
        ],
        compiler_params=pltpu.CompilerParams(
            collective_id=0, has_side_effects=True, vmem_limit_bytes=VMEM_BYTES
        ),
    )(*operands)


def shards(
    payload, opacity, depth_order, footprints, panel_map,
    conv1_weight, conv1_bias, conv2_weight, conv2_bias,
):
    shown = frame(
        payload.transpose(0, 2, 1, 3),
        opacity,
        jnp.asarray(patterns()),
        footprints,
        depth_order,
        panel_map,
        conv1_weight,
        conv1_bias[None],
        conv2_weight,
        conv2_bias[None],
    )
    return shown[None, None, None]


SPECS = (
    P(("gx", "gy"), None, None, None),
    P(("gx", "gy"), None, None),
    P(("gx", "gy"), None),
    P(),
    P(),
    P(),
    P(),
    P(),
    P(),
)


def solution(mesh):
    return jax.shard_map(
        shards,
        mesh=mesh,
        in_specs=SPECS,
        out_specs=P("gx", "gy", None, None, None),
        check_vma=False,
    )
```

```python
import functools

import jax
import jax.numpy as jnp
import numpy as np
from jax import lax
from jax.experimental import pallas as pl
from jax.experimental.pallas import tpu as pltpu
from jax.sharding import PartitionSpec as P

MESH = pl.DeviceIdType.MESH
TYD = 4
TXD = 2
TILES = 8
DEPTH = 16
CH = 35
ROWS = 4
COLS = 128
NX = 8
NY = 16
SIDE = 4
TSTEP = DEPTH + 2
MASKS = ((4, 12, 1, 3), (12, 4, 3, 1), (1, 3, 4, 12), (3, 1, 12, 4))


def kappa(q, k):
    m = MASKS[q]
    return (m[1] if k & 4 else 0) ^ (m[2] if k & 2 else 0) ^ (m[3] if k & 1 else 0)


def hops(offset):
    return sum(min(d, SIDE - d) for d in offset)


OTHERS = sorted(
    ((dx, dz) for dx in range(SIDE) for dz in range(SIDE) if dx or dz), key=hops, reverse=True
)


def shifted(c, offset):
    return (c // SIDE + offset[0]) % SIDE * SIDE + (c % SIDE + offset[1]) % SIDE


def flip4(p, d):
    if d == 0:
        return p
    if d == 1:
        return p + 1 - 2 * (p % 2)
    if d == 2:
        return (p + 2) % SIDE
    return 3 - p


def paired(c, mask):
    return flip4(c // SIDE, mask // SIDE) * SIDE + flip4(c % SIDE, mask % SIDE)


def patterns():
    base = np.zeros((2, 4, 8, 2), np.int32)
    rest = np.zeros((2, 4, 8, 2), np.int32)
    mask = np.zeros((4, 8, 3, 2), np.int32)
    which = np.zeros((4, 8, 3, 2), np.int32)
    for q in range(4):
        j, g = q % 2, q // 2
        for k in range(8):
            for s in range(2):
                flip = kappa(q, k) ^ (MASKS[q][0] if s else 0)
                for f in range(2):
                    jy = (1 + g) if f else (3 if g else 0)
                    base[s, q, k, f] = flip
                    rest[s, q, k, f] = jy * TXD + j
                for e in range(3):
                    jy = (1 + g) if e != 1 else (3 if g else 0)
                    mask[q, k, e, s] = flip
                    which[q, k, e, s] = jy * TXD + j + TILES * (0, 1 - g, 1)[e]
    rows = np.zeros((8, 128), np.int32)
    rows[0] = base.reshape(-1)
    rows[1] = rest.reshape(-1)
    rows[2:4].reshape(-1)[:192] = mask.reshape(-1)
    rows[4:6].reshape(-1)[:192] = which.reshape(-1)
    return rows


def fill_tables(rows, foot, order, out, gx, gy):
    i32 = jnp.int32
    own = foot[pl.ds(gx * NY + gy, 1), :]
    slot = ((own >> 3) & (NY - 1)) * TILES + (own & (TILES - 1))
    across = lax.broadcasted_iota(i32, (128, 128), 1)
    along = lax.broadcasted_iota(i32, (128, 128), 0)
    slots = jnp.sum(jnp.where(across == along, slot, 0), axis=1, keepdims=True)
    target = (rows[0:1] ^ gy) * TILES + rows[1:2]
    out[0:1] = jnp.max(jnp.where(slots == across, along, 0), axis=0, keepdims=True)
    out[1:2] = jnp.max(jnp.where(slots == target, along, 0), axis=0, keepdims=True)

    listed = order[...]
    tile = lax.broadcasted_iota(i32, (TILES, 128), 0)
    for n in range(2):
        which = rows[4 + n : 5 + n]
        local = which & (TILES - 1)
        brick = ((gx - (which >> 3)) & (NX - 1)) * NY + (rows[2 + n : 3 + n] ^ gy)
        rank = jnp.zeros((TILES, 128), i32)
        for d in range(DEPTH):
            hit = jnp.logical_and(listed[:, d : d + 1] == brick, tile == local)
            rank = jnp.minimum(rank, jnp.where(hit, d - (DEPTH + 1), 0))
        rank = jnp.min(rank, axis=0, keepdims=True)
        out[2 + n : 3 + n] = local * TSTEP + DEPTH + 1 + rank

    tile = lax.broadcasted_iota(i32, (TILES, DEPTH), 0)
    part = jnp.minimum((gx - (listed >> 4)) & (NX - 1), 1)
    out[8:16, 0:DEPTH] = (part * NY + (listed & (NY - 1))) * TILES + tile


OUT = 32
VMEM_BYTES = 62 << 20
WIDE = 3 * COLS
DEEP1 = (CH + 1) * ROWS
DEEP2 = OUT * ROWS


def frame_kernel(
    pay_h, opa_h, rows_h, foot_h, order_h, panel_h, w1_h, b1_h, w2_h, b2_h, shown,
    rows, foot, order, tabv, tab, panel, inv, w1, b1, w2, b2, tsem,
    pay, opa, asend, abuf, tb, tsend, trecv, s1, r1, s2, acc, r2, s3, r3, s4, r4, ys, yr,
    cov, cov_side, cov_over, cov_under, stage, stage_y, v1, pack, rim, edge, band1, band2, h_acc, v2, v2_top, v2_low, o_acc, shaded, strips,
    lsem, a_s, a_r, t_s, t_r, m_s, m_r, y_s, y_r, c_sem, h_s, h_r, d_sem,
):
    gx = lax.axis_index("gx")
    me = lax.axis_index("gy")
    up = (gx + 1) % NX
    down = (gx + NX - 1) % NX
    right = (me + 1) % NY
    left = (me + NY - 1) % NY
    early = [
        pltpu.make_async_copy(src, dst, tsem.at[n])
        for n, (src, dst) in enumerate(
            ((rows_h, rows), (foot_h, foot), (order_h, order), (opa_h, opa), (panel_h, panel),
             (w1_h, w1), (b1_h, b1), (w2_h, w2), (b2_h, b2))
        )
    ]
    loads = []
    for i in range(8):
        part = pl.ds(16 * i, 16)
        loads.append(pltpu.make_async_copy(pay_h.at[part], pay.at[part], lsem))
    for load in early[:4] + loads + early[4:]:
        load.start()

    barrier = pltpu.get_barrier_semaphore()

    def greet_row(i, _):
        pl.semaphore_signal(barrier, inc=1, device_id=(gx, (me + i) % NY), device_id_type=MESH)
        return 0

    def greet_next(i, _):
        pl.semaphore_signal(barrier, inc=1, device_id=(up, i), device_id_type=MESH)
        pl.semaphore_signal(barrier, inc=1, device_id=(down, i), device_id_type=MESH)
        return 0

    lax.fori_loop(1, NY, greet_row, 0)
    lax.fori_loop(0, NY, greet_next, 0)

    for load in early[:3]:
        load.wait()
    fill_tables(rows, foot, order, tabv, gx, me)
    to_smem = pltpu.make_async_copy(tabv, tab, tsem.at[9])
    early[3].wait()
    to_smem.start()
    to_smem.wait()

    def pack_alpha(i, _):
        asend[i] = opa[tab[0, i]]
        return 0

    lax.fori_loop(0, 128, pack_alpha, 0, unroll=8)
    for e in range(TILES):
        abuf[me * TILES + e] = asend[me * TILES + e]
    pltpu.make_async_copy(pay_h, pay, lsem).wait()

    def pack_raw(q, lo, hi):
        def body(k, _):
            for f in range(2):
                s1[q, k, f] = pay[tab[1, 64 + (q * 8 + k) * 2 + f]]
            return 0

        lax.fori_loop(lo, hi, body, 0)

    for q in range(4):
        pack_raw(q, 2, 8)
    pl.semaphore_wait(barrier, 47)

    def alpha_copy(i):
        return pltpu.make_async_remote_copy(
            src_ref=asend.at[pl.ds(i * TILES, TILES)],
            dst_ref=abuf.at[pl.ds(me * TILES, TILES)],
            send_sem=a_s.at[0],
            recv_sem=a_r.at[0],
            device_id=(gx, i),
            device_id_type=MESH,
        )

    alpha_on = pltpu.make_async_remote_copy(
        src_ref=abuf.at[pl.ds(0, 128)],
        dst_ref=abuf.at[pl.ds(128, 128)],
        send_sem=a_s.at[1],
        recv_sem=a_r.at[1],
        device_id=(up, me),
        device_id_type=MESH,
    )

    for offset in OTHERS:
        alpha_copy(shifted(me, offset)).start()

    groups = ((4, 8), (2, 4), (1, 2), (0, 1))

    def raw_copy(q, n):
        lo, hi = groups[n]
        part = pl.ds(lo, hi - lo)
        return pltpu.make_async_remote_copy(
            src_ref=s1.at[q, part],
            dst_ref=r1.at[q, part],
            send_sem=m_s.at[0],
            recv_sem=m_r.at[q, 0 if n == 0 else 1],
            device_id=(gx, paired(me, MASKS[q][0])),
            device_id_type=MESH,
        )

    raw = [[raw_copy(q, n) for n in range(4)] for q in range(4)]
    for n in range(2):
        for q in range(4):
            raw[q][n].start()
    for q in range(4):
        pack_raw(q, 0, 2)
    for load in early[4:]:
        load.wait()

    def invert(g, _):
        at = 0
        for strip in range(NY):
            at = jnp.where(panel[strip] == g, strip, at)
        inv[g] = at
        return 0

    lax.fori_loop(0, NY, invert, 0)

    spread_weights(w1, w2, band1, band2)

    others = pl.ds(0, (NY - 1) * TILES)
    alphas = pltpu.make_async_remote_copy(
        src_ref=asend.at[others],
        dst_ref=abuf.at[others],
        send_sem=a_s.at[0],
        recv_sem=a_r.at[0],
        device_id=(gx, right),
        device_id_type=MESH,
    )
    alphas.wait_recv()
    alpha_on.start()
    alpha_on.wait_recv()

    for t in range(TILES):
        tb[t * TSTEP + DEPTH + 1] = jnp.zeros((ROWS, COLS), jnp.float32)

    def through(d, passed):
        out = []
        for t in range(TILES):
            tb[t * TSTEP + d] = passed[t]
            alpha = abuf[tab[8 + t, d]].astype(jnp.float32)
            out.append(passed[t] * (1.0 - alpha))
        return tuple(out)

    last = lax.fori_loop(
        0, DEPTH, through, tuple(jnp.ones((ROWS, COLS), jnp.float32) for _ in range(TILES))
    )
    for t in range(TILES):
        cov[t] = (1.0 - last[t]).astype(jnp.bfloat16)

    def fill(i, _):
        tsend[i] = tb[tab[2, i]].astype(jnp.bfloat16)
        return 0

    def fill_rest(i, _):
        tsend[128 + i] = tb[tab[3, i]].astype(jnp.bfloat16)
        return 0

    lax.fori_loop(0, 128, fill, 0, unroll=8)
    lax.fori_loop(0, 64, fill_rest, 0, unroll=8)

    def weight_range(q, k, back):
        g = q // 2
        start, size = ((0, 4 if g else 2), (4 if g else 2, 2 if g else 4))[back]
        return pl.ds((q * 8 + k) * 6 + start, size)

    def weight_copy(q, k, back):
        part = weight_range(q, k, back)
        return pltpu.make_async_remote_copy(
            src_ref=tsend.at[part],
            dst_ref=trecv.at[part],
            send_sem=t_s,
            recv_sem=t_r.at[1 if k >= 4 else 0],
            device_id=(down if back else gx, paired(me, kappa(q, k))),
            device_id_type=MESH,
        )

    for k in (7, 6, 5, 4, 3, 2, 1, 0):
        for q in range(4):
            for back in range(2):
                if k == 0 and back == 0:
                    g = q // 2
                    for e in range(4 if g else 2):
                        trecv[q * 48 + e] = tsend[q * 48 + e]
                else:
                    weight_copy(q, k, back).start()

    def weight_group(size, sem):
        part = pl.ds(0, size)
        return pltpu.make_async_remote_copy(
            src_ref=tsend.at[part],
            dst_ref=trecv.at[part],
            send_sem=t_s,
            recv_sem=t_r.at[sem],
            device_id=(gx, right),
            device_id_type=MESH,
        )

    first_row = pl.ds(0, TXD)
    last_row = pl.ds((TYD - 1) * TXD, TXD)
    covers = [
        pltpu.make_async_remote_copy(
            src_ref=src,
            dst_ref=dst,
            send_sem=c_sem.at[0],
            recv_sem=c_sem.at[1],
            device_id=(row, col),
            device_id_type=MESH,
        )
        for src, dst, row, col in (
            (
                (cov, cov_side.at[0], gx, right),
                (cov, cov_side.at[1], gx, left),
                (cov.at[last_row], cov_over.at[0], up, right),
                (cov.at[last_row], cov_over.at[1], up, left),
                (cov.at[first_row], cov_under.at[0], down, right),
                (cov.at[first_row], cov_under.at[1], down, left),
                (cov.at[first_row], cov_under.at[2], down, me),
            )
        )
    ]
    for copy in covers:
        copy.start()
    covered_part = pl.ds(0, 2 * TILES + 5 * TXD)
    all_covers = pltpu.make_async_remote_copy(
        src_ref=asend.at[covered_part],
        dst_ref=abuf.at[covered_part],
        send_sem=c_sem.at[0],
        recv_sem=c_sem.at[1],
        device_id=(gx, right),
        device_id_type=MESH,
    )
    for n in range(2, 4):
        for q in range(4):
            raw[q][n].start()

    def weighed(q, k):
        own = (q * 8 + k) * 2
        lead = (q * 8 + k) * 6
        w = [trecv[lead + n].astype(jnp.float32)[None] for n in range(6)]
        own_f = pay[tab[1, own]].astype(jnp.float32)
        got_f = r1[q, k, 0].astype(jnp.float32)
        mid = w[2] * own_f + w[3] * got_f
        own_a = pay[tab[1, own + 1]].astype(jnp.float32)
        got_a = r1[q, k, 1].astype(jnp.float32)
        first = w[0] * own_a + w[1] * got_a
        third = w[4] * own_a + w[5] * got_a
        return first, mid, third

    def merge_sent(q, lo, hi):
        def body(k, _):
            for e, v in enumerate(weighed(q, k)):
                s2[q, k - 4, e] = v.astype(jnp.bfloat16)
            return 0

        lax.fori_loop(lo, hi, body, 0)

    def merge_kept(q, lo, hi):
        def body(k, _):
            for e, v in enumerate(weighed(q, k)):
                acc[q, k, e] = v
            return 0

        lax.fori_loop(lo, hi, body, 0)

    def step_copy(src, dst, q, lo, hi, step, sem):
        part = pl.ds(lo, hi - lo)
        return pltpu.make_async_remote_copy(
            src_ref=src.at[q, part],
            dst_ref=dst.at[q, part],
            send_sem=m_s.at[step - 1],
            recv_sem=m_r.at[q, sem],
            device_id=(gx, paired(me, MASKS[q][step - 1])),
            device_id_type=MESH,
        )

    def whole(src, dst, part, send, recv):
        return pltpu.make_async_remote_copy(
            src_ref=src.at[part],
            dst_ref=dst.at[part],
            send_sem=send,
            recv_sem=recv,
            device_id=(gx, right),
            device_id_type=MESH,
        )

    two = [[step_copy(s2, r2, q, lo, hi, 2, 2 + n) for n, (lo, hi) in enumerate(groups[1:])] for q in range(4)]
    three = [[step_copy(s3, r3, q, lo, hi, 3, 5 + n) for n, (lo, hi) in enumerate(groups[2:])] for q in range(4)]

    def last_copy(q, crossing):
        size = 2 - q // 2 if crossing else 1 + q // 2
        part = pl.ds(1 + q // 2 if crossing else 0, size)
        return pltpu.make_async_remote_copy(
            src_ref=s4.at[q, 0, part],
            dst_ref=r4.at[q, 0, part],
            send_sem=m_s.at[3],
            recv_sem=m_r.at[q, 7 + crossing],
            device_id=(gx, paired(me, MASKS[q][3])),
            device_id_type=MESH,
        )

    four = [[last_copy(q, crossing) for crossing in range(2)] for q in range(4)]

    weight_group(96, 1).wait_recv()
    for q in range(4):
        raw[q][0].wait_recv()
        merge_sent(q, 6, 8)
        two[q][0].start()
    for q in range(4):
        merge_sent(q, 4, 6)
        two[q][1].start()
        two[q][2].start()
    weight_group(84, 0).wait_recv()
    for q in range(4):
        half = (q, pl.ds(0, 4))
        whole(s1, r1, half, m_s.at[0], m_r.at[q, 1]).wait_recv()
        merge_kept(q, 0, 4)

    def added(src, q, k):
        return [acc[q, k, e] + src[q, k, e].astype(jnp.float32) for e in range(3)]

    def forward(dst, src, q, k, to):
        for e, v in enumerate(added(src, q, k)):
            dst[q, to, e] = v.astype(jnp.bfloat16)

    def keep(src, q, k):
        for e, v in enumerate(added(src, q, k)):
            acc[q, k, e] = v

    for q in range(4):
        two[q][0].wait_recv()
        forward(s3, r2, q, 3, 1)
        three[q][0].start()
        forward(s3, r2, q, 2, 0)
        three[q][1].start()
    for q in range(4):
        two[q][1].wait_recv()
        keep(r2, q, 1)
        two[q][2].wait_recv()
        keep(r2, q, 0)
    for q in range(4):
        three[q][0].wait_recv()
        forward(s4, r3, q, 1, 0)
        four[q][1].start()
        four[q][0].start()
    for q in range(4):
        three[q][1].wait_recv()
        keep(r3, q, 0)

    def cross_copy(q):
        part = pl.ds(q // 2, 2 - q // 2)
        return pltpu.make_async_remote_copy(
            src_ref=ys.at[q, part],
            dst_ref=yr.at[q, part],
            send_sem=y_s,
            recv_sem=y_r.at[q],
            device_id=(up, me),
            device_id_type=MESH,
        )

    cross = [cross_copy(q) for q in range(4)]

    def spread(ref, v):
        for c in range(CH):
            ref[pl.ds(c * ROWS, ROWS), :] = v[c]

    def place(jy, j, v):
        spread(stage.at[jy, j], v)
        stage[jy, j, pl.ds(CH * ROWS, ROWS), :] = cov[jy * TXD + j].astype(jnp.float32)
        v1[jy + 1, :, pl.ds(j * COLS, COLS)] = stage[jy, j].astype(jnp.bfloat16)

    def final(q, e):
        return acc[q, 0, e] + r4[q, 0, e].astype(jnp.float32)

    for q in range(4):
        g, j = q // 2, q % 2
        four[q][1].wait_recv()
        ys[q, 1] = final(q, 2).astype(jnp.bfloat16)
        if g == 0:
            ys[q, 0] = final(q, 1).astype(jnp.bfloat16)
        cross[q].start()
    for q in range(4):
        g, j = q // 2, q % 2
        spread(stage_y.at[1 + g, j], ys[q, 1].astype(jnp.float32))
        if g == 0:
            spread(stage_y.at[0, j], ys[q, 0].astype(jnp.float32))
    for q in range(4):
        g, j = q // 2, q % 2
        four[q][0].wait_recv()
        own = final(q, 0)
        acc[q, 0, 0] = own
        spread(stage.at[1 + g, j], own)
        if g:
            place(3, j, final(q, 1))

    def edge_copy(src, dst, n, row, col):
        n = min(n, 1)
        return pltpu.make_async_remote_copy(
            src_ref=src,
            dst_ref=dst,
            send_sem=h_s.at[n],
            recv_sem=h_r.at[n],
            device_id=(row, col),
            device_id_type=MESH,
        )

    mine = pl.ds(0, TXD * COLS)
    edges = (
        edge_copy(v1.at[4, :, mine], v1.at[0, :, mine], 0, up, me),
        edge_copy(pack.at[0, 0], rim.at[0, 0], 1, gx, right),
        edge_copy(pack.at[0, 1], rim.at[0, 1], 2, gx, left),
        edge_copy(pack.at[1, 0], rim.at[1, 0], 3, up, right),
        edge_copy(pack.at[1, 1], rim.at[1, 1], 4, up, left),
    )
    edges[0].start()

    lane = lax.broadcasted_iota(jnp.int32, (8, COLS), 1)
    groups_of = DEEP1 // 8

    def packed(ref, side):
        total = jnp.zeros((8, COLS), jnp.float32)
        for i in range(groups_of):
            v = ref[pl.ds(8 * i, 8), :]
            if i:
                v = pltpu.roll(v, 4 * i, 1)
            pair = (COLS // 2 - 1 + 2 * i) % (COLS // 2) if side == 0 else 2 * i
            total = jnp.where((lane >> 1) == pair, v, total)
        return total

    for side in range(2):
        j = 1 - side
        for n, ref in enumerate((stage.at[1, j], stage.at[2, j], stage.at[3, j], stage_y.at[0, j])):
            pack[0, side, pl.ds(8 * n, 8), :] = packed(ref, side)
        for n, ref in enumerate((stage.at[3, j], stage_y.at[0, j], stage_y.at[1, j], stage_y.at[2, j])):
            pack[1, side, pl.ds(8 * n, 8), :] = packed(ref, side)
        edges[1 + side].start()
        edges[3 + side].start()

    all_covers.wait_recv()
    for j in range(TXD):
        stage_y[0, j, pl.ds(CH * ROWS, ROWS), :] = cov_under[2, j].astype(jnp.float32)
        low = jnp.where(gx < NX - 1, stage_y[0, j], 0.0)
        v1[5, :, pl.ds(j * COLS, COLS)] = low.astype(jnp.bfloat16)
    for q in range(4):
        g, j = q // 2, q % 2
        cross[q].wait_recv()
        if g == 0:
            place(0, j, yr[q, 0].astype(jnp.float32))
        place(1 + g, j, acc[q, 0, 0] + yr[q, 1].astype(jnp.float32))
    rims = whole(pack, rim, pl.ds(0, 2), h_s.at[1], h_r.at[1])
    edges[0].wait_recv()
    rims.wait_recv()

    last_tile = pl.ds(2 * COLS, COLS)
    cover_lane = lax.broadcasted_iota(jnp.int32, (ROWS, COLS), 1)
    has = (me > 0, me < NY - 1)
    for blk in range(-1, TYD + 1):
        total = None
        for side in range(2):
            part = None
            if blk >= 1:
                part = rim[0, side, pl.ds(8 * (blk - 1), 8), :]
            if blk <= 2:
                more = rim[1, side, pl.ds(8 * (blk + 1), 8), :]
                part = more if part is None else part + more
            part = jnp.where(has[side], part, 0.0)
            total = part if total is None else total + part
        if blk < 0:
            sides = cov_over[0, 1], cov_over[1, 0]
            inside = gx > 0
        elif blk == TYD:
            sides = cov_under[0, 1], cov_under[1, 0]
            inside = gx < NX - 1
        else:
            sides = cov_side[0, blk * TXD + 1], cov_side[1, blk * TXD]
            inside = None
        covered = jnp.where(
            cover_lane >= COLS // 2,
            jnp.where(has[0], sides[0].astype(jnp.float32), 0.0),
            jnp.where(has[1], sides[1].astype(jnp.float32), 0.0),
        )
        for i in range(groups_of):
            edge[blk + 1, pl.ds(8 * i, 8), :] = pltpu.roll(total, COLS - 4 * i, 1) if i else total
        edge[blk + 1, pl.ds(CH * ROWS, ROWS), :] = covered
        value = edge[blk + 1]
        if inside is not None:
            value = jnp.where(inside, value, 0.0)
        v1[blk + 1, :, last_tile] = value.astype(jnp.bfloat16)
    wide_zero = jnp.zeros((DEEP1, TXD * COLS), jnp.bfloat16)

    @pl.when(gx == 0)
    def _():
        v1[0, :, mine] = wide_zero

    def product(band, rows, field):
        total = None
        for dx in range(3):
            z = jnp.dot(band(dx, rows), field, preferred_element_type=jnp.float32)
            if dx != 1:
                z = pltpu.roll(z, (1 - dx) % WIDE, 1)
            total = z if total is None else total + z
        return total

    def band_one(dx, rows):
        return band1[dx, rows, :]

    def band_two(dx, rows):
        return band2[dx, rows, :]

    def column(ref):
        eye = lax.broadcasted_iota(jnp.int32, (OUT, OUT), 0) == lax.broadcasted_iota(jnp.int32, (OUT, OUT), 1)
        return jnp.sum(jnp.where(eye, ref[...], 0.0), axis=1, keepdims=True)

    every = pl.ds(0, 6 * OUT)
    head = product(band_one, pl.ds(4 * OUT, 2 * OUT), v1[0])
    h_acc[0] = head[:OUT]
    h_acc[1] = head[OUT:]
    for blk in range(TYD):
        s = product(band_one, every, v1[blk + 1])
        y = 4 * blk
        for n in range(6):
            piece = s[n * OUT : (n + 1) * OUT]
            h_acc[y + n] = piece + h_acc[y + n] if n < 2 else piece
    tail = product(band_one, pl.ds(0, 2 * OUT), v1[5])
    bias_one = column(b1)
    far = lax.broadcasted_iota(jnp.int32, (OUT, WIDE), 1)
    cut = jnp.logical_or(
        jnp.logical_and(far >= 2 * COLS + COLS // 2, me == 0),
        jnp.logical_and(
            jnp.logical_and(far >= 2 * COLS, far < 2 * COLS + COLS // 2), me == NY - 1
        ),
    )
    for n in range(18):
        raw_sum = h_acc[n]
        if n >= 16:
            raw_sum = raw_sum + tail[(n - 16) * OUT : (n - 15) * OUT]
        pre = raw_sum + bias_one
        h = pre * lax.logistic(pre)
        h = jnp.where(cut, 0.0, h)
        if n == 0:
            v2_top[...] = jnp.where(gx > 0, h, 0.0).astype(jnp.bfloat16)
        elif n == 17:
            v2_low[...] = jnp.where(gx < NX - 1, h, 0.0).astype(jnp.bfloat16)
        else:
            v2[(n - 1) // 4, pl.ds((n - 1) % 4 * OUT, OUT), :] = h.astype(jnp.bfloat16)

    o_acc[0] = product(lambda dx, rows: w2[dx], every, v2_top[...])[:, : TXD * COLS]
    for blk in range(TYD):
        s = product(band_two, every, v2[blk])[:, : TXD * COLS]
        y = 4 * blk - 1
        for n in range(6):
            piece = s[n * OUT : (n + 1) * OUT]
            if 0 <= y + n < 16:
                o_acc[y + n] = piece + o_acc[y + n] if n < 2 else piece
    tail = product(lambda dx, rows: w2[6 + dx], every, v2_low[...])[:, : TXD * COLS]
    bias_two = column(b2)
    for n in range(16):
        rows = pl.ds(n % 4, OUT, stride=ROWS)
        base = jnp.concatenate([stage[n // 4, j, rows, :] for j in range(TXD)], axis=1)
        value = o_acc[n] + bias_two + base.astype(jnp.bfloat16).astype(jnp.float32)
        if n == 15:
            value = value + tail
        shaded[n] = value.astype(jnp.bfloat16)

    def window(col):
        start = pl.multiple_of(col * (TXD * COLS), TXD * COLS)
        return shown.at[:, pl.ds(start, TXD * COLS)]

    def strip_copy(g):
        return pltpu.make_async_remote_copy(
            src_ref=strips.at[g],
            dst_ref=window(me),
            send_sem=d_sem.at[0],
            recv_sem=d_sem.at[1],
            device_id=(gx, g),
            device_id_type=MESH,
        )

    for offset in OTHERS:
        g = shifted(me, offset)
        strips[g] = shaded[inv[g]]
        strip_copy(g).start()
    start = pl.multiple_of(me * (TXD * COLS), TXD * COLS)
    shown[:, pl.ds(start, TXD * COLS)] = shaded[inv[me]]

    edges[0].wait_send()
    rims.wait_send()
    all_covers.wait_send()

    alphas.wait_send()
    alpha_on.wait_send()
    weight_group(180, 0).wait_send()
    every_q = pl.ds(0, 4)
    for n, (src, dst) in enumerate(((s1, r1), (s2, r2), (s3, r3), (s4, r4))):
        whole(src, dst, every_q, m_s.at[n], m_r.at[0, 0]).wait_send()
    whole(ys, yr, pl.ds(0, 3), y_s, y_r.at[0]).wait_send()
    parts = pl.ds(0, NY - 1)
    all_strips = pltpu.make_async_remote_copy(
        src_ref=strips.at[parts],
        dst_ref=shaded.at[parts],
        send_sem=d_sem.at[0],
        recv_sem=d_sem.at[1],
        device_id=(gx, right),
        device_id_type=MESH,
    )
    all_strips.wait_send()
    all_strips.wait_recv()


def spread_weights(w1, w2, band1, band2):
    for ref, band, ins, wide, step in ((w1, band1, CH + 1, DEEP1, 4), (w2, band2, OUT, DEEP2, 1)):
        chan = lax.broadcasted_iota(jnp.int32, (ins, wide), 0)
        spot = lax.broadcasted_iota(jnp.int32, (ins, wide), 1)
        pick = []
        for r in range(ROWS):
            where = chan * ROWS + r if step == 4 else chan + OUT * r
            pick.append(jnp.where(spot == where, 1.0, 0.0).astype(jnp.bfloat16))
        for dx in range(3):
            for n in range(6):
                total = None
                for dy in range(3):
                    r = n - 1 + dy - 1
                    if 0 <= r < ROWS:
                        term = jnp.dot(
                            ref[3 * dy + dx], pick[r], preferred_element_type=jnp.float32
                        )
                        total = term if total is None else total + term
                band[dx, pl.ds(n * OUT, OUT), :] = total.astype(jnp.bfloat16)


def frame(*operands):
    unit = (CH, ROWS, COLS)
    bf16, f32 = jnp.bfloat16, jnp.float32
    vmem = pltpu.VMEM
    dma = pltpu.SemaphoreType.DMA
    return pl.pallas_call(
        frame_kernel,
        name="frame",
        out_shape=vmem((OUT, NY * TXD * COLS), bf16),
        in_specs=[pl.BlockSpec(memory_space=pl.ANY)] * len(operands),
        out_specs=pl.BlockSpec(memory_space=vmem),
        scratch_shapes=[
            vmem((8, 128), jnp.int32),
            vmem((128, 128), jnp.int32),
            vmem((TILES, DEPTH), jnp.int32),
            vmem((16, 128), jnp.int32),
            pltpu.SMEM((16, 128), jnp.int32),
            pltpu.SMEM((NY,), jnp.int32),
            pltpu.SMEM((NY,), jnp.int32),
            vmem((9, OUT, CH + 1), bf16),
            vmem((1, OUT), f32),
            vmem((9, OUT, OUT), bf16),
            vmem((1, OUT), f32),
            dma((10,)),
            vmem((128,) + unit, bf16),
            vmem((128, ROWS, COLS), bf16),
            vmem((128, ROWS, COLS), bf16),
            vmem((256, ROWS, COLS), bf16),
            vmem((TILES * TSTEP, ROWS, COLS), f32),
            vmem((192, ROWS, COLS), bf16),
            vmem((192, ROWS, COLS), bf16),
            vmem((4, 8, 2) + unit, bf16),
            vmem((4, 8, 2) + unit, bf16),
            vmem((4, 4, 3) + unit, bf16),
            vmem((4, 4, 3) + unit, f32),
            vmem((4, 4, 3) + unit, bf16),
            vmem((4, 2, 3) + unit, bf16),
            vmem((4, 2, 3) + unit, bf16),
            vmem((4, 1, 3) + unit, bf16),
            vmem((4, 1, 3) + unit, bf16),
            vmem((4, 2) + unit, bf16),
            vmem((4, 2) + unit, bf16),
            vmem((TILES, ROWS, COLS), bf16),
            vmem((2, TILES, ROWS, COLS), bf16),
            vmem((2, TXD, ROWS, COLS), bf16),
            vmem((3, TXD, ROWS, COLS), bf16),
            vmem((TYD, TXD, DEEP1, COLS), f32),
            vmem((3, TXD, DEEP1, COLS), f32),
            vmem((TYD + 2, DEEP1, WIDE), bf16),
            vmem((2, 2, 32, COLS), f32),
            vmem((2, 2, 32, COLS), f32),
            vmem((TYD + 2, DEEP1, COLS), f32),
            vmem((3, 6 * OUT, DEEP1), bf16),
            vmem((3, 6 * OUT, DEEP2), bf16),
            vmem((18, OUT, WIDE), f32),
            vmem((TYD, DEEP2, WIDE), bf16),
            vmem((OUT, WIDE), bf16),
            vmem((OUT, WIDE), bf16),
            vmem((16, OUT, TXD * COLS), f32),
            vmem((16, OUT, TXD * COLS), bf16),
            vmem((NY, OUT, TXD * COLS), bf16),
            dma(()),
            dma((2,)),
            dma((2,)),
            dma(()),
            dma((2,)),
            dma((4,)),
            dma((4, 9)),
            dma(()),
            dma((4,)),
            dma((2,)),
            dma((2,)),
            dma((2,)),
            dma((2,)),
        ],
        compiler_params=pltpu.CompilerParams(
            collective_id=0, has_side_effects=True, vmem_limit_bytes=VMEM_BYTES
        ),
    )(*operands)


def shards(
    payload, opacity, depth_order, footprints, panel_map,
    conv1_weight, conv1_bias, conv2_weight, conv2_bias,
):
    shown = frame(
        payload.transpose(0, 2, 1, 3),
        opacity,
        jnp.asarray(patterns()),
        footprints,
        depth_order,
        panel_map,
        conv1_weight,
        conv1_bias[None],
        conv2_weight,
        conv2_bias[None],
    )
    return shown[None, None, None]


SPECS = (
    P(("gx", "gy"), None, None, None),
    P(("gx", "gy"), None, None),
    P(("gx", "gy"), None),
    P(),
    P(),
    P(),
    P(),
    P(),
    P(),
)


def solution(mesh):
    return jax.shard_map(
        shards,
        mesh=mesh,
        in_specs=SPECS,
        out_specs=P("gx", "gy", None, None, None),
        check_vma=False,
    )
```

```python
import functools

import jax
import jax.numpy as jnp
import numpy as np
from jax import lax
from jax.experimental import pallas as pl
from jax.experimental.pallas import tpu as pltpu
from jax.sharding import PartitionSpec as P

MESH = pl.DeviceIdType.MESH
TYD = 4
TXD = 2
TILES = 8
DEPTH = 16
CH = 35
ROWS = 4
COLS = 128
NX = 8
NY = 16
SIDE = 4
TSTEP = DEPTH + 2
MASKS = ((4, 12, 1, 3), (12, 4, 3, 1), (1, 3, 4, 12), (3, 1, 12, 4))


def kappa(q, k):
    m = MASKS[q]
    return (m[1] if k & 4 else 0) ^ (m[2] if k & 2 else 0) ^ (m[3] if k & 1 else 0)


def hops(offset):
    return sum(min(d, SIDE - d) for d in offset)


OTHERS = sorted(
    ((dx, dz) for dx in range(SIDE) for dz in range(SIDE) if dx or dz), key=hops, reverse=True
)


def shifted(c, offset):
    return (c // SIDE + offset[0]) % SIDE * SIDE + (c % SIDE + offset[1]) % SIDE


def flip4(p, d):
    if d == 0:
        return p
    if d == 1:
        return p + 1 - 2 * (p % 2)
    if d == 2:
        return (p + 2) % SIDE
    return 3 - p


def paired(c, mask):
    return flip4(c // SIDE, mask // SIDE) * SIDE + flip4(c % SIDE, mask % SIDE)


def patterns():
    base = np.zeros((2, 4, 8, 2), np.int32)
    rest = np.zeros((2, 4, 8, 2), np.int32)
    mask = np.zeros((4, 8, 3, 2), np.int32)
    which = np.zeros((4, 8, 3, 2), np.int32)
    for q in range(4):
        j, g = q % 2, q // 2
        for k in range(8):
            for s in range(2):
                flip = kappa(q, k) ^ (MASKS[q][0] if s else 0)
                for f in range(2):
                    jy = (1 + g) if f else (3 if g else 0)
                    base[s, q, k, f] = flip
                    rest[s, q, k, f] = jy * TXD + j
                for e in range(3):
                    jy = (1 + g) if e != 1 else (3 if g else 0)
                    mask[q, k, e, s] = flip
                    which[q, k, e, s] = jy * TXD + j + TILES * (0, 1 - g, 1)[e]
    rows = np.zeros((8, 128), np.int32)
    rows[0] = base.reshape(-1)
    rows[1] = rest.reshape(-1)
    rows[2:4].reshape(-1)[:192] = mask.reshape(-1)
    rows[4:6].reshape(-1)[:192] = which.reshape(-1)
    return rows


def fill_tables(rows, foot, order, out, gx, gy):
    i32 = jnp.int32
    own = foot[pl.ds(gx * NY + gy, 1), :]
    slot = ((own >> 3) & (NY - 1)) * TILES + (own & (TILES - 1))
    across = lax.broadcasted_iota(i32, (128, 128), 1)
    along = lax.broadcasted_iota(i32, (128, 128), 0)
    slots = jnp.sum(jnp.where(across == along, slot, 0), axis=1, keepdims=True)
    target = (rows[0:1] ^ gy) * TILES + rows[1:2]
    out[0:1] = jnp.max(jnp.where(slots == across, along, 0), axis=0, keepdims=True)
    out[1:2] = jnp.max(jnp.where(slots == target, along, 0), axis=0, keepdims=True)

    listed = order[...]
    tile = lax.broadcasted_iota(i32, (TILES, 128), 0)
    for n in range(2):
        which = rows[4 + n : 5 + n]
        local = which & (TILES - 1)
        brick = ((gx - (which >> 3)) & (NX - 1)) * NY + (rows[2 + n : 3 + n] ^ gy)
        rank = jnp.zeros((TILES, 128), i32)
        for d in range(DEPTH):
            hit = jnp.logical_and(listed[:, d : d + 1] == brick, tile == local)
            rank = jnp.minimum(rank, jnp.where(hit, d - (DEPTH + 1), 0))
        rank = jnp.min(rank, axis=0, keepdims=True)
        out[2 + n : 3 + n] = local * TSTEP + DEPTH + 1 + rank

    tile = lax.broadcasted_iota(i32, (TILES, DEPTH), 0)
    part = jnp.minimum((gx - (listed >> 4)) & (NX - 1), 1)
    out[8:16, 0:DEPTH] = (part * NY + (listed & (NY - 1))) * TILES + tile


OUT = 32
GROUP = 4
VMEM_BYTES = 62 << 20
WIDE = 3 * COLS
DEEP1 = (CH + 1) * ROWS


def frame_kernel(
    pay_h, opa_h, rows_h, foot_h, order_h, panel_h, w1_h, b1_h, w2_h, b2_h, shown,
    rows, foot, order, tabv, tab, panel, inv, w1, b1, w2, b2, tsem,
    pay, opa, asend, abuf, tb, tsend, trecv, s1, r1, s2, acc, r2, s3, r3, s4, r4, ys, yr,
    cov, cov_side, cov_over, cov_under, stage, stage_y, v1, pack, rim, edge, band1, band2, h_acc, v2, base, strips,
    lsem, a_s, a_r, t_s, t_r, m_s, m_r, y_s, y_r, c_sem, h_s, h_r, d_sem,
):
    gx = lax.axis_index("gx")
    me = lax.axis_index("gy")
    up = (gx + 1) % NX
    down = (gx + NX - 1) % NX
    right = (me + 1) % NY
    left = (me + NY - 1) % NY
    early = [
        pltpu.make_async_copy(src, dst, tsem.at[n])
        for n, (src, dst) in enumerate(
            ((rows_h, rows), (foot_h, foot), (order_h, order), (opa_h, opa), (panel_h, panel),
             (w1_h, w1), (b1_h, b1), (w2_h, w2), (b2_h, b2))
        )
    ]
    loads = []
    for i in range(8):
        part = pl.ds(16 * i, 16)
        loads.append(pltpu.make_async_copy(pay_h.at[part], pay.at[part], lsem))
    for load in early[:4] + loads + early[4:]:
        load.start()

    barrier = pltpu.get_barrier_semaphore()

    for offset in OTHERS + [(0, 0)]:
        col = shifted(me, offset)
        for row in (up, down, gx):
            if row is not gx or offset != (0, 0):
                pl.semaphore_signal(barrier, inc=1, device_id=(row, col), device_id_type=MESH)

    for load in early[:3]:
        load.wait()
    fill_tables(rows, foot, order, tabv, gx, me)
    to_smem = pltpu.make_async_copy(tabv, tab, tsem.at[9])
    early[3].wait()
    to_smem.start()
    to_smem.wait()

    def pack_alpha(i, _):
        asend[i] = opa[tab[0, i]]
        return 0

    lax.fori_loop(0, 128, pack_alpha, 0, unroll=8)
    for e in range(TILES):
        abuf[me * TILES + e] = asend[me * TILES + e]
    pltpu.make_async_copy(pay_h, pay, lsem).wait()

    def pack_raw(q, lo, hi):
        def body(k, _):
            for f in range(2):
                s1[q, k, f] = pay[tab[1, 64 + (q * 8 + k) * 2 + f]]
            return 0

        lax.fori_loop(lo, hi, body, 0)

    for q in range(4):
        pack_raw(q, 2, 8)
    pl.semaphore_wait(barrier, 47)

    def alpha_copy(i):
        return pltpu.make_async_remote_copy(
            src_ref=asend.at[pl.ds(i * TILES, TILES)],
            dst_ref=abuf.at[pl.ds(me * TILES, TILES)],
            send_sem=a_s.at[0],
            recv_sem=a_r.at[0],
            device_id=(gx, i),
            device_id_type=MESH,
        )

    alpha_on = pltpu.make_async_remote_copy(
        src_ref=abuf.at[pl.ds(0, 128)],
        dst_ref=abuf.at[pl.ds(128, 128)],
        send_sem=a_s.at[1],
        recv_sem=a_r.at[1],
        device_id=(up, me),
        device_id_type=MESH,
    )

    for offset in OTHERS:
        alpha_copy(shifted(me, offset)).start()

    groups = ((4, 8), (2, 4), (1, 2), (0, 1))

    def raw_copy(q, n):
        lo, hi = groups[n]
        part = pl.ds(lo, hi - lo)
        return pltpu.make_async_remote_copy(
            src_ref=s1.at[q, part],
            dst_ref=r1.at[q, part],
            send_sem=m_s.at[0],
            recv_sem=m_r.at[q, 0 if n == 0 else 1],
            device_id=(gx, paired(me, MASKS[q][0])),
            device_id_type=MESH,
        )

    raw = [[raw_copy(q, n) for n in range(4)] for q in range(4)]
    for n in range(2):
        for q in range(4):
            raw[q][n].start()
    for q in range(4):
        pack_raw(q, 0, 2)
    for load in early[4:]:
        load.wait()

    def invert(g, _):
        at = 0
        for strip in range(NY):
            at = jnp.where(panel[strip] == g, strip, at)
        inv[g] = at
        return 0

    lax.fori_loop(0, NY, invert, 0)

    spread_weights(w1, w2, band1, band2)

    others = pl.ds(0, (NY - 1) * TILES)
    alphas = pltpu.make_async_remote_copy(
        src_ref=asend.at[others],
        dst_ref=abuf.at[others],
        send_sem=a_s.at[0],
        recv_sem=a_r.at[0],
        device_id=(gx, right),
        device_id_type=MESH,
    )
    alphas.wait_recv()
    alpha_on.start()
    alpha_on.wait_recv()

    for t in range(TILES):
        tb[t * TSTEP + DEPTH + 1] = jnp.zeros((ROWS, COLS), jnp.float32)

    def through(d, passed):
        out = []
        for t in range(TILES):
            tb[t * TSTEP + d] = passed[t]
            alpha = abuf[tab[8 + t, d]].astype(jnp.float32)
            out.append(passed[t] * (1.0 - alpha))
        return tuple(out)

    last = lax.fori_loop(
        0, DEPTH, through, tuple(jnp.ones((ROWS, COLS), jnp.float32) for _ in range(TILES))
    )
    for t in range(TILES):
        cov[t] = (1.0 - last[t]).astype(jnp.bfloat16)

    def fill(i, _):
        tsend[i] = tb[tab[2, i]].astype(jnp.bfloat16)
        return 0

    def fill_rest(i, _):
        tsend[128 + i] = tb[tab[3, i]].astype(jnp.bfloat16)
        return 0

    lax.fori_loop(0, 128, fill, 0, unroll=8)
    lax.fori_loop(0, 64, fill_rest, 0, unroll=8)

    def weight_range(q, k, back):
        g = q // 2
        start, size = ((0, 4 if g else 2), (4 if g else 2, 2 if g else 4))[back]
        return pl.ds((q * 8 + k) * 6 + start, size)

    def weight_copy(q, k, back):
        part = weight_range(q, k, back)
        return pltpu.make_async_remote_copy(
            src_ref=tsend.at[part],
            dst_ref=trecv.at[part],
            send_sem=t_s,
            recv_sem=t_r.at[1 if k >= 4 else 0],
            device_id=(down if back else gx, paired(me, kappa(q, k))),
            device_id_type=MESH,
        )

    for k in (7, 6, 5, 4, 3, 2, 1, 0):
        for q in range(4):
            for back in range(2):
                if k == 0 and back == 0:
                    g = q // 2
                    for e in range(4 if g else 2):
                        trecv[q * 48 + e] = tsend[q * 48 + e]
                else:
                    weight_copy(q, k, back).start()

    def weight_group(size, sem):
        part = pl.ds(0, size)
        return pltpu.make_async_remote_copy(
            src_ref=tsend.at[part],
            dst_ref=trecv.at[part],
            send_sem=t_s,
            recv_sem=t_r.at[sem],
            device_id=(gx, right),
            device_id_type=MESH,
        )

    first_row = pl.ds(0, TXD)
    last_row = pl.ds((TYD - 1) * TXD, TXD)
    covers = [
        pltpu.make_async_remote_copy(
            src_ref=src,
            dst_ref=dst,
            send_sem=c_sem.at[0],
            recv_sem=c_sem.at[1],
            device_id=(row, col),
            device_id_type=MESH,
        )
        for src, dst, row, col in (
            (
                (cov, cov_side.at[0], gx, right),
                (cov, cov_side.at[1], gx, left),
                (cov.at[last_row], cov_over.at[0], up, right),
                (cov.at[last_row], cov_over.at[1], up, left),
                (cov.at[first_row], cov_under.at[0], down, right),
                (cov.at[first_row], cov_under.at[1], down, left),
                (cov.at[first_row], cov_under.at[2], down, me),
            )
        )
    ]
    for copy in covers:
        copy.start()
    covered_part = pl.ds(0, 2 * TILES + 5 * TXD)
    all_covers = pltpu.make_async_remote_copy(
        src_ref=asend.at[covered_part],
        dst_ref=abuf.at[covered_part],
        send_sem=c_sem.at[0],
        recv_sem=c_sem.at[1],
        device_id=(gx, right),
        device_id_type=MESH,
    )
    for n in range(2, 4):
        for q in range(4):
            raw[q][n].start()

    def weighed(q, k):
        own = (q * 8 + k) * 2
        lead = (q * 8 + k) * 6
        w = [trecv[lead + n].astype(jnp.float32)[None] for n in range(6)]
        own_f = pay[tab[1, own]].astype(jnp.float32)
        got_f = r1[q, k, 0].astype(jnp.float32)
        mid = w[2] * own_f + w[3] * got_f
        own_a = pay[tab[1, own + 1]].astype(jnp.float32)
        got_a = r1[q, k, 1].astype(jnp.float32)
        first = w[0] * own_a + w[1] * got_a
        third = w[4] * own_a + w[5] * got_a
        return first, mid, third

    def merge_sent(q, lo, hi):
        def body(k, _):
            for e, v in enumerate(weighed(q, k)):
                s2[q, k - 4, e] = v.astype(jnp.bfloat16)
            return 0

        lax.fori_loop(lo, hi, body, 0)

    def merge_kept(q, lo, hi):
        def body(k, _):
            for e, v in enumerate(weighed(q, k)):
                acc[q, k, e] = v
            return 0

        lax.fori_loop(lo, hi, body, 0)

    def step_copy(src, dst, q, lo, hi, step, sem):
        part = pl.ds(lo, hi - lo)
        return pltpu.make_async_remote_copy(
            src_ref=src.at[q, part],
            dst_ref=dst.at[q, part],
            send_sem=m_s.at[step - 1],
            recv_sem=m_r.at[q, sem],
            device_id=(gx, paired(me, MASKS[q][step - 1])),
            device_id_type=MESH,
        )

    def whole(src, dst, part, send, recv):
        return pltpu.make_async_remote_copy(
            src_ref=src.at[part],
            dst_ref=dst.at[part],
            send_sem=send,
            recv_sem=recv,
            device_id=(gx, right),
            device_id_type=MESH,
        )

    two = [[step_copy(s2, r2, q, lo, hi, 2, 2 + n) for n, (lo, hi) in enumerate(groups[1:])] for q in range(4)]
    three = [[step_copy(s3, r3, q, lo, hi, 3, 5 + n) for n, (lo, hi) in enumerate(groups[2:])] for q in range(4)]

    def last_copy(q, crossing):
        size = 2 - q // 2 if crossing else 1 + q // 2
        part = pl.ds(1 + q // 2 if crossing else 0, size)
        return pltpu.make_async_remote_copy(
            src_ref=s4.at[q, 0, part],
            dst_ref=r4.at[q, 0, part],
            send_sem=m_s.at[3],
            recv_sem=m_r.at[q, 7 + crossing],
            device_id=(gx, paired(me, MASKS[q][3])),
            device_id_type=MESH,
        )

    four = [[last_copy(q, crossing) for crossing in range(2)] for q in range(4)]

    weight_group(96, 1).wait_recv()
    for q in range(4):
        raw[q][0].wait_recv()
        merge_sent(q, 6, 8)
        two[q][0].start()
    for q in range(4):
        merge_sent(q, 4, 6)
        two[q][1].start()
        two[q][2].start()
    weight_group(84, 0).wait_recv()
    for q in range(4):
        half = (q, pl.ds(0, 4))
        whole(s1, r1, half, m_s.at[0], m_r.at[q, 1]).wait_recv()
        merge_kept(q, 0, 4)

    def added(src, q, k):
        return [acc[q, k, e] + src[q, k, e].astype(jnp.float32) for e in range(3)]

    def forward(dst, src, q, k, to):
        for e, v in enumerate(added(src, q, k)):
            dst[q, to, e] = v.astype(jnp.bfloat16)

    def keep(src, q, k):
        for e, v in enumerate(added(src, q, k)):
            acc[q, k, e] = v

    for q in range(4):
        two[q][0].wait_recv()
        forward(s3, r2, q, 3, 1)
        three[q][0].start()
        forward(s3, r2, q, 2, 0)
        three[q][1].start()
    for q in range(4):
        two[q][1].wait_recv()
        keep(r2, q, 1)
        two[q][2].wait_recv()
        keep(r2, q, 0)
    for q in range(4):
        three[q][0].wait_recv()
        forward(s4, r3, q, 1, 0)
        four[q][1].start()
        four[q][0].start()
    for q in range(4):
        three[q][1].wait_recv()
        keep(r3, q, 0)

    def cross_copy(q):
        part = pl.ds(q // 2, 2 - q // 2)
        return pltpu.make_async_remote_copy(
            src_ref=ys.at[q, part],
            dst_ref=yr.at[q, part],
            send_sem=y_s,
            recv_sem=y_r.at[q],
            device_id=(up, me),
            device_id_type=MESH,
        )

    cross = [cross_copy(q) for q in range(4)]

    def spread(ref, v):
        for c in range(CH):
            ref[pl.ds(c * ROWS, ROWS), :] = v[c]

    def place(jy, j, v):
        spread(stage.at[jy, j], v)
        stage[jy, j, pl.ds(CH * ROWS, ROWS), :] = cov[jy * TXD + j].astype(jnp.float32)
        v1[jy + 1, :, pl.ds(j * COLS, COLS)] = stage[jy, j].astype(jnp.bfloat16)

    def final(q, e):
        return acc[q, 0, e] + r4[q, 0, e].astype(jnp.float32)

    for q in range(4):
        g, j = q // 2, q % 2
        four[q][1].wait_recv()
        ys[q, 1] = final(q, 2).astype(jnp.bfloat16)
        if g == 0:
            ys[q, 0] = final(q, 1).astype(jnp.bfloat16)
        cross[q].start()
    for q in range(4):
        g, j = q // 2, q % 2
        spread(stage_y.at[1 + g, j], ys[q, 1].astype(jnp.float32))
        if g == 0:
            spread(stage_y.at[0, j], ys[q, 0].astype(jnp.float32))
    for q in range(4):
        g, j = q // 2, q % 2
        four[q][0].wait_recv()
        own = final(q, 0)
        acc[q, 0, 0] = own
        spread(stage.at[1 + g, j], own)
        if g:
            place(3, j, final(q, 1))

    def edge_copy(src, dst, n, row, col):
        n = min(n, 1)
        return pltpu.make_async_remote_copy(
            src_ref=src,
            dst_ref=dst,
            send_sem=h_s.at[n],
            recv_sem=h_r.at[n],
            device_id=(row, col),
            device_id_type=MESH,
        )

    mine = pl.ds(0, TXD * COLS)
    edges = (
        edge_copy(v1.at[4, :, mine], v1.at[0, :, mine], 0, up, me),
        edge_copy(pack.at[0, 0], rim.at[0, 0], 1, gx, right),
        edge_copy(pack.at[0, 1], rim.at[0, 1], 2, gx, left),
        edge_copy(pack.at[1, 0], rim.at[1, 0], 3, up, right),
        edge_copy(pack.at[1, 1], rim.at[1, 1], 4, up, left),
    )
    edges[0].start()

    lane = lax.broadcasted_iota(jnp.int32, (8, COLS), 1)
    groups_of = DEEP1 // 8

    def packed(ref, side):
        total = jnp.zeros((8, COLS), jnp.float32)
        for i in range(groups_of):
            v = ref[pl.ds(8 * i, 8), :]
            if i:
                v = pltpu.roll(v, 4 * i, 1)
            pair = (COLS // 2 - 1 + 2 * i) % (COLS // 2) if side == 0 else 2 * i
            total = jnp.where((lane >> 1) == pair, v, total)
        return total

    for side in range(2):
        j = 1 - side
        for n, ref in enumerate((stage.at[1, j], stage.at[2, j], stage.at[3, j], stage_y.at[0, j])):
            pack[0, side, pl.ds(8 * n, 8), :] = packed(ref, side)
        for n, ref in enumerate((stage.at[3, j], stage_y.at[0, j], stage_y.at[1, j], stage_y.at[2, j])):
            pack[1, side, pl.ds(8 * n, 8), :] = packed(ref, side)
        edges[1 + side].start()
        edges[3 + side].start()

    all_covers.wait_recv()
    for j in range(TXD):
        stage_y[0, j, pl.ds(CH * ROWS, ROWS), :] = cov_under[2, j].astype(jnp.float32)
        low = jnp.where(gx < NX - 1, stage_y[0, j], 0.0)
        v1[5, :, pl.ds(j * COLS, COLS)] = low.astype(jnp.bfloat16)
    for q in range(4):
        g, j = q // 2, q % 2
        cross[q].wait_recv()
        if g == 0:
            place(0, j, yr[q, 0].astype(jnp.float32))
        place(1 + g, j, acc[q, 0, 0] + yr[q, 1].astype(jnp.float32))
    for n in range(16):
        rows_of = pl.ds(n % 4, OUT, stride=ROWS)
        row = jnp.concatenate([stage[n // 4, j, rows_of, :] for j in range(TXD)], axis=1)
        base[n] = row.astype(jnp.bfloat16).astype(jnp.float32)
    rims = whole(pack, rim, pl.ds(0, 2), h_s.at[1], h_r.at[1])
    edges[0].wait_recv()
    rims.wait_recv()

    last_tile = pl.ds(2 * COLS, COLS)
    cover_lane = lax.broadcasted_iota(jnp.int32, (ROWS, COLS), 1)
    has = (me > 0, me < NY - 1)
    for blk in range(-1, TYD + 1):
        total = None
        for side in range(2):
            part = None
            if blk >= 1:
                part = rim[0, side, pl.ds(8 * (blk - 1), 8), :]
            if blk <= 2:
                more = rim[1, side, pl.ds(8 * (blk + 1), 8), :]
                part = more if part is None else part + more
            part = jnp.where(has[side], part, 0.0)
            total = part if total is None else total + part
        if blk < 0:
            sides = cov_over[0, 1], cov_over[1, 0]
            inside = gx > 0
        elif blk == TYD:
            sides = cov_under[0, 1], cov_under[1, 0]
            inside = gx < NX - 1
        else:
            sides = cov_side[0, blk * TXD + 1], cov_side[1, blk * TXD]
            inside = None
        covered = jnp.where(
            cover_lane >= COLS // 2,
            jnp.where(has[0], sides[0].astype(jnp.float32), 0.0),
            jnp.where(has[1], sides[1].astype(jnp.float32), 0.0),
        )
        for i in range(groups_of):
            edge[blk + 1, pl.ds(8 * i, 8), :] = pltpu.roll(total, COLS - 4 * i, 1) if i else total
        edge[blk + 1, pl.ds(CH * ROWS, ROWS), :] = covered
        value = edge[blk + 1]
        if inside is not None:
            value = jnp.where(inside, value, 0.0)
        v1[blk + 1, :, last_tile] = value.astype(jnp.bfloat16)
    wide_zero = jnp.zeros((DEEP1, TXD * COLS), jnp.bfloat16)

    @pl.when(gx == 0)
    def _():
        v1[0, :, mine] = wide_zero

    def product(band, rows, field):
        total = None
        for dx in range(3):
            z = jnp.dot(band(dx, rows), field, preferred_element_type=jnp.float32)
            if dx != 1:
                z = pltpu.roll(z, (1 - dx) % WIDE, 1)
            total = z if total is None else total + z
        return total

    def band_one(dx, rows):
        return band1[dx, rows, :]

    def column(ref):
        eye = lax.broadcasted_iota(jnp.int32, (OUT, OUT), 0) == lax.broadcasted_iota(jnp.int32, (OUT, OUT), 1)
        return jnp.sum(jnp.where(eye, ref[...], 0.0), axis=1, keepdims=True)

    every = pl.ds(0, 6 * OUT)
    head = product(band_one, pl.ds(4 * OUT, 2 * OUT), v1[0])
    h_acc[0] = head[:OUT]
    h_acc[1] = head[OUT:]
    for blk in range(TYD):
        s = product(band_one, every, v1[blk + 1])
        y = 4 * blk
        for n in range(6):
            piece = s[n * OUT : (n + 1) * OUT]
            h_acc[y + n] = piece + h_acc[y + n] if n < 2 else piece
    tail = product(band_one, pl.ds(0, 2 * OUT), v1[5])
    bias_one = column(b1)
    far = lax.broadcasted_iota(jnp.int32, (OUT, WIDE), 1)
    cut = jnp.logical_or(
        jnp.logical_and(far >= 2 * COLS + COLS // 2, me == 0),
        jnp.logical_and(
            jnp.logical_and(far >= 2 * COLS, far < 2 * COLS + COLS // 2), me == NY - 1
        ),
    )
    for n in range(18):
        raw_sum = h_acc[n]
        if n >= 16:
            raw_sum = raw_sum + tail[(n - 16) * OUT : (n - 15) * OUT]
        pre = raw_sum + bias_one
        h = pre * lax.logistic(pre)
        h = jnp.where(cut, 0.0, h)
        if n == 0:
            h = jnp.where(gx > 0, h, 0.0)
        elif n == 17:
            h = jnp.where(gx < NX - 1, h, 0.0)
        v2[n] = h.astype(jnp.bfloat16)

    bias_two = column(b2)

    def shade(g):
        row = inv[g]
        field = jnp.concatenate([v2[row], v2[row + 1], v2[row + 2]], axis=0)
        z = jnp.dot(band2[...], field, preferred_element_type=jnp.float32)
        total = z[OUT : 2 * OUT] + pltpu.roll(z[:OUT], 1, 1)
        total = total + pltpu.roll(z[2 * OUT :], WIDE - 1, 1)
        return (total[:, : TXD * COLS] + bias_two + base[row]).astype(jnp.bfloat16)

    def window(col):
        start = pl.multiple_of(col * (TXD * COLS), TXD * COLS)
        return shown.at[:, pl.ds(start, TXD * COLS)]

    def strip_copy(g):
        return pltpu.make_async_remote_copy(
            src_ref=strips.at[g],
            dst_ref=window(me),
            send_sem=d_sem.at[0],
            recv_sem=d_sem.at[1],
            device_id=(gx, g),
            device_id_type=MESH,
        )

    for n in range(0, len(OTHERS), GROUP):
        columns = [shifted(me, offset) for offset in OTHERS[n : n + GROUP]]
        for g in columns:
            strips[g] = shade(g)
        for g in columns:
            strip_copy(g).start()
    start = pl.multiple_of(me * (TXD * COLS), TXD * COLS)
    shown[:, pl.ds(start, TXD * COLS)] = shade(me)

    edges[0].wait_send()
    rims.wait_send()
    all_covers.wait_send()

    alphas.wait_send()
    alpha_on.wait_send()
    weight_group(180, 0).wait_send()
    every_q = pl.ds(0, 4)
    for n, (src, dst) in enumerate(((s1, r1), (s2, r2), (s3, r3), (s4, r4))):
        whole(src, dst, every_q, m_s.at[n], m_r.at[0, 0]).wait_send()
    whole(ys, yr, pl.ds(0, 3), y_s, y_r.at[0]).wait_send()
    parts = pl.ds(0, NY - 1)
    all_strips = pltpu.make_async_remote_copy(
        src_ref=strips.at[parts],
        dst_ref=strips.at[parts],
        send_sem=d_sem.at[0],
        recv_sem=d_sem.at[1],
        device_id=(gx, right),
        device_id_type=MESH,
    )
    all_strips.wait_send()
    all_strips.wait_recv()


def spread_weights(w1, w2, band1, band2):
    def pick(ins, wide, first, step):
        chan = lax.broadcasted_iota(jnp.int32, (ins, wide), 0)
        spot = lax.broadcasted_iota(jnp.int32, (ins, wide), 1)
        return jnp.where(spot == chan * step + first, 1.0, 0.0).astype(jnp.bfloat16)

    def spread(terms):
        total = None
        for taps, place in terms:
            term = jnp.dot(taps, place, preferred_element_type=jnp.float32)
            total = term if total is None else total + term
        return total.astype(jnp.bfloat16)

    picks = [pick(CH + 1, DEEP1, r, ROWS) for r in range(ROWS)]
    for dx in range(3):
        for n in range(6):
            rows = [(dy, n + dy - 2) for dy in range(3) if 0 <= n + dy - 2 < ROWS]
            band1[dx, pl.ds(n * OUT, OUT), :] = spread([(w1[3 * dy + dx], picks[r]) for dy, r in rows])
    picks = [pick(OUT, 3 * OUT, dy * OUT, 1) for dy in range(3)]
    for dx in range(3):
        band2[pl.ds(dx * OUT, OUT), :] = spread([(w2[3 * dy + dx], picks[dy]) for dy in range(3)])


def frame(*operands):
    unit = (CH, ROWS, COLS)
    bf16, f32 = jnp.bfloat16, jnp.float32
    vmem = pltpu.VMEM
    dma = pltpu.SemaphoreType.DMA
    return pl.pallas_call(
        frame_kernel,
        name="frame",
        out_shape=vmem((OUT, NY * TXD * COLS), bf16),
        in_specs=[pl.BlockSpec(memory_space=pl.ANY)] * len(operands),
        out_specs=pl.BlockSpec(memory_space=vmem),
        scratch_shapes=[
            vmem((8, 128), jnp.int32),
            vmem((128, 128), jnp.int32),
            vmem((TILES, DEPTH), jnp.int32),
            vmem((16, 128), jnp.int32),
            pltpu.SMEM((16, 128), jnp.int32),
            pltpu.SMEM((NY,), jnp.int32),
            pltpu.SMEM((NY,), jnp.int32),
            vmem((9, OUT, CH + 1), bf16),
            vmem((1, OUT), f32),
            vmem((9, OUT, OUT), bf16),
            vmem((1, OUT), f32),
            dma((10,)),
            vmem((128,) + unit, bf16),
            vmem((128, ROWS, COLS), bf16),
            vmem((128, ROWS, COLS), bf16),
            vmem((256, ROWS, COLS), bf16),
            vmem((TILES * TSTEP, ROWS, COLS), f32),
            vmem((192, ROWS, COLS), bf16),
            vmem((192, ROWS, COLS), bf16),
            vmem((4, 8, 2) + unit, bf16),
            vmem((4, 8, 2) + unit, bf16),
            vmem((4, 4, 3) + unit, bf16),
            vmem((4, 4, 3) + unit, f32),
            vmem((4, 4, 3) + unit, bf16),
            vmem((4, 2, 3) + unit, bf16),
            vmem((4, 2, 3) + unit, bf16),
            vmem((4, 1, 3) + unit, bf16),
            vmem((4, 1, 3) + unit, bf16),
            vmem((4, 2) + unit, bf16),
            vmem((4, 2) + unit, bf16),
            vmem((TILES, ROWS, COLS), bf16),
            vmem((2, TILES, ROWS, COLS), bf16),
            vmem((2, TXD, ROWS, COLS), bf16),
            vmem((3, TXD, ROWS, COLS), bf16),
            vmem((TYD, TXD, DEEP1, COLS), f32),
            vmem((3, TXD, DEEP1, COLS), f32),
            vmem((TYD + 2, DEEP1, WIDE), bf16),
            vmem((2, 2, 32, COLS), f32),
            vmem((2, 2, 32, COLS), f32),
            vmem((TYD + 2, DEEP1, COLS), f32),
            vmem((3, 6 * OUT, DEEP1), bf16),
            vmem((3 * OUT, 3 * OUT), bf16),
            vmem((18, OUT, WIDE), f32),
            vmem((18, OUT, WIDE), bf16),
            vmem((16, OUT, TXD * COLS), f32),
            vmem((NY, OUT, TXD * COLS), bf16),
            dma(()),
            dma((2,)),
            dma((2,)),
            dma(()),
            dma((2,)),
            dma((4,)),
            dma((4, 9)),
            dma(()),
            dma((4,)),
            dma((2,)),
            dma((2,)),
            dma((2,)),
            dma((2,)),
        ],
        compiler_params=pltpu.CompilerParams(
            collective_id=0, has_side_effects=True, vmem_limit_bytes=VMEM_BYTES
        ),
    )(*operands)


def shards(
    payload, opacity, depth_order, footprints, panel_map,
    conv1_weight, conv1_bias, conv2_weight, conv2_bias,
):
    shown = frame(
        payload.transpose(0, 2, 1, 3),
        opacity,
        jnp.asarray(patterns()),
        footprints,
        depth_order,
        panel_map,
        conv1_weight,
        conv1_bias[None],
        conv2_weight,
        conv2_bias[None],
    )
    return shown[None, None, None]


SPECS = (
    P(("gx", "gy"), None, None, None),
    P(("gx", "gy"), None, None),
    P(("gx", "gy"), None),
    P(),
    P(),
    P(),
    P(),
    P(),
    P(),
)


def solution(mesh):
    return jax.shard_map(
        shards,
        mesh=mesh,
        in_specs=SPECS,
        out_specs=P("gx", "gy", None, None, None),
        check_vma=False,
    )
```

```python
import functools

import jax
import jax.numpy as jnp
import numpy as np
from jax import lax
from jax.experimental import pallas as pl
from jax.experimental.pallas import tpu as pltpu
from jax.sharding import PartitionSpec as P

MESH = pl.DeviceIdType.MESH
TYD = 4
TXD = 2
TILES = 8
DEPTH = 16
CH = 35
ROWS = 4
COLS = 128
NX = 8
NY = 16
SIDE = 4
TSTEP = DEPTH + 2
MASKS = ((4, 12, 1, 3), (12, 4, 3, 1), (1, 3, 4, 12), (3, 1, 12, 4))


def kappa(q, k):
    m = MASKS[q]
    return (m[1] if k & 4 else 0) ^ (m[2] if k & 2 else 0) ^ (m[3] if k & 1 else 0)


def hops(offset):
    return sum(min(d, SIDE - d) for d in offset)


OTHERS = sorted(
    ((dx, dz) for dx in range(SIDE) for dz in range(SIDE) if dx or dz), key=hops, reverse=True
)


def shifted(c, offset):
    return (c // SIDE + offset[0]) % SIDE * SIDE + (c % SIDE + offset[1]) % SIDE


def flip4(p, d):
    if d == 0:
        return p
    if d == 1:
        return p + 1 - 2 * (p % 2)
    if d == 2:
        return (p + 2) % SIDE
    return 3 - p


def paired(c, mask):
    return flip4(c // SIDE, mask // SIDE) * SIDE + flip4(c % SIDE, mask % SIDE)


def patterns():
    base = np.zeros((2, 4, 8, 2), np.int32)
    rest = np.zeros((2, 4, 8, 2), np.int32)
    mask = np.zeros((4, 8, 3, 2), np.int32)
    which = np.zeros((4, 8, 3, 2), np.int32)
    for q in range(4):
        j, g = q % 2, q // 2
        for k in range(8):
            for s in range(2):
                flip = kappa(q, k) ^ (MASKS[q][0] if s else 0)
                for f in range(2):
                    jy = (1 + g) if f else (3 if g else 0)
                    base[s, q, k, f] = flip
                    rest[s, q, k, f] = jy * TXD + j
                for e in range(3):
                    jy = (1 + g) if e != 1 else (3 if g else 0)
                    mask[q, k, e, s] = flip
                    which[q, k, e, s] = jy * TXD + j + TILES * (0, 1 - g, 1)[e]
    rows = np.zeros((8, 128), np.int32)
    rows[0] = base.reshape(-1)
    rows[1] = rest.reshape(-1)
    rows[2:4].reshape(-1)[:192] = mask.reshape(-1)
    rows[4:6].reshape(-1)[:192] = which.reshape(-1)
    return rows


def fill_tables(rows, foot, order, out, gx, gy):
    i32 = jnp.int32
    own = foot[pl.ds(gx * NY + gy, 1), :]
    slot = ((own >> 3) & (NY - 1)) * TILES + (own & (TILES - 1))
    across = lax.broadcasted_iota(i32, (128, 128), 1)
    along = lax.broadcasted_iota(i32, (128, 128), 0)
    slots = jnp.sum(jnp.where(across == along, slot, 0), axis=1, keepdims=True)
    target = (rows[0:1] ^ gy) * TILES + rows[1:2]
    out[0:1] = jnp.max(jnp.where(slots == across, along, 0), axis=0, keepdims=True)
    out[1:2] = jnp.max(jnp.where(slots == target, along, 0), axis=0, keepdims=True)

    listed = order[...]
    tile = lax.broadcasted_iota(i32, (TILES, 128), 0)
    for n in range(2):
        which = rows[4 + n : 5 + n]
        local = which & (TILES - 1)
        brick = ((gx - (which >> 3)) & (NX - 1)) * NY + (rows[2 + n : 3 + n] ^ gy)
        rank = jnp.zeros((TILES, 128), i32)
        for d in range(DEPTH):
            hit = jnp.logical_and(listed[:, d : d + 1] == brick, tile == local)
            rank = jnp.minimum(rank, jnp.where(hit, d - (DEPTH + 1), 0))
        rank = jnp.min(rank, axis=0, keepdims=True)
        out[2 + n : 3 + n] = local * TSTEP + DEPTH + 1 + rank

    tile = lax.broadcasted_iota(i32, (TILES, DEPTH), 0)
    part = jnp.minimum((gx - (listed >> 4)) & (NX - 1), 1)
    out[8:16, 0:DEPTH] = (part * NY + (listed & (NY - 1))) * TILES + tile


OUT = 32
GROUP = 4
VMEM_BYTES = 62 << 20
WIDE = 3 * COLS
DEEP1 = (CH + 1) * ROWS


def frame_kernel(
    pay_h, opa_h, rows_h, foot_h, order_h, panel_h, w1_h, b1_h, w2_h, b2_h, shown,
    rows, foot, order, tabv, tab, panel, inv, w1, b1, w2, b2, tsem,
    pay, opa, asend, abuf, tb, tsend, trecv, s1, r1, s2, acc, r2, s3, r3, s4, r4, ys, yr,
    cov, cov_side, cov_over, cov_under, stage, stage_y, v1, pack, rim, edge, band1, band2, h_acc, v2, base, strips,
    lsem, a_s, a_r, t_s, t_r, m_s, m_r, y_s, y_r, c_sem, h_s, h_r, d_sem,
):
    gx = lax.axis_index("gx")
    me = lax.axis_index("gy")
    up = (gx + 1) % NX
    down = (gx + NX - 1) % NX
    right = (me + 1) % NY
    left = (me + NY - 1) % NY
    early = [
        pltpu.make_async_copy(src, dst, tsem.at[n])
        for n, (src, dst) in enumerate(
            ((rows_h, rows), (foot_h, foot), (order_h, order), (opa_h, opa), (panel_h, panel),
             (w1_h, w1), (b1_h, b1), (w2_h, w2), (b2_h, b2))
        )
    ]
    loads = []
    for i in range(8):
        part = pl.ds(16 * i, 16)
        loads.append(pltpu.make_async_copy(pay_h.at[part], pay.at[part], lsem))
    for load in early[:4] + loads + early[4:]:
        load.start()

    barrier = pltpu.get_barrier_semaphore()

    for offset in OTHERS + [(0, 0)]:
        col = shifted(me, offset)
        for row in (up, down, gx):
            if row is not gx or offset != (0, 0):
                pl.semaphore_signal(barrier, inc=1, device_id=(row, col), device_id_type=MESH)

    for load in early[:3]:
        load.wait()
    fill_tables(rows, foot, order, tabv, gx, me)
    to_smem = pltpu.make_async_copy(tabv, tab, tsem.at[9])
    early[3].wait()
    to_smem.start()
    to_smem.wait()

    def pack_alpha(i, _):
        asend[i] = opa[tab[0, i]]
        return 0

    lax.fori_loop(0, 128, pack_alpha, 0, unroll=8)
    for e in range(TILES):
        abuf[me * TILES + e] = asend[me * TILES + e]
    pltpu.make_async_copy(pay_h, pay, lsem).wait()

    def pack_raw(q, lo, hi):
        def body(k, _):
            for f in range(2):
                s1[q, k, f] = pay[tab[1, 64 + (q * 8 + k) * 2 + f]]
            return 0

        lax.fori_loop(lo, hi, body, 0)

    for q in range(4):
        pack_raw(q, 2, 8)
    pl.semaphore_wait(barrier, 47)

    def alpha_copy(i):
        return pltpu.make_async_remote_copy(
            src_ref=asend.at[pl.ds(i * TILES, TILES)],
            dst_ref=abuf.at[pl.ds(me * TILES, TILES)],
            send_sem=a_s.at[0],
            recv_sem=a_r.at[0],
            device_id=(gx, i),
            device_id_type=MESH,
        )

    alpha_on = pltpu.make_async_remote_copy(
        src_ref=abuf.at[pl.ds(0, 128)],
        dst_ref=abuf.at[pl.ds(128, 128)],
        send_sem=a_s.at[1],
        recv_sem=a_r.at[1],
        device_id=(up, me),
        device_id_type=MESH,
    )

    for offset in OTHERS:
        alpha_copy(shifted(me, offset)).start()

    groups = ((4, 8), (2, 4), (1, 2), (0, 1))

    def raw_copy(q, n):
        lo, hi = groups[n]
        part = pl.ds(lo, hi - lo)
        return pltpu.make_async_remote_copy(
            src_ref=s1.at[q, part],
            dst_ref=r1.at[q, part],
            send_sem=m_s.at[0],
            recv_sem=m_r.at[q, 0 if n == 0 else 1],
            device_id=(gx, paired(me, MASKS[q][0])),
            device_id_type=MESH,
        )

    raw = [[raw_copy(q, n) for n in range(4)] for q in range(4)]
    for n in range(1):
        for q in range(4):
            raw[q][n].start()
    for q in range(4):
        pack_raw(q, 0, 2)
    for load in early[4:]:
        load.wait()

    def invert(g, _):
        at = 0
        for strip in range(NY):
            at = jnp.where(panel[strip] == g, strip, at)
        inv[g] = at
        return 0

    lax.fori_loop(0, NY, invert, 0)

    spread_weights(w1, w2, band1, band2)

    others = pl.ds(0, (NY - 1) * TILES)
    alphas = pltpu.make_async_remote_copy(
        src_ref=asend.at[others],
        dst_ref=abuf.at[others],
        send_sem=a_s.at[0],
        recv_sem=a_r.at[0],
        device_id=(gx, right),
        device_id_type=MESH,
    )
    alphas.wait_recv()
    alpha_on.start()
    alpha_on.wait_recv()

    for t in range(TILES):
        tb[t * TSTEP + DEPTH + 1] = jnp.zeros((ROWS, COLS), jnp.float32)

    def through(d, passed):
        out = []
        for t in range(TILES):
            tb[t * TSTEP + d] = passed[t]
            alpha = abuf[tab[8 + t, d]].astype(jnp.float32)
            out.append(passed[t] * (1.0 - alpha))
        return tuple(out)

    last = lax.fori_loop(
        0, DEPTH, through, tuple(jnp.ones((ROWS, COLS), jnp.float32) for _ in range(TILES))
    )
    for t in range(TILES):
        cov[t] = (1.0 - last[t]).astype(jnp.bfloat16)

    def fill(i, _):
        tsend[i] = tb[tab[2, i]].astype(jnp.bfloat16)
        return 0

    def fill_rest(i, _):
        tsend[128 + i] = tb[tab[3, i]].astype(jnp.bfloat16)
        return 0

    lax.fori_loop(0, 128, fill, 0, unroll=8)
    lax.fori_loop(0, 64, fill_rest, 0, unroll=8)

    def weight_range(q, k, back):
        g = q // 2
        start, size = ((0, 4 if g else 2), (4 if g else 2, 2 if g else 4))[back]
        return pl.ds((q * 8 + k) * 6 + start, size)

    def weight_copy(q, k, back):
        part = weight_range(q, k, back)
        return pltpu.make_async_remote_copy(
            src_ref=tsend.at[part],
            dst_ref=trecv.at[part],
            send_sem=t_s,
            recv_sem=t_r.at[1 if k >= 4 else 0],
            device_id=(down if back else gx, paired(me, kappa(q, k))),
            device_id_type=MESH,
        )

    for k in (7, 6, 5, 4, 3, 2, 1, 0):
        for q in range(4):
            for back in range(2):
                if k == 0 and back == 0:
                    g = q // 2
                    for e in range(4 if g else 2):
                        trecv[q * 48 + e] = tsend[q * 48 + e]
                else:
                    weight_copy(q, k, back).start()

    def weight_group(size, sem):
        part = pl.ds(0, size)
        return pltpu.make_async_remote_copy(
            src_ref=tsend.at[part],
            dst_ref=trecv.at[part],
            send_sem=t_s,
            recv_sem=t_r.at[sem],
            device_id=(gx, right),
            device_id_type=MESH,
        )

    first_row = pl.ds(0, TXD)
    last_row = pl.ds((TYD - 1) * TXD, TXD)
    covers = [
        pltpu.make_async_remote_copy(
            src_ref=src,
            dst_ref=dst,
            send_sem=c_sem.at[0],
            recv_sem=c_sem.at[1],
            device_id=(row, col),
            device_id_type=MESH,
        )
        for src, dst, row, col in (
            (
                (cov, cov_side.at[0], gx, right),
                (cov, cov_side.at[1], gx, left),
                (cov.at[last_row], cov_over.at[0], up, right),
                (cov.at[last_row], cov_over.at[1], up, left),
                (cov.at[first_row], cov_under.at[0], down, right),
                (cov.at[first_row], cov_under.at[1], down, left),
                (cov.at[first_row], cov_under.at[2], down, me),
            )
        )
    ]
    for copy in covers:
        copy.start()
    covered_part = pl.ds(0, 2 * TILES + 5 * TXD)
    all_covers = pltpu.make_async_remote_copy(
        src_ref=asend.at[covered_part],
        dst_ref=abuf.at[covered_part],
        send_sem=c_sem.at[0],
        recv_sem=c_sem.at[1],
        device_id=(gx, right),
        device_id_type=MESH,
    )
    for n in range(1, 4):
        for q in range(4):
            raw[q][n].start()

    def weighed(q, k):
        own = (q * 8 + k) * 2
        lead = (q * 8 + k) * 6
        w = [trecv[lead + n].astype(jnp.float32)[None] for n in range(6)]
        own_f = pay[tab[1, own]].astype(jnp.float32)
        got_f = r1[q, k, 0].astype(jnp.float32)
        mid = w[2] * own_f + w[3] * got_f
        own_a = pay[tab[1, own + 1]].astype(jnp.float32)
        got_a = r1[q, k, 1].astype(jnp.float32)
        first = w[0] * own_a + w[1] * got_a
        third = w[4] * own_a + w[5] * got_a
        return first, mid, third

    def merge_sent(q, lo, hi):
        def body(k, _):
            for e, v in enumerate(weighed(q, k)):
                s2[q, k - 4, e] = v.astype(jnp.bfloat16)
            return 0

        lax.fori_loop(lo, hi, body, 0)

    def merge_kept(q, lo, hi):
        def body(k, _):
            for e, v in enumerate(weighed(q, k)):
                acc[q, k, e] = v
            return 0

        lax.fori_loop(lo, hi, body, 0)

    def step_copy(src, dst, q, lo, hi, step, sem):
        part = pl.ds(lo, hi - lo)
        return pltpu.make_async_remote_copy(
            src_ref=src.at[q, part],
            dst_ref=dst.at[q, part],
            send_sem=m_s.at[step - 1],
            recv_sem=m_r.at[q, sem],
            device_id=(gx, paired(me, MASKS[q][step - 1])),
            device_id_type=MESH,
        )

    def whole(src, dst, part, send, recv):
        return pltpu.make_async_remote_copy(
            src_ref=src.at[part],
            dst_ref=dst.at[part],
            send_sem=send,
            recv_sem=recv,
            device_id=(gx, right),
            device_id_type=MESH,
        )

    two = [[step_copy(s2, r2, q, lo, hi, 2, 2 + n) for n, (lo, hi) in enumerate(groups[1:])] for q in range(4)]
    three = [[step_copy(s3, r3, q, lo, hi, 3, 5 + n) for n, (lo, hi) in enumerate(groups[2:])] for q in range(4)]

    def last_copy(q, crossing):
        size = 2 - q // 2 if crossing else 1 + q // 2
        part = pl.ds(1 + q // 2 if crossing else 0, size)
        return pltpu.make_async_remote_copy(
            src_ref=s4.at[q, 0, part],
            dst_ref=r4.at[q, 0, part],
            send_sem=m_s.at[3],
            recv_sem=m_r.at[q, 7 + crossing],
            device_id=(gx, paired(me, MASKS[q][3])),
            device_id_type=MESH,
        )

    four = [[last_copy(q, crossing) for crossing in range(2)] for q in range(4)]

    weight_group(96, 1).wait_recv()
    for q in range(4):
        raw[q][0].wait_recv()
        merge_sent(q, 6, 8)
        two[q][0].start()
    for q in range(4):
        merge_sent(q, 4, 6)
        two[q][1].start()
        two[q][2].start()
    weight_group(84, 0).wait_recv()
    for q in range(4):
        half = (q, pl.ds(0, 4))
        whole(s1, r1, half, m_s.at[0], m_r.at[q, 1]).wait_recv()
        merge_kept(q, 0, 4)

    def added(src, q, k):
        return [acc[q, k, e] + src[q, k, e].astype(jnp.float32) for e in range(3)]

    def forward(dst, src, q, k, to):
        for e, v in enumerate(added(src, q, k)):
            dst[q, to, e] = v.astype(jnp.bfloat16)

    def keep(src, q, k):
        for e, v in enumerate(added(src, q, k)):
            acc[q, k, e] = v

    for q in range(4):
        two[q][0].wait_recv()
        forward(s3, r2, q, 3, 1)
        three[q][0].start()
        forward(s3, r2, q, 2, 0)
        three[q][1].start()
    for q in range(4):
        two[q][1].wait_recv()
        keep(r2, q, 1)
        two[q][2].wait_recv()
        keep(r2, q, 0)
    for q in range(4):
        three[q][0].wait_recv()
        forward(s4, r3, q, 1, 0)
        four[q][1].start()
        four[q][0].start()
    for q in range(4):
        three[q][1].wait_recv()
        keep(r3, q, 0)

    def cross_copy(q):
        part = pl.ds(q // 2, 2 - q // 2)
        return pltpu.make_async_remote_copy(
            src_ref=ys.at[q, part],
            dst_ref=yr.at[q, part],
            send_sem=y_s,
            recv_sem=y_r.at[q],
            device_id=(up, me),
            device_id_type=MESH,
        )

    cross = [cross_copy(q) for q in range(4)]

    def spread(ref, v):
        for c in range(CH):
            ref[pl.ds(c * ROWS, ROWS), :] = v[c]

    def place(jy, j, v):
        spread(stage.at[jy, j], v)
        stage[jy, j, pl.ds(CH * ROWS, ROWS), :] = cov[jy * TXD + j].astype(jnp.float32)
        v1[jy + 1, :, pl.ds(j * COLS, COLS)] = stage[jy, j].astype(jnp.bfloat16)

    def final(q, e):
        return acc[q, 0, e] + r4[q, 0, e].astype(jnp.float32)

    for q in range(4):
        g, j = q // 2, q % 2
        four[q][1].wait_recv()
        ys[q, 1] = final(q, 2).astype(jnp.bfloat16)
        if g == 0:
            ys[q, 0] = final(q, 1).astype(jnp.bfloat16)
        cross[q].start()
    for q in range(4):
        g, j = q // 2, q % 2
        spread(stage_y.at[1 + g, j], ys[q, 1].astype(jnp.float32))
        if g == 0:
            spread(stage_y.at[0, j], ys[q, 0].astype(jnp.float32))
    for q in range(4):
        g, j = q // 2, q % 2
        four[q][0].wait_recv()
        own = final(q, 0)
        acc[q, 0, 0] = own
        spread(stage.at[1 + g, j], own)
        if g:
            place(3, j, final(q, 1))

    def edge_copy(src, dst, n, row, col):
        n = min(n, 1)
        return pltpu.make_async_remote_copy(
            src_ref=src,
            dst_ref=dst,
            send_sem=h_s.at[n],
            recv_sem=h_r.at[n],
            device_id=(row, col),
            device_id_type=MESH,
        )

    mine = pl.ds(0, TXD * COLS)
    edges = (
        edge_copy(v1.at[4, :, mine], v1.at[0, :, mine], 0, up, me),
        edge_copy(pack.at[0, 0], rim.at[0, 0], 1, gx, right),
        edge_copy(pack.at[0, 1], rim.at[0, 1], 2, gx, left),
        edge_copy(pack.at[1, 0], rim.at[1, 0], 3, up, right),
        edge_copy(pack.at[1, 1], rim.at[1, 1], 4, up, left),
    )
    edges[0].start()

    lane = lax.broadcasted_iota(jnp.int32, (8, COLS), 1)
    groups_of = DEEP1 // 8

    def packed(ref, side):
        total = jnp.zeros((8, COLS), jnp.float32)
        for i in range(groups_of):
            v = ref[pl.ds(8 * i, 8), :]
            if i:
                v = pltpu.roll(v, 4 * i, 1)
            pair = (COLS // 2 - 1 + 2 * i) % (COLS // 2) if side == 0 else 2 * i
            total = jnp.where((lane >> 1) == pair, v, total)
        return total

    for side in range(2):
        j = 1 - side
        for n, ref in enumerate((stage.at[1, j], stage.at[2, j], stage.at[3, j], stage_y.at[0, j])):
            pack[0, side, pl.ds(8 * n, 8), :] = packed(ref, side)
        for n, ref in enumerate((stage.at[3, j], stage_y.at[0, j], stage_y.at[1, j], stage_y.at[2, j])):
            pack[1, side, pl.ds(8 * n, 8), :] = packed(ref, side)
        edges[1 + side].start()
        edges[3 + side].start()

    all_covers.wait_recv()
    for j in range(TXD):
        stage_y[0, j, pl.ds(CH * ROWS, ROWS), :] = cov_under[2, j].astype(jnp.float32)
        low = jnp.where(gx < NX - 1, stage_y[0, j], 0.0)
        v1[5, :, pl.ds(j * COLS, COLS)] = low.astype(jnp.bfloat16)
    for q in range(4):
        g, j = q // 2, q % 2
        cross[q].wait_recv()
        if g == 0:
            place(0, j, yr[q, 0].astype(jnp.float32))
        place(1 + g, j, acc[q, 0, 0] + yr[q, 1].astype(jnp.float32))
    for n in range(16):
        rows_of = pl.ds(n % 4, OUT, stride=ROWS)
        row = jnp.concatenate([stage[n // 4, j, rows_of, :] for j in range(TXD)], axis=1)
        base[n] = row.astype(jnp.bfloat16).astype(jnp.float32)
    rims = whole(pack, rim, pl.ds(0, 2), h_s.at[1], h_r.at[1])
    edges[0].wait_recv()
    rims.wait_recv()

    last_tile = pl.ds(2 * COLS, COLS)
    cover_lane = lax.broadcasted_iota(jnp.int32, (ROWS, COLS), 1)
    has = (me > 0, me < NY - 1)
    for blk in range(-1, TYD + 1):
        total = None
        for side in range(2):
            part = None
            if blk >= 1:
                part = rim[0, side, pl.ds(8 * (blk - 1), 8), :]
            if blk <= 2:
                more = rim[1, side, pl.ds(8 * (blk + 1), 8), :]
                part = more if part is None else part + more
            part = jnp.where(has[side], part, 0.0)
            total = part if total is None else total + part
        if blk < 0:
            sides = cov_over[0, 1], cov_over[1, 0]
            inside = gx > 0
        elif blk == TYD:
            sides = cov_under[0, 1], cov_under[1, 0]
            inside = gx < NX - 1
        else:
            sides = cov_side[0, blk * TXD + 1], cov_side[1, blk * TXD]
            inside = None
        covered = jnp.where(
            cover_lane >= COLS // 2,
            jnp.where(has[0], sides[0].astype(jnp.float32), 0.0),
            jnp.where(has[1], sides[1].astype(jnp.float32), 0.0),
        )
        for i in range(groups_of):
            edge[blk + 1, pl.ds(8 * i, 8), :] = pltpu.roll(total, COLS - 4 * i, 1) if i else total
        edge[blk + 1, pl.ds(CH * ROWS, ROWS), :] = covered
        value = edge[blk + 1]
        if inside is not None:
            value = jnp.where(inside, value, 0.0)
        v1[blk + 1, :, last_tile] = value.astype(jnp.bfloat16)
    wide_zero = jnp.zeros((DEEP1, TXD * COLS), jnp.bfloat16)

    @pl.when(gx == 0)
    def _():
        v1[0, :, mine] = wide_zero

    def product(band, rows, field):
        total = None
        for dx in range(3):
            z = jnp.dot(band(dx, rows), field, preferred_element_type=jnp.float32)
            if dx != 1:
                z = pltpu.roll(z, (1 - dx) % WIDE, 1)
            total = z if total is None else total + z
        return total

    def band_one(dx, rows):
        return band1[dx, rows, :]

    def column(ref):
        eye = lax.broadcasted_iota(jnp.int32, (OUT, OUT), 0) == lax.broadcasted_iota(jnp.int32, (OUT, OUT), 1)
        return jnp.sum(jnp.where(eye, ref[...], 0.0), axis=1, keepdims=True)

    every = pl.ds(0, 6 * OUT)
    head = product(band_one, pl.ds(4 * OUT, 2 * OUT), v1[0])
    h_acc[0] = head[:OUT]
    h_acc[1] = head[OUT:]
    for blk in range(TYD):
        s = product(band_one, every, v1[blk + 1])
        y = 4 * blk
        for n in range(6):
            piece = s[n * OUT : (n + 1) * OUT]
            h_acc[y + n] = piece + h_acc[y + n] if n < 2 else piece
    tail = product(band_one, pl.ds(0, 2 * OUT), v1[5])
    bias_one = column(b1)
    far = lax.broadcasted_iota(jnp.int32, (OUT, WIDE), 1)
    cut = jnp.logical_or(
        jnp.logical_and(far >= 2 * COLS + COLS // 2, me == 0),
        jnp.logical_and(
            jnp.logical_and(far >= 2 * COLS, far < 2 * COLS + COLS // 2), me == NY - 1
        ),
    )
    for n in range(18):
        raw_sum = h_acc[n]
        if n >= 16:
            raw_sum = raw_sum + tail[(n - 16) * OUT : (n - 15) * OUT]
        pre = raw_sum + bias_one
        h = pre * lax.logistic(pre)
        h = jnp.where(cut, 0.0, h)
        if n == 0:
            h = jnp.where(gx > 0, h, 0.0)
        elif n == 17:
            h = jnp.where(gx < NX - 1, h, 0.0)
        v2[n] = h.astype(jnp.bfloat16)

    bias_two = column(b2)

    def shade(g):
        row = inv[g]
        field = jnp.concatenate([v2[row], v2[row + 1], v2[row + 2]], axis=0)
        z = jnp.dot(band2[...], field, preferred_element_type=jnp.float32)
        total = z[OUT : 2 * OUT] + pltpu.roll(z[:OUT], 1, 1)
        total = total + pltpu.roll(z[2 * OUT :], WIDE - 1, 1)
        return (total[:, : TXD * COLS] + bias_two + base[row]).astype(jnp.bfloat16)

    def window(col):
        start = pl.multiple_of(col * (TXD * COLS), TXD * COLS)
        return shown.at[:, pl.ds(start, TXD * COLS)]

    def strip_copy(g):
        return pltpu.make_async_remote_copy(
            src_ref=strips.at[g],
            dst_ref=window(me),
            send_sem=d_sem.at[0],
            recv_sem=d_sem.at[1],
            device_id=(gx, g),
            device_id_type=MESH,
        )

    for n in range(0, len(OTHERS), GROUP):
        columns = [shifted(me, offset) for offset in OTHERS[n : n + GROUP]]
        for g in columns:
            strips[g] = shade(g)
        for g in columns:
            strip_copy(g).start()
    start = pl.multiple_of(me * (TXD * COLS), TXD * COLS)
    shown[:, pl.ds(start, TXD * COLS)] = shade(me)

    edges[0].wait_send()
    rims.wait_send()
    all_covers.wait_send()

    alphas.wait_send()
    alpha_on.wait_send()
    weight_group(180, 0).wait_send()
    every_q = pl.ds(0, 4)
    for n, (src, dst) in enumerate(((s1, r1), (s2, r2), (s3, r3), (s4, r4))):
        whole(src, dst, every_q, m_s.at[n], m_r.at[0, 0]).wait_send()
    whole(ys, yr, pl.ds(0, 3), y_s, y_r.at[0]).wait_send()
    parts = pl.ds(0, NY - 1)
    all_strips = pltpu.make_async_remote_copy(
        src_ref=strips.at[parts],
        dst_ref=strips.at[parts],
        send_sem=d_sem.at[0],
        recv_sem=d_sem.at[1],
        device_id=(gx, right),
        device_id_type=MESH,
    )
    all_strips.wait_send()
    all_strips.wait_recv()


def spread_weights(w1, w2, band1, band2):
    def pick(ins, wide, first, step):
        chan = lax.broadcasted_iota(jnp.int32, (ins, wide), 0)
        spot = lax.broadcasted_iota(jnp.int32, (ins, wide), 1)
        return jnp.where(spot == chan * step + first, 1.0, 0.0).astype(jnp.bfloat16)

    def spread(terms):
        total = None
        for taps, place in terms:
            term = jnp.dot(taps, place, preferred_element_type=jnp.float32)
            total = term if total is None else total + term
        return total.astype(jnp.bfloat16)

    picks = [pick(CH + 1, DEEP1, r, ROWS) for r in range(ROWS)]
    for dx in range(3):
        for n in range(6):
            rows = [(dy, n + dy - 2) for dy in range(3) if 0 <= n + dy - 2 < ROWS]
            band1[dx, pl.ds(n * OUT, OUT), :] = spread([(w1[3 * dy + dx], picks[r]) for dy, r in rows])
    picks = [pick(OUT, 3 * OUT, dy * OUT, 1) for dy in range(3)]
    for dx in range(3):
        band2[pl.ds(dx * OUT, OUT), :] = spread([(w2[3 * dy + dx], picks[dy]) for dy in range(3)])


def frame(*operands):
    unit = (CH, ROWS, COLS)
    bf16, f32 = jnp.bfloat16, jnp.float32
    vmem = pltpu.VMEM
    dma = pltpu.SemaphoreType.DMA
    return pl.pallas_call(
        frame_kernel,
        name="frame",
        out_shape=vmem((OUT, NY * TXD * COLS), bf16),
        in_specs=[pl.BlockSpec(memory_space=pl.ANY)] * len(operands),
        out_specs=pl.BlockSpec(memory_space=vmem),
        scratch_shapes=[
            vmem((8, 128), jnp.int32),
            vmem((128, 128), jnp.int32),
            vmem((TILES, DEPTH), jnp.int32),
            vmem((16, 128), jnp.int32),
            pltpu.SMEM((16, 128), jnp.int32),
            pltpu.SMEM((NY,), jnp.int32),
            pltpu.SMEM((NY,), jnp.int32),
            vmem((9, OUT, CH + 1), bf16),
            vmem((1, OUT), f32),
            vmem((9, OUT, OUT), bf16),
            vmem((1, OUT), f32),
            dma((10,)),
            vmem((128,) + unit, bf16),
            vmem((128, ROWS, COLS), bf16),
            vmem((128, ROWS, COLS), bf16),
            vmem((256, ROWS, COLS), bf16),
            vmem((TILES * TSTEP, ROWS, COLS), f32),
            vmem((192, ROWS, COLS), bf16),
            vmem((192, ROWS, COLS), bf16),
            vmem((4, 8, 2) + unit, bf16),
            vmem((4, 8, 2) + unit, bf16),
            vmem((4, 4, 3) + unit, bf16),
            vmem((4, 4, 3) + unit, f32),
            vmem((4, 4, 3) + unit, bf16),
            vmem((4, 2, 3) + unit, bf16),
            vmem((4, 2, 3) + unit, bf16),
            vmem((4, 1, 3) + unit, bf16),
            vmem((4, 1, 3) + unit, bf16),
            vmem((4, 2) + unit, bf16),
            vmem((4, 2) + unit, bf16),
            vmem((TILES, ROWS, COLS), bf16),
            vmem((2, TILES, ROWS, COLS), bf16),
            vmem((2, TXD, ROWS, COLS), bf16),
            vmem((3, TXD, ROWS, COLS), bf16),
            vmem((TYD, TXD, DEEP1, COLS), f32),
            vmem((3, TXD, DEEP1, COLS), f32),
            vmem((TYD + 2, DEEP1, WIDE), bf16),
            vmem((2, 2, 32, COLS), f32),
            vmem((2, 2, 32, COLS), f32),
            vmem((TYD + 2, DEEP1, COLS), f32),
            vmem((3, 6 * OUT, DEEP1), bf16),
            vmem((3 * OUT, 3 * OUT), bf16),
            vmem((18, OUT, WIDE), f32),
            vmem((18, OUT, WIDE), bf16),
            vmem((16, OUT, TXD * COLS), f32),
            vmem((NY, OUT, TXD * COLS), bf16),
            dma(()),
            dma((2,)),
            dma((2,)),
            dma(()),
            dma((2,)),
            dma((4,)),
            dma((4, 9)),
            dma(()),
            dma((4,)),
            dma((2,)),
            dma((2,)),
            dma((2,)),
            dma((2,)),
        ],
        compiler_params=pltpu.CompilerParams(
            collective_id=0, has_side_effects=True, vmem_limit_bytes=VMEM_BYTES
        ),
    )(*operands)


def shards(
    payload, opacity, depth_order, footprints, panel_map,
    conv1_weight, conv1_bias, conv2_weight, conv2_bias,
):
    shown = frame(
        payload.transpose(0, 2, 1, 3),
        opacity,
        jnp.asarray(patterns()),
        footprints,
        depth_order,
        panel_map,
        conv1_weight,
        conv1_bias[None],
        conv2_weight,
        conv2_bias[None],
    )
    return shown[None, None, None]


SPECS = (
    P(("gx", "gy"), None, None, None),
    P(("gx", "gy"), None, None),
    P(("gx", "gy"), None),
    P(),
    P(),
    P(),
    P(),
    P(),
    P(),
)


def solution(mesh):
    return jax.shard_map(
        shards,
        mesh=mesh,
        in_specs=SPECS,
        out_specs=P("gx", "gy", None, None, None),
        check_vma=False,
    )
```
